32 devices in a mesh: groups: 2 (over x), ctx: 4 (over y, core), heads: 4 (over z).
Axes of the slice: x: 2, y: 2, z: 4, core: 2. Of those that a mesh axis runs over, the one named last changes fastest.
Arguments:
- tokens: bfloat16 [4096, 2048], P(('groups', 'ctx', 'heads')), parts along dimension 0, may hold values from -60 to 60
- state_in: float32 [4, 256, 128], P('heads', 'groups'), parts along dimension 1, may hold values from -256 to 256
- past_kv: bfloat16 [2, 1024, 512], P(None, 'groups', 'heads'), parts along dimension 1, may hold values from -6 to 6
- w_qkv: bfloat16 [2048, 3, 512], P(None, None, 'heads'), may hold values from -0.125 to 0.125
- w_out: bfloat16 [512, 2048], P('heads'), may hold values from -0.25 to 0.25
- w_gate: bfloat16 [16, 2048, 768], P(('ctx', 'heads')), may hold values from -0.125 to 0.125
- w_up: bfloat16 [16, 2048, 768], P(('ctx', 'heads')), may hold values from -0.125 to 0.125
- w_down: bfloat16 [16, 768, 2048], P(('ctx', 'heads')), may hold values from -0.21875 to 0.21875
- expert_ids: int32 [4096, 8], P(('groups', 'ctx', 'heads')), parts along dimension 0, may hold values from 0 to 15, all different within a row; in each aligned block of 128 rows (0 to 127, 128 to 255, ...) at most 128 rows name the same one
- gate_weights: float32 [4096, 8], P(('groups', 'ctx', 'heads')), parts along dimension 0, may hold values from 0.1 to 1
Outputs:
- mixed: bfloat16 [4096, 2048], P(('groups', 'ctx', 'heads')), parts along dimension 0
The draws below stay inside these ranges and needn't reach their ends.
There are 2 independent parts, one for each index of `groups`. The reference program is written for one: setup_inputs(seed, part) draws one part's arguments, and reference() takes and returns one part's arrays. A program takes and returns all parts, laid end to end along the dimension named above; an argument that names none is the same for every part. Nothing has to cross between parts.
Inputs may be any that keep to these rules, and one draw needn't show every extreme that they name: `expert_ids`: each row names 8 different experts; in each aligned block of 128 rows (the rows of one device) no expert is named by more than 128 rows, a bound that some block reaches.
All inputs are finite; a program needn't handle non-finite values.
Results may differ from the reference program's by a relative error of at most 0.017.
Values may be sent and summed in bfloat16 or wider, within the bound.
A program may use at most 128 MiB of HBM per device.

```python
import math
import jax
import jax.numpy as jnp
import numpy as np
from jax import lax

D = 2048
HDIM = 128
INNER = 768
TOP = 8
WINDOW = 512
TOK_DEV = 512
TOKENS = 2048
ROWS = 128
HEADS = 4
EXPERTS = 16
CAP = 128


def draw_tokens(key, part):
    base_key = jax.random.fold_in(jax.random.fold_in(key, 11), 0)
    values = jax.random.normal(base_key, (TOKENS, D), jnp.float32)
    return jnp.clip(values, -60.0, 60.0).astype(jnp.bfloat16)


def block_scale(stream_key, dims, shards, low, largest):
    def one(axis_at, parts):
        draws = jax.random.uniform(jax.random.fold_in(jax.random.fold_in(stream_key, 6), axis_at), (parts,), jnp.float32, low / len(shards), largest / len(shards))
        return jnp.repeat(jnp.exp(draws), dims[axis_at] // parts).reshape((-1,) + (1,) * (len(dims) - axis_at - 1))

    gain = one(*shards[0])
    for cut in shards[1:]:
        gain = gain * one(*cut)
    return gain


def routed_block(key, own, number, rows, amount, top, most, slope):
    sequence = jax.random.permutation(key, amount)
    crowded, common = shares(amount, rows * top, most, slope, True), shares(amount, rows * top, most, slope, False)
    places = jnp.arange(amount)

    def named(tallies, offset_by):
        used = int((tallies > 0).sum())
        fixed = max(1, used // 4)
        shifted = fixed + (places - fixed + offset_by * (used - fixed)) % max(1, amount - fixed)
        return jnp.zeros((amount,), jnp.int32).at[sequence[jnp.where(places < fixed, places, shifted)]].set(jnp.asarray(tallies, jnp.int32))

    tallies = jnp.where(number % 4 == 0, named(crowded, number // 4), named(common, number - number // 4 - 1))
    mixed = jax.random.permutation(jax.random.fold_in(own, 3), amount)
    source_of, taker = mixed[0:amount // 2 * 2:2], mixed[1:amount // 2 * 2:2]
    room = jnp.minimum(tallies[source_of] - 1, most - tallies[taker]) // 2
    room = jnp.where((source_of == sequence[0]) | (taker == sequence[0]) | (tallies[taker] == 0), 0, jnp.maximum(room, 0))
    shifted = jax.random.randint(jax.random.fold_in(own, 4), (amount // 2,), 0, 1 << 20) % (room + 1)
    tallies = tallies.at[source_of].add(-shifted).at[taker].add(shifted)
    labels = jnp.searchsorted(jnp.cumsum(tallies), jnp.arange(rows * top), side="right").astype(jnp.int32)
    grid = labels.reshape(top, rows).T
    grid = grid[jax.random.permutation(jax.random.fold_in(own, 1), rows)]
    offset_by = jax.random.randint(jax.random.fold_in(own, 2), (rows, 1), 0, top)
    return jnp.take_along_axis(grid, (jnp.arange(top)[None, :] + offset_by) % top, axis=1)


def shares(number_of, total, limit, slope, full):
    portions = [(1 << 20) // math.isqrt(grade ** slope) + 1 for grade in range(1, number_of + 1)]
    largest = limit if full else min(limit, max(-(-total // number_of), total * portions[0] // sum(portions)))
    least = 1 if total - largest >= number_of - 1 else 0
    given, rest = [largest] + [least] * (number_of - 1), total - largest - least * (number_of - 1)
    while rest > 0:
        candidates = [i for i in range(1, number_of) if given[i] < largest] or [i for i in range(1, number_of) if given[i] < limit]
        whole, left = sum([portions[i] for i in candidates]), rest
        for i in candidates:
            more = min(limit - given[i], max(1, left * portions[i] // whole), rest)
            given[i] = given[i] + more
            rest = rest - more
    return np.array(given)


def normal_values(stream_key, dims, scale, bound, cuts=(), kind=jnp.bfloat16):
    result = scale * jax.random.normal(stream_key, dims, jnp.float32)
    if cuts:
        result = result * block_scale(stream_key, dims, cuts, -0.22, 0.18)
    return jnp.clip(result, -bound, bound).astype(kind)


def setup_inputs(seed: int = 0, part: int = 0) -> dict:
    splits = jax.random.split(jax.random.key(seed), 11)
    own_keys = jax.random.split(jax.random.fold_in(splits[10], part), 11)
    tokens = draw_tokens(jax.random.fold_in(jax.random.fold_in(splits[10], part), 71), part)
    state_in = normal_values(own_keys[1], (HEADS, HDIM, HDIM), (TOKENS ** 0.5), 256.0, ((0, 4),), jnp.float32)
    past_kv = normal_values(own_keys[2], (2, WINDOW, HEADS * HDIM), 1.0, 6.0, ((2, 4),))
    w_qkv = normal_values(splits[3], (D, 3, HEADS * HDIM), D ** -0.5, 0.125, ((2, 4),))
    w_out = normal_values(splits[4], (HEADS * HDIM, D), (HEADS * HDIM) ** -0.5, 0.25, ((0, 4),))
    w_gate = normal_values(splits[5], (EXPERTS, D, INNER), D ** -0.5, 0.125, ((0, 16),))
    w_up = normal_values(splits[6], (EXPERTS, D, INNER), D ** -0.5, 0.125, ((0, 16),))
    w_down = normal_values(splits[7], (EXPERTS, INNER, D), INNER ** -0.5, 0.21875, ((0, 16),))
    expert_ids_keys = jax.random.split(jax.random.fold_in(own_keys[8], 1), TOKENS // ROWS)
    expert_ids_turns = jax.random.permutation(jax.random.fold_in(own_keys[8], 3), TOKENS // ROWS)
    expert_ids = jax.vmap(lambda own, number: routed_block(jax.random.fold_in(own_keys[8], 2), own, number, ROWS, EXPERTS, TOP, CAP, 2))(expert_ids_keys, expert_ids_turns).reshape((TOKENS, TOP))
    gate_weights = jnp.clip(jnp.exp(math.log(1.0) - 2.3025851 * jax.random.uniform(own_keys[9], (TOKENS, TOP), jnp.float32) ** block_scale(own_keys[9], (TOKENS, TOP), ((0, 16),), -0.2, 0.2)), 0.1, 1.0)
    return dict(tokens=tokens, state_in=state_in, past_kv=past_kv, w_qkv=w_qkv, w_out=w_out, w_gate=w_gate, w_up=w_up, w_down=w_down, expert_ids=expert_ids, gate_weights=gate_weights)


def normalize(value):
    return value * lax.rsqrt(lax.optimization_barrier(jnp.mean(value * value, axis=-1, keepdims=True)) + 1e-06)

def one_head(query, keys, values, start_state, past_keys, past_values):
    block_rows = min(TOK_DEV, 512)
    block_count = TOKENS // block_rows
    scale = 1.0 / math.sqrt(HDIM)
    causal = jnp.arange(block_rows)[:, None] >= jnp.arange(block_rows)[None, :]
    offsets = jnp.arange(WINDOW + block_rows)[None, :] - jnp.arange(block_rows)[:, None]
    in_window = (offsets > 0) & (offsets <= WINDOW)
    all_keys = jnp.concatenate([past_keys, keys], axis=0)
    all_values = jnp.concatenate([past_values, values], axis=0)

    def step(state, index):
        first = (index * block_rows).astype(jnp.int32)
        q_block = lax.dynamic_slice_in_dim(query, first, block_rows, 0)
        k_block = lax.dynamic_slice_in_dim(keys, first, block_rows, 0)
        v_block = lax.dynamic_slice_in_dim(values, first, block_rows, 0)
        carried = jnp.dot(q_block.astype(jnp.float32), state, precision=lax.Precision.HIGHEST)
        inside = jnp.dot(q_block, k_block.T, preferred_element_type=jnp.float32)
        inside = jnp.where(causal, inside, 0.0).astype(jnp.bfloat16)
        linear = carried + jnp.dot(inside, v_block, preferred_element_type=jnp.float32)
        w_keys = lax.dynamic_slice_in_dim(all_keys, first, WINDOW + block_rows, 0)
        w_values = lax.dynamic_slice_in_dim(all_values, first, WINDOW + block_rows, 0)
        scores = jnp.dot(q_block, w_keys.T, preferred_element_type=jnp.float32) * scale
        scores = jnp.where(in_window, scores, -jnp.inf)
        top_score = lax.optimization_barrier(jnp.max(scores, axis=-1, keepdims=True))
        expo = jnp.exp(scores - top_score)
        probs = (expo / lax.optimization_barrier(jnp.sum(expo, axis=-1, keepdims=True))).astype(jnp.bfloat16)
        window_out = jnp.dot(probs, w_values, preferred_element_type=jnp.float32)
        combined = (normalize(linear) + window_out).astype(jnp.bfloat16)
        new_state = state + jnp.dot(k_block.T, v_block, preferred_element_type=jnp.float32)
        return (new_state, combined)
    _, outs = lax.scan(step, start_state, jnp.arange(block_count, dtype=jnp.int32))
    return outs.reshape(TOKENS, HDIM)

def slot_block(block_ids):
    onehot = (block_ids[:, None] == jnp.arange(EXPERTS, dtype=jnp.int32)[None, :]).astype(jnp.int32)
    earlier = jnp.cumsum(onehot, axis=0) - onehot
    return lax.optimization_barrier(jnp.sum(onehot * earlier, axis=1)).astype(jnp.int32)

def reference(tokens, state_in, past_kv, w_qkv, w_out, w_gate, w_up, w_down, expert_ids, gate_weights):
    projected = jnp.dot(tokens, w_qkv.reshape(D, 3 * HEADS * HDIM), preferred_element_type=jnp.float32)
    projected = projected.astype(jnp.bfloat16).reshape(TOKENS, 3, HEADS, HDIM)
    query = jnp.transpose(projected[:, 0], (1, 0, 2))
    keys = jnp.transpose(projected[:, 1], (1, 0, 2))
    values = jnp.transpose(projected[:, 2], (1, 0, 2))
    past = jnp.transpose(past_kv.reshape(2, WINDOW, HEADS, HDIM), (0, 2, 1, 3))

    def per_head(inputs):
        return one_head(*inputs)
    heads_out = lax.map(per_head, (query, keys, values, state_in, past[0], past[1]))
    heads_out = jnp.transpose(heads_out, (1, 0, 2)).reshape(TOKENS, HEADS * HDIM)
    attn = jnp.dot(heads_out, w_out, preferred_element_type=jnp.float32)
    hidden_state = (tokens.astype(jnp.float32) + attn).astype(jnp.bfloat16)
    normed = normalize(hidden_state.astype(jnp.float32)).astype(jnp.bfloat16)
    sources = TOKENS // ROWS
    picks = expert_ids.reshape(sources, ROWS * TOP).astype(jnp.int32)
    slots = lax.map(slot_block, picks)
    source_ids = jnp.broadcast_to(jnp.arange(sources, dtype=jnp.int32)[:, None], picks.shape)
    token_ids = source_ids * ROWS + (jnp.arange(ROWS * TOP, dtype=jnp.int32) // TOP)[None, :]
    table = jnp.full((EXPERTS, sources, CAP), TOKENS, jnp.int32).at[picks, source_ids, slots].set(token_ids)
    weight_table = jnp.zeros((EXPERTS, sources, CAP), jnp.float32).at[picks, source_ids, slots].set(gate_weights.reshape(sources, ROWS * TOP))
    padded = jnp.concatenate([normed, jnp.zeros((1, D), jnp.bfloat16)], axis=0)

    def expert_step(total, inputs):
        index_rows, weight_rows, gate_mat, up_mat, down_mat = inputs
        flat_index = index_rows.reshape(-1)
        rows_in = padded[flat_index]
        gate_act = jnp.dot(rows_in, gate_mat, preferred_element_type=jnp.float32)
        up_act = jnp.dot(rows_in, up_mat, preferred_element_type=jnp.float32)
        hid = (jax.nn.silu(gate_act) * up_act).astype(jnp.bfloat16)
        out_rows = jnp.dot(hid, down_mat, preferred_element_type=jnp.float32).astype(jnp.bfloat16)
        total = total.at[flat_index].add(weight_rows.reshape(-1)[:, None] * out_rows.astype(jnp.float32))
        return (total, None)
    total, _ = lax.scan(expert_step, jnp.zeros((TOKENS + 1, D), jnp.float32), (table, weight_table, w_gate, w_up, w_down))
    return (hidden_state.astype(jnp.float32) + total[:TOKENS]).astype(jnp.bfloat16)
```

```python
import functools
import math

import jax
import jax.numpy as jnp
from jax import lax
from jax.experimental import pallas as pl
from jax.experimental.pallas import tpu as pltpu
from jax.sharding import PartitionSpec as P

HDIM = 128
WINDOW = 512


def entering(x, axis, join, neutral):
    place = lax.axis_index(axis)
    gathered = lax.all_gather(x.astype(jnp.bfloat16), axis)
    state = jnp.zeros_like(x) + jnp.asarray(neutral, x.dtype)

    def one(lap, state):
        return join(state, lax.dynamic_index_in_dim(gathered, lap, 0, False).astype(x.dtype))

    return lax.fori_loop(0, place, one, state)


def from_behind(block, axis, distance):
    devices = range(lax.axis_size(axis))
    route = [(i - distance, i) for i in devices if i - distance in devices]
    return lax.ppermute(block, axis, route)


def normalize(value):
    return value * lax.rsqrt(jnp.mean(value * value, axis=-1, keepdims=True) + 1e-06)


MESH = pl.DeviceIdType.MESH
VMEM_BYTES = 60 * 1024 * 1024
ADD_ROWS = 16
DOT_COLUMNS = 512
HID_COLUMNS = 256
NEAR_EIGHTHS = 5


def place(count):
    z = lax.axis_index("heads")
    c = lax.axis_index("ctx")
    beside = c + 1 - 2 * lax.rem(c, 2)
    across = lax.rem(c + 2, 4)
    diagonal = lax.rem(beside + 2, 4)
    return z, c, beside, across, diagonal


def greet(z, count, beside, across):
    barrier = pltpu.get_barrier_semaphore()

    def signal(target):
        pl.semaphore_signal(barrier, inc=1, device_id=target, device_id_type=MESH)

    signal({"ctx": beside})
    signal({"ctx": across})

    @pl.when(z > 0)
    def _():
        signal({"heads": z - 1})

    @pl.when(z < count - 1)
    def _():
        signal({"heads": z + 1})

    pl.semaphore_wait(barrier, 2 + jnp.minimum(z, 1) + jnp.minimum(count - 1 - z, 1))


def gather_kernel(count, kinds, *refs):
    size = len(kinds)
    groups = [refs[first * size : (first + 1) * size] for first in range(4)]
    own_sem = refs[4 * size]
    z, c, beside, across, diagonal = place(count)
    greet(z, count, beside, across)

    def origin(kind, source, full):
        if kind != "share":
            return source
        share = full.shape[1]
        return source.at[pl.ds(pl.multiple_of(c * share, share), share), :]

    def slot_of(kind, zz, cc):
        return {"group": cc * count + zz, "share": zz * 4 + cc, "line": zz}[kind]

    def copies(zz, cc, way, target, own=False):
        result = []
        for kind, source, full, send, recv in zip(kinds, *groups):
            if kind == "line" and (way > 1 or cc is not c):
                continue
            slot = slot_of(kind, zz, cc)
            result.append(
                pltpu.make_async_remote_copy(
                    src_ref=origin(kind, source, full) if own else full.at[slot],
                    dst_ref=full.at[slot],
                    send_sem=send.at[way, slot],
                    recv_sem=recv.at[slot],
                    device_id=target,
                    device_id_type=MESH,
                )
            )
        return result

    def start(zz, cc, way, target, own=False):
        for copy in copies(zz, cc, way, target, own):
            copy.start()

    def arrived(zz, cc):
        for copy in copies(zz, cc, 0, {"ctx": beside}):
            copy.wait_recv()

    def left(zz, cc, way, target):
        for copy in copies(zz, cc, way, target):
            copy.wait_send()

    def along(act, down, up, zz, **options):
        if down:

            @pl.when(z > 0)
            def _():
                act(zz, c, 0, {"heads": z - 1}, **options)

        if up:

            @pl.when(z < count - 1)
            def _():
                act(zz, c, 1, {"heads": z + 1}, **options)

        act(zz, c, 2, {"ctx": across}, **options)
        act(zz, c, 3, {"ctx": beside}, **options)

    local = [
        pltpu.make_async_copy(
            origin(kind, source, full), full.at[slot_of(kind, z, c)], own_sem.at[index]
        )
        for index, (kind, source, full) in enumerate(zip(kinds, *groups[:2]))
    ]
    for copy in local:
        copy.start()
    along(start, True, True, z, own=True)

    def over(zz):
        arrived(zz, across)
        start(zz, across, 3, {"ctx": beside})

    for d in range(1, count + 1):
        if d < count:

            @pl.when(z >= d)
            def _():
                arrived(z - d, c)
                along(start, False, True, z - d)

            @pl.when(z + d < count)
            def _():
                arrived(z + d, c)
                along(start, True, False, z + d)

        if d == 1:
            over(z)
        else:

            @pl.when(z >= d - 1)
            def _():
                over(z - d + 1)

            @pl.when(z + d - 1 < count)
            def _():
                over(z + d - 1)

    for zz in range(count):
        arrived(zz, beside)
        arrived(zz, diagonal)
    for copy in local:
        copy.wait()
    along(left, True, True, z)
    for d in range(1, count):

        @pl.when(z >= d)
        def _():
            along(left, False, True, z - d)

        @pl.when(z + d < count)
        def _():
            along(left, True, False, z + d)

    for zz in range(count):
        left(zz, across, 3, {"ctx": beside})


def expert_kernel(
    count, near_rows, hidden_ref, own_ref, table_ref, gate_hbm, up_hbm, down_hbm, out_ref,
    rows_ref, part_ref, hid_ref, scale_ref, gate_ref, up_ref, down_ref,
    from_beside, to_across, from_across, line_out, line_in, last_out, last_in,
    local_sem, row_send, row_recv, beside_send, beside_recv, across_send, across_recv,
    line_send, line_recv, last_send, last_recv,
):
    z, c, beside, across, diagonal = place(count)
    row_count, width = own_ref.shape
    far_rows = row_count - near_rows
    spans = [(0, near_rows), (near_rows, far_rows)]
    expert = c * count + z
    local = [
        pltpu.make_async_copy(source, target, local_sem.at[index])
        for index, (source, target) in enumerate(
            [
                (gate_hbm, gate_ref),
                (up_hbm, up_ref),
                (down_hbm, down_ref),
                (own_ref, rows_ref.at[z, pl.ds(pl.multiple_of(c * row_count, row_count), row_count), :]),
            ]
        )
    ]
    for copy in local:
        copy.start()
    greet(z, count, beside, across)

    def window(cc, span):
        first, size = spans[span]
        return pl.ds(pl.multiple_of(cc * row_count + first, 16), size)

    def row_copy(zz, cc, span, way, target, own=False):
        first, size = spans[span]
        slot = zz * 4 + cc
        block = rows_ref.at[zz, window(cc, span), :]
        return pltpu.make_async_remote_copy(
            src_ref=own_ref.at[pl.ds(first, size), :] if own else block,
            dst_ref=block,
            send_sem=row_send.at[way, span, slot],
            recv_sem=row_recv.at[span, slot],
            device_id=target,
            device_id_type=MESH,
        )

    def started(copy):
        copy.start()

    def left(copy):
        copy.wait_send()

    def received(zz, cc, span):
        row_copy(zz, cc, span, 0, {"ctx": beside}).wait_recv()

    def along(act, zz, cc, span, own=False):
        @pl.when(jnp.logical_and(zz >= z, z > 0))
        def _():
            act(row_copy(zz, cc, span, 0, {"heads": z - 1}, own))

        @pl.when(jnp.logical_and(zz <= z, z < count - 1))
        def _():
            act(row_copy(zz, cc, span, 1, {"heads": z + 1}, own))

    def over(act, zz, cc, span, own=False):
        act(row_copy(zz, cc, span, 2, {"ctx": across}, own))

    def aside(act, zz, cc, span, own=False):
        act(row_copy(zz, cc, span, 3, {"ctx": beside}, own))

    def own_sends(act, own):
        for span in (0, 1):
            along(act, z, c, span, own)
            over(act, z, c, span, own)
        for span in (0, 1):
            aside(act, z, c, span, own)

    def own_plane_sends(act, wait):
        for span in (1, 0):
            if wait:
                received(z, across, span)
            if span == 1:
                along(act, z, across, span)
            aside(act, z, across, span)

    def line_sends(act, wait, zz):
        for span in (0, 1):
            if wait:
                received(zz, c, span)
            along(act, zz, c, span)
            if span == 0:
                over(act, zz, c, span)
            aside(act, zz, c, span)
        if wait:
            received(zz, across, 1)
        along(act, zz, across, 1)
        aside(act, zz, across, 1)

    def side_sends(act, wait, zz):
        if wait:
            received(zz, across, 0)
        aside(act, zz, across, 0)

    def near(index):
        index = count - 1 - index
        more = jnp.maximum(z, count - 1 - z)
        fewer = count - 1 - more
        alone = more - fewer
        paired = jnp.maximum(index - alone, 0)
        up = jnp.where(z + more < count, more - index, index - more)
        both = (fewer - paired // 2) * (1 - 2 * (paired % 2))
        offset = jnp.where(index < alone, up, both)
        return z + jnp.where(index < count - 1, offset, 0)

    def compute(zz):
        for cc in range(4):
            row = table_ref[cc * count + zz, pl.ds(expert, 1), :]
            scale_ref[cc * row_count : (cc + 1) * row_count, :] = jnp.broadcast_to(
                row, (HDIM, row_count)
            ).T

        inner = gate_ref.shape[1]

        def hidden_tile(index, _):
            columns = pl.ds(pl.multiple_of(index * HID_COLUMNS, HID_COLUMNS), HID_COLUMNS)
            gate = jnp.dot(rows_ref[zz], gate_ref[:, columns], preferred_element_type=jnp.float32)
            up = jnp.dot(rows_ref[zz], up_ref[:, columns], preferred_element_type=jnp.float32)
            scale = jnp.concatenate([scale_ref[...]] * (HID_COLUMNS // HDIM), axis=1)
            hid_ref[:, columns] = (jax.nn.silu(gate) * up * scale).astype(hid_ref.dtype)
            return 0

        lax.fori_loop(0, inner // HID_COLUMNS, hidden_tile, 0)

        def out_tile(index, _):
            columns = pl.ds(pl.multiple_of(index * DOT_COLUMNS, DOT_COLUMNS), DOT_COLUMNS)
            product = jnp.dot(
                hid_ref[...], down_ref[:, columns], preferred_element_type=jnp.float32
            )
            part_ref[zz, :, columns] = product.astype(part_ref.dtype)
            return 0

        lax.fori_loop(0, width // DOT_COLUMNS, out_tile, 0)

    def beside_copy(kind, zz):
        cc = diagonal if kind == 0 else beside
        return pltpu.make_async_remote_copy(
            src_ref=part_ref.at[zz, pl.ds(pl.multiple_of(cc * row_count, row_count), row_count), :],
            dst_ref=from_beside.at[kind, zz],
            send_sem=beside_send.at[kind, zz],
            recv_sem=beside_recv.at[kind, zz],
            device_id={"ctx": beside},
            device_id_type=MESH,
        )

    def across_copy(zz):
        return pltpu.make_async_remote_copy(
            src_ref=to_across.at[zz],
            dst_ref=from_across.at[zz],
            send_sem=across_send.at[zz],
            recv_sem=across_recv.at[zz],
            device_id={"ctx": across},
            device_id_type=MESH,
        )

    line_spans = [(0, near_rows), (near_rows, far_rows), (row_count, far_rows)]

    def line_copy(side, zz, chunk):
        first, size = line_spans[chunk]
        return pltpu.make_async_remote_copy(
            src_ref=line_out.at[zz, pl.ds(first, size), :],
            dst_ref=line_in.at[side, zz, pl.ds(first, size), :],
            send_sem=line_send.at[chunk, zz],
            recv_sem=line_recv.at[chunk, side, zz],
            device_id={"heads": z + 1 - 2 * side},
            device_id_type=MESH,
        )

    def last_copy():
        return pltpu.make_async_remote_copy(
            src_ref=last_out,
            dst_ref=last_in,
            send_sem=last_send,
            recv_sem=last_recv,
            device_id={"ctx": across},
            device_id_type=MESH,
        )

    def add(target, sources):
        def chunk(index, _):
            rows = pl.ds(pl.multiple_of(index * ADD_ROWS, ADD_ROWS), ADD_ROWS)
            total = sources[0][rows, :].astype(jnp.float32)
            for source in sources[1:]:
                total = total + source[rows, :].astype(jnp.float32)
            target[rows, :] = total.astype(target.dtype)
            return 0

        lax.fori_loop(0, target.shape[0] // ADD_ROWS, chunk, 0)

    def chip_sources(zz, chunk):
        cc, kind = (across, 0) if chunk == 2 else (c, 1)
        span = 0 if chunk == 0 else 1
        first, size = spans[span]
        sources = [
            part_ref.at[zz, window(cc, span), :],
            from_beside.at[kind, zz, pl.ds(first, size), :],
        ]
        return sources + ([from_across.at[zz]] if chunk == 0 else [])

    def exchange(zz):
        beside_copy(0, zz).start()
        beside_copy(1, zz).start()
        beside_copy(0, zz).wait_recv()
        add(
            to_across.at[zz],
            [part_ref.at[zz, window(across, 0), :], from_beside.at[0, zz, pl.ds(0, near_rows), :]],
        )
        across_copy(zz).start()
        beside_copy(1, zz).wait_recv()

    def line_block(side, zz, chunk):
        first, size = line_spans[chunk]
        return line_in.at[side, zz, pl.ds(first, size), :]

    def starts(side):
        return z == side * (count - 1)

    def pass_line(side, zz):
        for chunk in (1, 2, 0):
            if chunk == 0:
                across_copy(zz).wait_recv()

            @pl.when(jnp.logical_not(starts(side)))
            def _():
                line_copy(side, zz, chunk).wait_recv()

            first, size = line_spans[chunk]
            add(
                line_out.at[zz, pl.ds(first, size), :],
                chip_sources(zz, chunk) + [line_block(side, zz, chunk)],
            )
            line_copy(side, zz, chunk).start()

    own_sends(started, True)

    for side in (0, 1):

        @pl.when(starts(side))
        def _():
            def clear(index, _):
                line_in[side, index] = jnp.zeros(line_in.shape[2:], line_in.dtype)
                return 0

            lax.fori_loop(0, count, clear, 0)

    for copy in local:
        copy.wait()
    own_plane_sends(started, True)

    def distance(zz):
        return jnp.abs(zz - z)

    end_side = jnp.where(z == 0, 0, 1)
    at_end = jnp.logical_or(z == 0, z == count - 1)

    def step(index, _):
        zz = near(index)
        before = near(jnp.maximum(index - 1, 0))
        after = near(jnp.minimum(index + 1, count - 1))
        opens = jnp.logical_and(index > 0, distance(zz) != distance(before))

        @pl.when(opens)
        def _():
            line_sends(started, True, zz)

        @pl.when(jnp.logical_and(opens, jnp.logical_and(index < count - 1, distance(after) == distance(zz))))
        def _():
            line_sends(started, True, after)

        @pl.when(jnp.logical_and(at_end, index > 1))
        def _():
            pass_line(end_side, before)

        @pl.when(index > 0)
        def _():
            side_sends(started, True, zz)

        for span in (0, 1):
            received(zz, beside, span)
            received(zz, diagonal, span)
        compute(zz)
        exchange(zz)
        return 0

    lax.fori_loop(0, count, step, 0)

    def link(index, _):
        key = index // 2 + 1
        low = z < count - 1 - z
        side = jnp.where(low, index % 2, 1 - index % 2)
        zz = jnp.where(side == 0, key, count - 1 - key)
        valid = jnp.where(side == 0, zz > z, zz < z)
        done = jnp.logical_and(starts(side), key < count - 1)

        @pl.when(jnp.logical_and(valid, jnp.logical_not(done)))
        def _():
            pass_line(side, zz)

        return 0

    lax.fori_loop(0, 2 * (count - 1), link, 0)

    def both_sides(chunk):
        for side in (0, 1):

            @pl.when(jnp.logical_not(starts(side)))
            def _():
                line_copy(side, z, chunk).wait_recv()

        return [line_block(side, z, chunk) for side in (0, 1)]

    sides = both_sides(2)
    add(last_out, chip_sources(z, 2) + sides)
    last_copy().start()
    across_copy(z).wait_recv()
    sides = both_sides(0)
    add(
        out_ref.at[pl.ds(0, near_rows), :],
        [hidden_ref.at[pl.ds(0, near_rows), :]] + chip_sources(z, 0) + sides,
    )
    sides = both_sides(1)
    last_copy().wait_recv()
    add(
        out_ref.at[pl.ds(near_rows, far_rows), :],
        [hidden_ref.at[pl.ds(near_rows, far_rows), :]] + chip_sources(z, 1) + sides + [last_in],
    )

    last_copy().wait_send()
    own_sends(left, True)
    own_plane_sends(left, False)

    def drain(zz, _):
        beside_copy(0, zz).wait_send()
        beside_copy(1, zz).wait_send()
        across_copy(zz).wait_send()

        @pl.when(zz != z)
        def _():
            line_sends(left, False, zz)
            side_sends(left, False, zz)
            side = jnp.where(zz > z, 0, 1)
            for chunk in range(3):
                line_copy(side, zz, chunk).wait_send()

        return 0

    lax.fori_loop(0, count, drain, 0)


def gather_blocks(kinds, operands, collective_id, name):
    count, ctx_count = lax.axis_size("heads"), lax.axis_size("ctx")
    slots = [count if kind == "line" else count * ctx_count for kind in kinds]
    shapes = [
        (value.shape[0] // ctx_count if kind == "share" else value.shape[0], value.shape[1])
        for kind, value in zip(kinds, operands)
    ]
    return pl.pallas_call(
        functools.partial(gather_kernel, count, kinds),
        out_shape=[
            jax.ShapeDtypeStruct((slot,) + shape, value.dtype)
            for slot, shape, value in zip(slots, shapes, operands)
        ],
        in_specs=[pl.BlockSpec(memory_space=pltpu.VMEM)] * len(kinds),
        out_specs=[pl.BlockSpec(memory_space=pl.ANY)] * len(kinds),
        scratch_shapes=[pltpu.SemaphoreType.DMA((4, slot)) for slot in slots]
        + [pltpu.SemaphoreType.DMA((slot,)) for slot in slots]
        + [pltpu.SemaphoreType.DMA((len(kinds),))],
        compiler_params=pltpu.CompilerParams(
            collective_id=collective_id, has_side_effects=True
        ),
        name=name,
    )(*operands)


def near_share(row_count):
    return max(16, row_count * NEAR_EIGHTHS // 8 // 16 * 16)


def run_experts(hidden, normed, tables, w_gate, w_up, w_down):
    count = lax.axis_size("heads")
    row_count, width = normed.shape
    inner = w_gate.shape[1]
    near_rows = near_share(row_count)
    far_rows = row_count - near_rows
    dma = pltpu.SemaphoreType.DMA
    kind = normed.dtype
    vmem, anywhere = pl.BlockSpec(memory_space=pltpu.VMEM), pl.BlockSpec(memory_space=pl.ANY)
    return pl.pallas_call(
        functools.partial(expert_kernel, count, near_rows),
        out_shape=jax.ShapeDtypeStruct((row_count, width), kind),
        in_specs=[vmem] * 3 + [anywhere] * 3,
        out_specs=vmem,
        scratch_shapes=[
            pltpu.VMEM((count, 4 * row_count, width), kind),
            pltpu.VMEM((count, 4 * row_count, width), kind),
            pltpu.VMEM((4 * row_count, inner), kind),
            pltpu.VMEM((4 * row_count, HDIM), jnp.float32),
            pltpu.VMEM(w_gate.shape, kind),
            pltpu.VMEM(w_up.shape, kind),
            pltpu.VMEM(w_down.shape, kind),
            pltpu.VMEM((2, count, row_count, width), kind),
            pltpu.VMEM((count, near_rows, width), kind),
            pltpu.VMEM((count, near_rows, width), kind),
            pltpu.VMEM((count, row_count + far_rows, width), kind),
            pltpu.VMEM((2, count, row_count + far_rows, width), kind),
            pltpu.VMEM((far_rows, width), kind),
            pltpu.VMEM((far_rows, width), kind),
            dma((4,)),
            dma((4, 2, 4 * count)),
            dma((2, 4 * count)),
            dma((2, count)),
            dma((2, count)),
            dma((count,)),
            dma((count,)),
            dma((3, count)),
            dma((3, 2, count)),
            dma(()),
            dma(()),
        ],
        compiler_params=pltpu.CompilerParams(
            collective_id=0, has_side_effects=True, vmem_limit_bytes=VMEM_BYTES
        ),
        name="run_experts",
    )(hidden, normed, tables, w_gate, w_up, w_down)


def expert_table(expert_ids, gate_weights, expert_count):
    chosen = expert_ids[:, :, None] == jnp.arange(expert_count, dtype=jnp.int32)
    return jnp.sum(jnp.where(chosen, gate_weights[:, :, None], 0.0), axis=1).T


def gather_inputs(tokens, w_out, table):
    slab, w_rows, tables = gather_blocks(
        ("line", "share", "group"), (tokens, w_out, table), 2, "gather_inputs"
    )
    return slab.reshape(-1, tokens.shape[1]), w_rows.reshape(-1, w_out.shape[1]), tables


def on_device(
    tokens, state_in, past_kv, w_qkv, w_out, w_gate, w_up, w_down, expert_ids, gate_weights
):
    row_count, model_width = tokens.shape
    inner_width = w_qkv.shape[2]
    local_heads = inner_width // HDIM
    w_flat = w_qkv.reshape(model_width, 3 * inner_width)
    ctx_count = lax.axis_size("ctx")
    head_count = lax.axis_size("heads")
    exp_local = w_gate.shape[0]
    devices = ctx_count * head_count
    expert_count = exp_local * devices
    top_count = expert_ids.shape[1]
    capacity = max(2, 2 * row_count * top_count // expert_count)
    dense = (
        ctx_count == 4
        and exp_local == 1
        and row_count % HDIM == 0
        and w_out.shape[0] % 64 == 0
        and w_gate.shape[2] % HID_COLUMNS == 0
        and row_count * devices <= expert_count * capacity
    )
    if dense:
        table = expert_table(expert_ids, gate_weights, expert_count)
        slab, w_rows, tables = gather_inputs(tokens, w_out, table)
    else:
        slab, w_rows = [
            lax.all_gather(value, "heads", axis=0, tiled=True) for value in (tokens, w_out)
        ]
    projected = jnp.dot(
        slab,
        w_flat,
        preferred_element_type=jnp.float32,
    ).astype(jnp.bfloat16)
    slab_rows = projected.shape[0]
    projected = projected.reshape(slab_rows, 3, local_heads, HDIM)
    query = jnp.transpose(projected[:, 0], (1, 0, 2))
    keys = jnp.transpose(projected[:, 1], (1, 0, 2))
    values = jnp.transpose(projected[:, 2], (1, 0, 2))
    local_state = jnp.einsum("hsd,hse->hde", keys, values, preferred_element_type=jnp.float32)
    earlier_state = entering(
        local_state, "ctx", lambda first, second: first + second, jnp.zeros_like(local_state)
    )
    start_state = state_in + earlier_state
    tail = jnp.stack([keys, values], axis=0)
    arrived = from_behind(tail, "ctx", 1)
    past = jnp.transpose(past_kv.reshape(2, WINDOW, local_heads, HDIM), (0, 2, 1, 3))
    previous = jnp.where(lax.axis_index("ctx") == 0, past, arrived)
    all_keys = jnp.concatenate([previous[0], keys], axis=1)
    all_values = jnp.concatenate([previous[1], values], axis=1)
    block_rows = min(slab_rows, 512)
    block_count = slab_rows // block_rows
    scale = 1.0 / math.sqrt(HDIM)
    causal = jnp.arange(block_rows)[:, None] >= jnp.arange(block_rows)[None, :]
    offsets = jnp.arange(WINDOW + block_rows)[None, :] - jnp.arange(block_rows)[:, None]
    in_window = (offsets > 0) & (offsets <= WINDOW)

    def block_step(state, index):
        first = index * block_rows
        carried = jnp.einsum(
            "hsd,hde->hse", query.astype(jnp.float32), state, precision=lax.Precision.HIGHEST
        )
        inside = jnp.einsum("hsd,htd->hst", query, keys, preferred_element_type=jnp.float32)
        inside = jnp.where(causal[None], inside, 0.0).astype(jnp.bfloat16)
        linear = carried + jnp.einsum(
            "hst,hte->hse", inside, values, preferred_element_type=jnp.float32
        )
        scores = (
            jnp.einsum("hsd,htd->hst", query, all_keys, preferred_element_type=jnp.float32) * scale
        )
        scores = jnp.where(in_window[None], scores, -jnp.inf)
        top_score = jnp.max(scores, axis=-1, keepdims=True)
        expo = jnp.exp(scores - top_score)
        probs = (expo / jnp.sum(expo, axis=-1, keepdims=True)).astype(jnp.bfloat16)
        window_out = jnp.einsum(
            "hst,hte->hse", probs, all_values, preferred_element_type=jnp.float32
        )
        combined = (normalize(linear) + window_out).astype(jnp.bfloat16)
        new_state = state + jnp.einsum(
            "hsd,hse->hde", keys, values, preferred_element_type=jnp.float32
        )
        return (new_state, combined)

    _, outs = lax.scan(block_step, start_state, jnp.arange(block_count, dtype=jnp.int32))
    heads_out = jnp.transpose(outs, (0, 2, 1, 3)).reshape(slab_rows, inner_width)
    regrouped = lax.all_to_all(heads_out, "heads", split_axis=0, concat_axis=1, tiled=True)
    attn = jnp.dot(
        regrouped,
        w_rows,
        preferred_element_type=jnp.float32,
    )
    hidden_state = (tokens.astype(jnp.float32) + attn).astype(jnp.bfloat16)
    hidden_float = hidden_state.astype(jnp.float32)
    normed = normalize(hidden_float).astype(jnp.bfloat16)
    if dense:
        return run_experts(hidden_state, normed, tables, w_gate[0], w_up[0], w_down[0])
    picks = expert_ids.reshape(-1)
    onehot = (picks[:, None] == jnp.arange(expert_count, dtype=jnp.int32)[None, :]).astype(
        jnp.int32
    )
    earlier = jnp.cumsum(onehot, axis=0) - onehot
    slots = jnp.sum(onehot * earlier, axis=1)
    destination = picks * capacity + slots
    source_rows = jnp.arange(row_count * top_count, dtype=jnp.int32) // top_count
    outgoing = jnp.zeros((expert_count * capacity, model_width), jnp.bfloat16)
    outgoing = outgoing.at[destination].set(normed[source_rows])
    sendable = outgoing.reshape(expert_count, 1, capacity, model_width)
    arrived_rows = lax.all_to_all(
        sendable, ("ctx", "heads"), split_axis=0, concat_axis=1, tiled=True
    )
    e_count, n_count, c_count, d_count = arrived_rows.shape
    flat = arrived_rows.reshape(e_count, n_count * c_count, d_count)
    gate_act = jnp.einsum("erd,edf->erf", flat, w_gate, preferred_element_type=jnp.float32)
    up_act = jnp.einsum("erd,edf->erf", flat, w_up, preferred_element_type=jnp.float32)
    hid = (jax.nn.silu(gate_act) * up_act).astype(jnp.bfloat16)
    out_rows = jnp.einsum("erf,efd->erd", hid, w_down, preferred_element_type=jnp.float32)
    finished = out_rows.astype(jnp.bfloat16).reshape(e_count, n_count, c_count, d_count)
    returned = lax.all_to_all(finished, ("ctx", "heads"), split_axis=1, concat_axis=0, tiled=True)
    returned = returned.reshape(expert_count * capacity, model_width)
    picked = returned[destination].reshape(row_count, top_count, model_width).astype(jnp.float32)
    routed = jnp.sum(gate_weights[:, :, None] * picked, axis=1)
    return (hidden_float + routed).astype(jnp.bfloat16)


def solution(mesh):
    return jax.shard_map(
        on_device,
        mesh=mesh,
        in_specs=(
            P(("groups", "ctx", "heads"), None),
            P("heads", "groups", None),
            P(None, "groups", "heads"),
            P(None, None, "heads"),
            P("heads", None),
            P(("ctx", "heads"), None, None),
            P(("ctx", "heads"), None, None),
            P(("ctx", "heads"), None, None),
            P(("groups", "ctx", "heads"), None),
            P(("groups", "ctx", "heads"), None),
        ),
        out_specs=P(("groups", "ctx", "heads"), None),
        check_vma=False,
    )
```

```python
import functools
import math

import jax
import jax.numpy as jnp
from jax import lax
from jax.experimental import pallas as pl
from jax.experimental.pallas import tpu as pltpu
from jax.sharding import PartitionSpec as P

HDIM = 128
WINDOW = 512


def entering(x, axis, join, neutral):
    place = lax.axis_index(axis)
    gathered = lax.all_gather(x.astype(jnp.bfloat16), axis)
    state = jnp.zeros_like(x) + jnp.asarray(neutral, x.dtype)

    def one(lap, state):
        return join(state, lax.dynamic_index_in_dim(gathered, lap, 0, False).astype(x.dtype))

    return lax.fori_loop(0, place, one, state)


def from_behind(block, axis, distance):
    devices = range(lax.axis_size(axis))
    route = [(i - distance, i) for i in devices if i - distance in devices]
    return lax.ppermute(block, axis, route)


def normalize(value):
    return value * lax.rsqrt(jnp.mean(value * value, axis=-1, keepdims=True) + 1e-06)


MESH = pl.DeviceIdType.MESH
VMEM_BYTES = 60 * 1024 * 1024
FRONT_BYTES = 60 * 1024 * 1024
ADD_ROWS = 16
DOT_COLUMNS = 512
HID_COLUMNS = 256
LOAD_TIME = 0.6
UNIT_TIME = 0.75
SLACK = 0.05
NEAR_EIGHTHS = 5


def place(count):
    z = lax.axis_index("heads")
    c = lax.axis_index("ctx")
    beside = c + 1 - 2 * lax.rem(c, 2)
    across = lax.rem(c + 2, 4)
    diagonal = lax.rem(beside + 2, 4)
    return z, c, beside, across, diagonal


def greet(z, count, beside, across):
    barrier = pltpu.get_barrier_semaphore()

    def signal(target):
        pl.semaphore_signal(barrier, inc=1, device_id=target, device_id_type=MESH)

    signal({"ctx": beside})
    signal({"ctx": across})

    @pl.when(z > 0)
    def _():
        signal({"heads": z - 1})

    @pl.when(z < count - 1)
    def _():
        signal({"heads": z + 1})

    pl.semaphore_wait(barrier, 2 + jnp.minimum(z, 1) + jnp.minimum(count - 1 - z, 1))


def nearest(count, z, index):
    index = count - 1 - index
    more = jnp.maximum(z, count - 1 - z)
    fewer = count - 1 - more
    alone = more - fewer
    paired = jnp.maximum(index - alone, 0)
    up = jnp.where(z + more < count, more - index, index - more)
    both = (fewer - paired // 2) * (1 - 2 * (paired % 2))
    offset = jnp.where(index < alone, up, both)
    return z + jnp.where(index < count - 1, offset, 0)


def attend_kernel(
    count, tokens_ref, share_hbm, table_ref, state_ref, past_hbm, qkv_hbm,
    hidden_ref, normed_ref, tables_ref,
    slab_ref, qkv_ref, w_ref, query_ref, kv_ref, before_ref, inside_ref, linear_ref,
    state_out, states_in, heads_out, heads_in,
    local_sem, token_send, token_recv, share_send, share_recv,
    tail_send, tail_recv, state_send, state_recv, head_send, head_recv,
):
    z, c, beside, across, diagonal = place(count)
    row_count, width = tokens_ref.shape
    slab_rows = count * row_count
    share = w_ref.shape[0] // (4 * count)

    def rows_of(index, size):
        return pl.ds(pl.multiple_of(index * size, size), size)

    def share_block(kind, zz, cc):
        if kind == 0:
            return w_ref.at[rows_of(zz * 4 + cc, share), :]
        return tables_ref.at[cc * count + zz]

    def share_source(kind):
        return table_ref if kind else share_hbm.at[rows_of(c, share), :]

    local = [
        pltpu.make_async_copy(source, target, local_sem.at[index])
        for index, (source, target) in enumerate(
            [(qkv_hbm.at[one], qkv_ref.at[:, one * HDIM : (one + 1) * HDIM]) for one in range(3)]
            + [(tokens_ref, slab_ref.at[z])]
            + [(share_source(kind), share_block(kind, z, c)) for kind in (0, 1)]
        )
    ]
    past_copy = pltpu.make_async_copy(past_hbm, before_ref, local_sem.at[6])
    for copy in local:
        copy.start()

    @pl.when(c == 0)
    def _():
        past_copy.start()

    barrier = pltpu.get_barrier_semaphore()
    for target in (beside, across, diagonal):
        pl.semaphore_signal(barrier, inc=1, device_id={"ctx": target}, device_id_type=MESH)
    for zz in range(count):

        @pl.when(zz != z)
        def _():
            pl.semaphore_signal(barrier, inc=1, device_id={"heads": zz}, device_id_type=MESH)

    pl.semaphore_wait(barrier, 3 + count - 1)

    def remote(source, target, send, recv, device):
        return pltpu.make_async_remote_copy(
            src_ref=source, dst_ref=target, send_sem=send, recv_sem=recv,
            device_id=device, device_id_type=MESH,
        )

    def started(copy):
        copy.start()

    def left(copy):
        copy.wait_send()

    def along(act, zz, copy):
        @pl.when(jnp.logical_and(zz >= z, z > 0))
        def _():
            act(copy(0, {"heads": z - 1}))

        @pl.when(jnp.logical_and(zz <= z, z < count - 1))
        def _():
            act(copy(1, {"heads": z + 1}))

    def token_copy(zz, own=False):
        def copy(way, device):
            source = tokens_ref if own else slab_ref.at[zz]
            return remote(source, slab_ref.at[zz], token_send.at[way, zz], token_recv.at[zz], device)

        return copy

    def share_copy(kind, zz, cc, own=False):
        def copy(way, device):
            block = share_block(kind, zz, cc)
            slot = zz * 4 + cc
            source = share_source(kind) if own else block
            return remote(
                source, block, share_send.at[kind, way, slot], share_recv.at[kind, slot], device
            )

        return copy

    def aside(act, zz, cc, own=False):
        for kind in (0, 1):
            act(share_copy(kind, zz, cc, own)(3, {"ctx": beside}))

    def share_relay(act, zz, own=False):
        for kind in (0, 1):
            act(share_copy(kind, zz, c, own)(2, {"ctx": across}))
        aside(act, zz, c, own)

    def share_along(act, zz, own=False):
        for kind in (0, 1):
            along(act, zz, share_copy(kind, zz, c, own))

    def share_received(zz, cc):
        for kind in (0, 1):
            share_copy(kind, zz, cc)(3, {"ctx": beside}).wait_recv()

    def at_distance(distance, act):
        @pl.when(z >= distance)
        def _():
            act(z - distance)

        @pl.when(z + distance < count)
        def _():
            act(z + distance)

    def share_stage(distance):
        def one(zz):
            share_received(zz, c)
            share_along(started, zz)
            share_relay(started, zz)

        at_distance(distance, one)

    def share_over(zz):
        share_received(zz, across)
        aside(started, zz, across)

    along(started, z, token_copy(z, True))
    share_relay(started, z, True)
    for copy in local:
        copy.wait()

    def project(zz):
        product = jnp.dot(slab_ref[zz], qkv_ref[...], preferred_element_type=jnp.float32)
        product = product.astype(query_ref.dtype)
        rows = rows_of(zz, row_count)
        query_ref[rows, :] = product[:, :HDIM]
        kv_ref[0, rows, :] = product[:, HDIM : 2 * HDIM]
        kv_ref[1, rows, :] = product[:, 2 * HDIM :]

    def token_relay(zz):
        token_copy(zz)(0, {"heads": z - 1}).wait_recv()
        along(started, zz, token_copy(zz))

    def step(index, _):
        zz = nearest(count, z, index)
        last = nearest(count, z, jnp.maximum(index - 1, 0))
        after = nearest(count, z, jnp.minimum(index + 1, count - 1))
        opens = jnp.logical_and(index > 0, jnp.abs(zz - z) != jnp.abs(last - z))
        double = jnp.logical_and(index < count - 1, jnp.abs(after - z) == jnp.abs(zz - z))

        @pl.when(opens)
        def _():
            token_relay(zz)

        @pl.when(jnp.logical_and(opens, double))
        def _():
            token_relay(after)

        project(zz)
        return 0

    lax.fori_loop(0, count, step, 0)

    tail = remote(kv_ref, before_ref, tail_send, tail_recv, {"ctx": jnp.minimum(c + 1, 3)})

    @pl.when(c < 3)
    def _():
        tail.start()

    local_state = lax.dot_general(
        kv_ref[0], kv_ref[1], (((0,), (0,)), ((), ())), preferred_element_type=jnp.float32
    )
    state_out[...] = local_state.astype(state_out.dtype)
    others = [beside, across, diagonal]
    state_copies = [
        remote(state_out, states_in.at[c], state_send.at[way], state_recv.at[c], {"ctx": target})
        for way, target in enumerate(others)
    ]
    for copy in state_copies:
        copy.start()
    share_along(started, z, True)
    share_over(z)

    blocks = slab_rows // row_count
    for block in range(blocks):
        first, end = block * row_count, (block + 1) * row_count
        query = query_ref[first:end, :]
        scores = lax.dot_general(
            query, kv_ref[0, :end, :], (((1,), (1,)), ((), ())), preferred_element_type=jnp.float32
        )
        shape = scores.shape
        causal = lax.broadcasted_iota(jnp.int32, shape, 1) <= first + lax.broadcasted_iota(
            jnp.int32, shape, 0
        )
        inside_ref[first:end, :end] = scores
        weights = jnp.where(causal, scores, 0.0).astype(kv_ref.dtype)
        linear_ref[first:end, :] = jnp.dot(
            weights, kv_ref[1, :end, :], preferred_element_type=jnp.float32
        )

    if count > 1:
        share_stage(1)
    for target in others:
        remote(
            state_out, states_in.at[target], state_send.at[0], state_recv.at[target],
            {"ctx": beside},
        ).wait_recv()
    start = state_ref[...]
    for cc in range(4):
        start = start + jnp.where(cc < c, states_in[cc].astype(jnp.float32), 0.0)

    @pl.when(c == 0)
    def _():
        past_copy.wait()

    @pl.when(c > 0)
    def _():
        tail.wait_recv()

    scale = 1.0 / math.sqrt(HDIM)

    def head_copy(zz):
        columns = pl.ds(pl.multiple_of(z * HDIM, HDIM), HDIM)
        return remote(
            heads_out.at[zz], heads_in.at[:, columns], head_send.at[zz], head_recv.at[z],
            {"heads": zz},
        )

    for block in range(blocks):
        first, end = block * row_count, (block + 1) * row_count
        query = query_ref[first:end, :]
        old = lax.dot_general(
            query, before_ref[0, first:, :], (((1,), (1,)), ((), ())),
            preferred_element_type=jnp.float32,
        )
        old_seen = lax.broadcasted_iota(jnp.int32, old.shape, 1) > lax.broadcasted_iota(
            jnp.int32, old.shape, 0
        )
        old = jnp.where(old_seen, old * scale, -jnp.inf)
        new = inside_ref[first:end, :end]
        new_seen = lax.broadcasted_iota(jnp.int32, new.shape, 1) <= first + lax.broadcasted_iota(
            jnp.int32, new.shape, 0
        )
        new = jnp.where(new_seen, new * scale, -jnp.inf)
        top = jnp.maximum(
            jnp.max(old, axis=-1, keepdims=True), jnp.max(new, axis=-1, keepdims=True)
        )
        old = jnp.exp(old - top)
        new = jnp.exp(new - top)
        inverse = 1.0 / (
            jnp.sum(old, axis=-1, keepdims=True) + jnp.sum(new, axis=-1, keepdims=True)
        )
        window = jnp.dot(
            (old * inverse).astype(kv_ref.dtype), before_ref[1, first:, :],
            preferred_element_type=jnp.float32,
        ) + jnp.dot(
            (new * inverse).astype(kv_ref.dtype), kv_ref[1, :end, :],
            preferred_element_type=jnp.float32,
        )
        linear = linear_ref[first:end, :] + jnp.dot(
            query.astype(jnp.float32), start, precision=lax.Precision.HIGHEST,
            preferred_element_type=jnp.float32,
        )
        heads_out[block] = (normalize(linear) + window).astype(heads_out.dtype)

        @pl.when(block != z)
        def _():
            head_copy(block).start()

        @pl.when(block == z)
        def _():
            columns = pl.ds(pl.multiple_of(z * HDIM, HDIM), HDIM)
            heads_in[:, columns] = heads_out[block]

        if block + 1 < count:
            at_distance(block + 1, share_over)
        if block + 2 < count:
            share_stage(block + 2)

    for zz in range(count):
        share_received(zz, beside)
        share_received(zz, diagonal)

        @pl.when(zz != z)
        def _():
            remote(
                heads_out.at[zz], heads_in.at[:, zz * HDIM : (zz + 1) * HDIM], head_send.at[zz],
                head_recv.at[zz], {"heads": zz},
            ).wait_recv()

    def out_tile(index, total):
        columns = pl.ds(pl.multiple_of(index * DOT_COLUMNS, DOT_COLUMNS), DOT_COLUMNS)
        attn = jnp.dot(heads_in[...], w_ref[:, columns], preferred_element_type=jnp.float32)
        hidden = (tokens_ref[:, columns].astype(jnp.float32) + attn).astype(hidden_ref.dtype)
        hidden_ref[:, columns] = hidden
        hidden = hidden.astype(jnp.float32)
        return total + jnp.sum(hidden * hidden, axis=-1, keepdims=True)

    total = lax.fori_loop(
        0, width // DOT_COLUMNS, out_tile, jnp.zeros((row_count, 1), jnp.float32)
    )
    inverse = lax.rsqrt(total / width + 1e-06)
    for first in range(0, width, DOT_COLUMNS):
        hidden = hidden_ref[:, first : first + DOT_COLUMNS].astype(jnp.float32)
        normed_ref[:, first : first + DOT_COLUMNS] = (hidden * inverse).astype(normed_ref.dtype)

    along(left, z, token_copy(z, True))
    share_along(left, z, True)
    share_relay(left, z, True)

    @pl.when(c < 3)
    def _():
        tail.wait_send()

    for copy in state_copies:
        copy.wait_send()
    for zz in range(count):
        aside(left, zz, across)

        @pl.when(zz != z)
        def _():
            along(left, zz, token_copy(zz))
            share_along(left, zz)
            share_relay(left, zz)
            head_copy(zz).wait_send()


def plan_steps(count, at, share):
    near, far = 2 * share, 2 * (1 - share)
    stage = near + 2 * far

    def begin(place, zz):
        return (abs(zz - place) - 1) * stage

    def arrivals(place):
        events = [(2.0, ("cross", place)), (2.0, ("side", place))]
        ready = {(place, 0): LOAD_TIME, (place, 1): 2.1}
        link = 2.0
        for zz in sorted(set(range(count)) - {place}, key=lambda other: abs(other - place)):
            first = begin(place, zz)
            events.append((first + near, ("near", zz)))
            events.append((first + near + far, ("far", zz)))
            events.append((first + stage, ("cross", zz)))
            link = max(link, first + near) + near
            events.append((link, ("side", zz)))
            ready[zz, 0] = first + near + far + 0.1
            ready[zz, 1] = max(first + stage, link) + 0.1
        return sorted(events, key=lambda event: event[0]), ready

    def simulate(place):
        events, ready = arrivals(place)
        segments, order, now, ends, current = [], [], 0.0, {}, []
        while ready or events:
            while events and events[0][0] <= now + SLACK:
                when, op = events.pop(0)
                current.append(op)
                zz = op[-1]
                if op[0] == "exchange" and zz != place and place in (0, count - 1):
                    events.append((now, ("passfar", int(zz < place), zz)))
                    events.append((now + near + 0.3, ("passnear", int(zz < place), zz)))
                    events.sort(key=lambda event: event[0])
            able = [unit for unit in ready if ready[unit] <= now + SLACK]
            if not able and not ready and not events:
                break
            if not able:
                now = min([event[0] for event in events[:1]] + list(ready.values()))
                continue
            unit = min(able, key=lambda one: ready[one])
            del ready[unit]
            segments.append(current + [("pair",) + unit])
            order.append(unit)
            now += UNIT_TIME
            zz, pair = unit
            ends[zz] = ends.get(zz, 0) + 1
            current = [("beside", zz, 1 - pair)]
            if ends[zz] == 2:
                events.append((now + 0.5, ("exchange", zz)))
                events.sort(key=lambda event: event[0])
                ends[zz] = now + 1.0
        segments.append(current)
        return segments, order, ends

    everyone = [simulate(place) for place in range(count)]
    segments, order, _ = everyone[at]
    if 0 < at < count - 1:

        def chain(side, zz, place, op):
            own = everyone[place][2][zz] + (near if op == "passnear" else 0)
            if place == side * (count - 1):
                return own
            hop = near if op == "passnear" else 2 * far
            return max(own, chain(side, zz, place + 2 * side - 1, op) + hop + 0.2)

        passes = [
            (op, int(zz < at), zz)
            for zz in range(count)
            for op in ("passfar", "passnear")
            if zz != at
        ]
        passes.sort(key=lambda one: chain(one[1], one[2], at, one[0]))
        segments = segments[:-1] + [segments[-1] + passes]
    return segments, order


def expert_kernel(
    count, near_rows, hidden_ref, own_ref, table_ref, gate_hbm, up_hbm, down_hbm, out_ref,
    rows_ref, part_ref, hid_ref, scale_ref, gate_ref, up_ref, down_ref,
    from_beside, to_across, from_across, line_out, line_in, last_out, last_in,
    local_sem, row_send, row_recv, beside_send, beside_recv, across_send, across_recv,
    line_send, line_recv, last_send, last_recv,
):
    z, c, beside, across, diagonal = place(count)
    row_count, width = own_ref.shape
    far_rows = row_count - near_rows
    spans = [(0, near_rows), (near_rows, far_rows)]
    expert = c * count + z
    local = [
        pltpu.make_async_copy(source, target, local_sem.at[index])
        for index, (source, target) in enumerate(
            [
                (gate_hbm, gate_ref),
                (up_hbm, up_ref),
                (down_hbm, down_ref),
                (own_ref, rows_ref.at[z, pl.ds(pl.multiple_of(c * row_count, row_count), row_count), :]),
            ]
        )
    ]
    for copy in local:
        copy.start()
    greet(z, count, beside, across)

    def window(cc, span):
        first, size = spans[span]
        return pl.ds(pl.multiple_of(cc * row_count + first, 16), size)

    def row_copy(zz, cc, span, way, target, own=False):
        first, size = spans[span]
        slot = zz * 4 + cc
        block = rows_ref.at[zz, window(cc, span), :]
        return pltpu.make_async_remote_copy(
            src_ref=own_ref.at[pl.ds(first, size), :] if own else block,
            dst_ref=block,
            send_sem=row_send.at[way, span, slot],
            recv_sem=row_recv.at[span, slot],
            device_id=target,
            device_id_type=MESH,
        )

    def started(copy):
        copy.start()

    def left(copy):
        copy.wait_send()

    def received(zz, cc, span):
        row_copy(zz, cc, span, 0, {"ctx": beside}).wait_recv()

    def along(act, at, zz, cc, span, own=False):
        if zz >= at and at > 0:
            act(row_copy(zz, cc, span, 0, {"heads": at - 1}, own))
        if zz <= at and at < count - 1:
            act(row_copy(zz, cc, span, 1, {"heads": at + 1}, own))

    def over(act, zz, cc, span, own=False):
        act(row_copy(zz, cc, span, 2, {"ctx": across}, own))

    def aside(act, zz, cc, span, own=False):
        act(row_copy(zz, cc, span, 3, {"ctx": beside}, own))

    def own_sends(act, at):
        for span in (0, 1):
            along(act, at, at, c, span, True)
            over(act, at, c, span, True)
            aside(act, at, c, span, True)

    def relays(op, at, zz, act, wait):
        cc = c if op in ("near", "far") else across
        span = 0 if op in ("near", "side") else 1
        if wait:
            received(zz, cc, span)
        if op != "side":
            along(act, at, zz, cc, span)
        if op == "near":
            over(act, zz, cc, span)
        aside(act, zz, cc, span)

    def paired(zz, pair):
        for span in (0, 1):
            received(zz, diagonal if pair else beside, span)

    def compute(zz, pair):
        half = jnp.where(pair == 0, c // 2, 1 - c // 2)
        for core in range(2):
            row = table_ref[(half * 2 + core) * count + zz, pl.ds(expert, 1), :]
            scale_ref[core * row_count : (core + 1) * row_count, :] = jnp.broadcast_to(
                row, (HDIM, row_count)
            ).T

        inner = gate_ref.shape[1]
        rows = pl.ds(pl.multiple_of(half * 2 * row_count, 2 * row_count), 2 * row_count)

        def hidden_tile(index, _):
            columns = pl.ds(pl.multiple_of(index * HID_COLUMNS, HID_COLUMNS), HID_COLUMNS)
            block = rows_ref[zz, rows, :]
            gate = jnp.dot(block, gate_ref[:, columns], preferred_element_type=jnp.float32)
            up = jnp.dot(block, up_ref[:, columns], preferred_element_type=jnp.float32)
            scale = jnp.concatenate([scale_ref[...]] * (HID_COLUMNS // HDIM), axis=1)
            hid_ref[:, columns] = (jax.nn.silu(gate) * up * scale).astype(hid_ref.dtype)
            return 0

        lax.fori_loop(0, inner // HID_COLUMNS, hidden_tile, 0)

        def out_tile(index, _):
            columns = pl.ds(pl.multiple_of(index * DOT_COLUMNS, DOT_COLUMNS), DOT_COLUMNS)
            product = jnp.dot(
                hid_ref[...], down_ref[:, columns], preferred_element_type=jnp.float32
            )
            part_ref[zz, rows, columns] = product.astype(part_ref.dtype)
            return 0

        lax.fori_loop(0, width // DOT_COLUMNS, out_tile, 0)

    def beside_copy(kind, zz):
        cc = diagonal if kind == 0 else beside
        return pltpu.make_async_remote_copy(
            src_ref=part_ref.at[zz, pl.ds(pl.multiple_of(cc * row_count, row_count), row_count), :],
            dst_ref=from_beside.at[kind, zz],
            send_sem=beside_send.at[kind, zz],
            recv_sem=beside_recv.at[kind, zz],
            device_id={"ctx": beside},
            device_id_type=MESH,
        )

    def across_copy(zz):
        return pltpu.make_async_remote_copy(
            src_ref=to_across.at[zz],
            dst_ref=from_across.at[zz],
            send_sem=across_send.at[zz],
            recv_sem=across_recv.at[zz],
            device_id={"ctx": across},
            device_id_type=MESH,
        )

    line_spans = [(0, near_rows), (near_rows, far_rows), (row_count, far_rows)]

    def line_copy(side, zz, chunk):
        first, size = line_spans[chunk]
        return pltpu.make_async_remote_copy(
            src_ref=line_out.at[zz, pl.ds(first, size), :],
            dst_ref=line_in.at[side, zz, pl.ds(first, size), :],
            send_sem=line_send.at[chunk, zz],
            recv_sem=line_recv.at[chunk, side, zz],
            device_id={"heads": z + 1 - 2 * side},
            device_id_type=MESH,
        )

    def last_copy():
        return pltpu.make_async_remote_copy(
            src_ref=last_out,
            dst_ref=last_in,
            send_sem=last_send,
            recv_sem=last_recv,
            device_id={"ctx": across},
            device_id_type=MESH,
        )

    def add(target, sources):
        def chunk(index, _):
            rows = pl.ds(pl.multiple_of(index * ADD_ROWS, ADD_ROWS), ADD_ROWS)
            total = sources[0][rows, :].astype(jnp.float32)
            for source in sources[1:]:
                total = total + source[rows, :].astype(jnp.float32)
            target[rows, :] = total.astype(target.dtype)
            return 0

        lax.fori_loop(0, target.shape[0] // ADD_ROWS, chunk, 0)

    def chip_sources(zz, chunk):
        cc, kind = (across, 0) if chunk == 2 else (c, 1)
        span = 0 if chunk == 0 else 1
        first, size = spans[span]
        sources = [
            part_ref.at[zz, window(cc, span), :],
            from_beside.at[kind, zz, pl.ds(first, size), :],
        ]
        return sources + ([from_across.at[zz]] if chunk == 0 else [])

    def exchange(zz):
        beside_copy(0, zz).wait_recv()
        add(
            to_across.at[zz],
            [part_ref.at[zz, window(across, 0), :], from_beside.at[0, zz, pl.ds(0, near_rows), :]],
        )
        across_copy(zz).start()
        beside_copy(1, zz).wait_recv()

    def line_block(side, zz, chunk):
        first, size = line_spans[chunk]
        return line_in.at[side, zz, pl.ds(first, size), :]

    def starts(side, at):
        return at == side * (count - 1)

    def pass_line(at, side, zz, chunks):
        for chunk in chunks:
            if chunk == 0:
                across_copy(zz).wait_recv()
            sources = chip_sources(zz, chunk)
            if not starts(side, at):
                line_copy(side, zz, chunk).wait_recv()
                sources = sources + [line_block(side, zz, chunk)]
            first, size = line_spans[chunk]
            add(line_out.at[zz, pl.ds(first, size), :], sources)
            line_copy(side, zz, chunk).start()

    def perform(at, ops):
        for op, *where in ops:
            if op == "pair":
                paired(*where)
            elif op == "beside":
                beside_copy(where[1], where[0]).start()
            elif op == "exchange":
                exchange(*where)
            elif op == "passfar":
                pass_line(at, *where, (1, 2))
            elif op == "passnear":
                pass_line(at, *where, (0,))
            else:
                relays(op, at, where[0], started, True)

    def each_place(act):
        for at in range(count):

            @pl.when(z == at)
            def _():
                act(at)

    each_place(lambda at: own_sends(started, at))

    for copy in local:
        copy.wait()
    plans = [plan_steps(count, at, near_rows / row_count) for at in range(count)]
    units = 2 * count

    def choose(index, pick):
        value = jnp.int32(0)
        for at in range(count):
            for unit in range(units):
                here = jnp.logical_and(z == at, index == unit)
                value = jnp.where(here, pick(plans[at][1][unit]), value)
        return value

    def step(index, _):
        def segment(at):
            for unit in range(units):

                @pl.when(index == unit)
                def _():
                    perform(at, plans[at][0][unit])

        each_place(segment)
        compute(choose(index, lambda unit: unit[0]), choose(index, lambda unit: unit[1]))
        return 0

    lax.fori_loop(0, units, step, 0)
    each_place(lambda at: perform(at, plans[at][0][units]))

    def finish(at):
        sides = [side for side in (0, 1) if not starts(side, at)]

        def arrived(chunk):
            for side in sides:
                line_copy(side, at, chunk).wait_recv()
            return chip_sources(at, chunk) + [line_block(side, at, chunk) for side in sides]

        add(last_out, arrived(2))
        last_copy().start()
        across_copy(at).wait_recv()
        for chunk, (first, size) in enumerate(spans):
            rows = pl.ds(first, size)
            sources = arrived(chunk)
            if chunk == 1:
                last_copy().wait_recv()
                sources = sources + [last_in]
            add(out_ref.at[rows, :], [hidden_ref.at[rows, :]] + sources)
        last_copy().wait_send()
        own_sends(left, at)
        relays("side", at, at, left, False)
        relays("cross", at, at, left, False)
        for zz in range(count):
            beside_copy(0, zz).wait_send()
            beside_copy(1, zz).wait_send()
            across_copy(zz).wait_send()
            if zz != at:
                for op in ("near", "far", "cross", "side"):
                    relays(op, at, zz, left, False)
                for chunk in range(3):
                    line_copy(int(zz < at), zz, chunk).wait_send()

    each_place(finish)


def attend(tokens, w_out, table, state_in, past_kv, w_qkv):
    count = lax.axis_size("heads")
    row_count, width = tokens.shape
    slab_rows = count * row_count
    kind = tokens.dtype
    slots = 4 * count
    dma = pltpu.SemaphoreType.DMA
    vmem, anywhere = pl.BlockSpec(memory_space=pltpu.VMEM), pl.BlockSpec(memory_space=pl.ANY)
    return pl.pallas_call(
        functools.partial(attend_kernel, count),
        out_shape=[
            jax.ShapeDtypeStruct((row_count, width), kind),
            jax.ShapeDtypeStruct((row_count, width), kind),
            jax.ShapeDtypeStruct((slots,) + table.shape, table.dtype),
        ],
        in_specs=[vmem, anywhere, vmem, vmem, anywhere, anywhere],
        out_specs=[vmem, vmem, anywhere],
        scratch_shapes=[
            pltpu.VMEM((count, row_count, width), kind),
            pltpu.VMEM((width, 3 * HDIM), kind),
            pltpu.VMEM((count * HDIM, width), kind),
            pltpu.VMEM((slab_rows, HDIM), kind),
            pltpu.VMEM((2, slab_rows, HDIM), kind),
            pltpu.VMEM((2, WINDOW, HDIM), kind),
            pltpu.VMEM((slab_rows, slab_rows), jnp.float32),
            pltpu.VMEM((slab_rows, HDIM), jnp.float32),
            pltpu.VMEM((HDIM, HDIM), kind),
            pltpu.VMEM((4, HDIM, HDIM), kind),
            pltpu.VMEM((count, row_count, HDIM), kind),
            pltpu.VMEM((row_count, count * HDIM), kind),
            dma((7,)),
            dma((2, count)),
            dma((count,)),
            dma((2, 4, slots)),
            dma((2, slots)),
            dma(()),
            dma(()),
            dma((3,)),
            dma((4,)),
            dma((count,)),
            dma((count,)),
        ],
        compiler_params=pltpu.CompilerParams(
            collective_id=2, has_side_effects=True, vmem_limit_bytes=FRONT_BYTES
        ),
        name="attend",
    )(tokens, w_out, table, state_in, past_kv, w_qkv)


def near_share(row_count):
    return max(16, row_count * NEAR_EIGHTHS // 8 // 16 * 16)


def run_experts(hidden, normed, tables, w_gate, w_up, w_down):
    count = lax.axis_size("heads")
    row_count, width = normed.shape
    inner = w_gate.shape[1]
    near_rows = near_share(row_count)
    far_rows = row_count - near_rows
    dma = pltpu.SemaphoreType.DMA
    kind = normed.dtype
    vmem, anywhere = pl.BlockSpec(memory_space=pltpu.VMEM), pl.BlockSpec(memory_space=pl.ANY)
    return pl.pallas_call(
        functools.partial(expert_kernel, count, near_rows),
        out_shape=jax.ShapeDtypeStruct((row_count, width), kind),
        in_specs=[vmem] * 3 + [anywhere] * 3,
        out_specs=vmem,
        scratch_shapes=[
            pltpu.VMEM((count, 4 * row_count, width), kind),
            pltpu.VMEM((count, 4 * row_count, width), kind),
            pltpu.VMEM((2 * row_count, inner), kind),
            pltpu.VMEM((2 * row_count, HDIM), jnp.float32),
            pltpu.VMEM(w_gate.shape, kind),
            pltpu.VMEM(w_up.shape, kind),
            pltpu.VMEM(w_down.shape, kind),
            pltpu.VMEM((2, count, row_count, width), kind),
            pltpu.VMEM((count, near_rows, width), kind),
            pltpu.VMEM((count, near_rows, width), kind),
            pltpu.VMEM((count, row_count + far_rows, width), kind),
            pltpu.VMEM((2, count, row_count + far_rows, width), kind),
            pltpu.VMEM((far_rows, width), kind),
            pltpu.VMEM((far_rows, width), kind),
            dma((4,)),
            dma((4, 2, 4 * count)),
            dma((2, 4 * count)),
            dma((2, count)),
            dma((2, count)),
            dma((count,)),
            dma((count,)),
            dma((3, count)),
            dma((3, 2, count)),
            dma(()),
            dma(()),
        ],
        compiler_params=pltpu.CompilerParams(
            collective_id=0, has_side_effects=True, vmem_limit_bytes=VMEM_BYTES
        ),
        name="run_experts",
    )(hidden, normed, tables, w_gate, w_up, w_down)


def expert_table(expert_ids, gate_weights, expert_count):
    chosen = expert_ids[:, :, None] == jnp.arange(expert_count, dtype=jnp.int32)
    return jnp.sum(jnp.where(chosen, gate_weights[:, :, None], 0.0), axis=1).T


def on_device(
    tokens, state_in, past_kv, w_qkv, w_out, w_gate, w_up, w_down, expert_ids, gate_weights
):
    row_count, model_width = tokens.shape
    inner_width = w_qkv.shape[2]
    local_heads = inner_width // HDIM
    ctx_count = lax.axis_size("ctx")
    head_count = lax.axis_size("heads")
    exp_local = w_gate.shape[0]
    devices = ctx_count * head_count
    expert_count = exp_local * devices
    top_count = expert_ids.shape[1]
    capacity = max(2, 2 * row_count * top_count // expert_count)
    dense = (
        ctx_count == 4
        and exp_local == 1
        and row_count % HDIM == 0
        and local_heads == 1
        and head_count * row_count == WINDOW
        and w_gate.shape[2] % HID_COLUMNS == 0
        and row_count * devices <= expert_count * capacity
    )
    if dense:
        table = expert_table(expert_ids, gate_weights, expert_count)
        hidden_state, normed, tables = attend(
            tokens, w_out, table, state_in[0], past_kv, jnp.transpose(w_qkv, (1, 0, 2))
        )
        return run_experts(hidden_state, normed, tables, w_gate[0], w_up[0], w_down[0])
    slab, w_rows = [
        lax.all_gather(value, "heads", axis=0, tiled=True) for value in (tokens, w_out)
    ]
    projected = jnp.dot(
        slab,
        w_qkv.reshape(model_width, 3 * inner_width),
        preferred_element_type=jnp.float32,
    ).astype(jnp.bfloat16)
    slab_rows = projected.shape[0]
    projected = projected.reshape(slab_rows, 3, local_heads, HDIM)
    query = jnp.transpose(projected[:, 0], (1, 0, 2))
    keys = jnp.transpose(projected[:, 1], (1, 0, 2))
    values = jnp.transpose(projected[:, 2], (1, 0, 2))
    local_state = jnp.einsum("hsd,hse->hde", keys, values, preferred_element_type=jnp.float32)
    earlier_state = entering(
        local_state, "ctx", lambda first, second: first + second, jnp.zeros_like(local_state)
    )
    start_state = state_in + earlier_state
    tail = jnp.stack([keys, values], axis=0)
    arrived = from_behind(tail, "ctx", 1)
    past = jnp.transpose(past_kv.reshape(2, WINDOW, local_heads, HDIM), (0, 2, 1, 3))
    previous = jnp.where(lax.axis_index("ctx") == 0, past, arrived)
    all_keys = jnp.concatenate([previous[0], keys], axis=1)
    all_values = jnp.concatenate([previous[1], values], axis=1)
    block_rows = min(slab_rows, 512)
    block_count = slab_rows // block_rows
    scale = 1.0 / math.sqrt(HDIM)
    causal = jnp.arange(block_rows)[:, None] >= jnp.arange(block_rows)[None, :]
    offsets = jnp.arange(WINDOW + block_rows)[None, :] - jnp.arange(block_rows)[:, None]
    in_window = (offsets > 0) & (offsets <= WINDOW)

    def block_step(state, index):
        first = index * block_rows
        carried = jnp.einsum(
            "hsd,hde->hse", query.astype(jnp.float32), state, precision=lax.Precision.HIGHEST
        )
        inside = jnp.einsum("hsd,htd->hst", query, keys, preferred_element_type=jnp.float32)
        inside = jnp.where(causal[None], inside, 0.0).astype(jnp.bfloat16)
        linear = carried + jnp.einsum(
            "hst,hte->hse", inside, values, preferred_element_type=jnp.float32
        )
        scores = (
            jnp.einsum("hsd,htd->hst", query, all_keys, preferred_element_type=jnp.float32) * scale
        )
        scores = jnp.where(in_window[None], scores, -jnp.inf)
        top_score = jnp.max(scores, axis=-1, keepdims=True)
        expo = jnp.exp(scores - top_score)
        probs = (expo / jnp.sum(expo, axis=-1, keepdims=True)).astype(jnp.bfloat16)
        window_out = jnp.einsum(
            "hst,hte->hse", probs, all_values, preferred_element_type=jnp.float32
        )
        combined = (normalize(linear) + window_out).astype(jnp.bfloat16)
        new_state = state + jnp.einsum(
            "hsd,hse->hde", keys, values, preferred_element_type=jnp.float32
        )
        return (new_state, combined)

    _, outs = lax.scan(block_step, start_state, jnp.arange(block_count, dtype=jnp.int32))
    heads_out = jnp.transpose(outs, (0, 2, 1, 3)).reshape(slab_rows, inner_width)
    regrouped = lax.all_to_all(heads_out, "heads", split_axis=0, concat_axis=1, tiled=True)
    attn = jnp.dot(
        regrouped,
        w_rows,
        preferred_element_type=jnp.float32,
    )
    hidden_state = (tokens.astype(jnp.float32) + attn).astype(jnp.bfloat16)
    hidden_float = hidden_state.astype(jnp.float32)
    normed = normalize(hidden_float).astype(jnp.bfloat16)
    picks = expert_ids.reshape(-1)
    onehot = (picks[:, None] == jnp.arange(expert_count, dtype=jnp.int32)[None, :]).astype(
        jnp.int32
    )
    earlier = jnp.cumsum(onehot, axis=0) - onehot
    slots = jnp.sum(onehot * earlier, axis=1)
    destination = picks * capacity + slots
    source_rows = jnp.arange(row_count * top_count, dtype=jnp.int32) // top_count
    outgoing = jnp.zeros((expert_count * capacity, model_width), jnp.bfloat16)
    outgoing = outgoing.at[destination].set(normed[source_rows])
    sendable = outgoing.reshape(expert_count, 1, capacity, model_width)
    arrived_rows = lax.all_to_all(
        sendable, ("ctx", "heads"), split_axis=0, concat_axis=1, tiled=True
    )
    e_count, n_count, c_count, d_count = arrived_rows.shape
    flat = arrived_rows.reshape(e_count, n_count * c_count, d_count)
    gate_act = jnp.einsum("erd,edf->erf", flat, w_gate, preferred_element_type=jnp.float32)
    up_act = jnp.einsum("erd,edf->erf", flat, w_up, preferred_element_type=jnp.float32)
    hid = (jax.nn.silu(gate_act) * up_act).astype(jnp.bfloat16)
    out_rows = jnp.einsum("erf,efd->erd", hid, w_down, preferred_element_type=jnp.float32)
    finished = out_rows.astype(jnp.bfloat16).reshape(e_count, n_count, c_count, d_count)
    returned = lax.all_to_all(finished, ("ctx", "heads"), split_axis=1, concat_axis=0, tiled=True)
    returned = returned.reshape(expert_count * capacity, model_width)
    picked = returned[destination].reshape(row_count, top_count, model_width).astype(jnp.float32)
    routed = jnp.sum(gate_weights[:, :, None] * picked, axis=1)
    return (hidden_float + routed).astype(jnp.bfloat16)


def solution(mesh):
    return jax.shard_map(
        on_device,
        mesh=mesh,
        in_specs=(
            P(("groups", "ctx", "heads"), None),
            P("heads", "groups", None),
            P(None, "groups", "heads"),
            P(None, None, "heads"),
            P("heads", None),
            P(("ctx", "heads"), None, None),
            P(("ctx", "heads"), None, None),
            P(("ctx", "heads"), None, None),
            P(("groups", "ctx", "heads"), None),
            P(("groups", "ctx", "heads"), None),
        ),
        out_specs=P(("groups", "ctx", "heads"), None),
        check_vma=False,
    )
```

```python
import functools
import math

import jax
import jax.numpy as jnp
from jax import lax
from jax.experimental import pallas as pl
from jax.experimental.pallas import tpu as pltpu
from jax.sharding import PartitionSpec as P

HDIM = 128
WINDOW = 512


def entering(x, axis, join, neutral):
    place = lax.axis_index(axis)
    gathered = lax.all_gather(x.astype(jnp.bfloat16), axis)
    state = jnp.zeros_like(x) + jnp.asarray(neutral, x.dtype)

    def one(lap, state):
        return join(state, lax.dynamic_index_in_dim(gathered, lap, 0, False).astype(x.dtype))

    return lax.fori_loop(0, place, one, state)


def from_behind(block, axis, distance):
    devices = range(lax.axis_size(axis))
    route = [(i - distance, i) for i in devices if i - distance in devices]
    return lax.ppermute(block, axis, route)


def normalize(value):
    return value * lax.rsqrt(jnp.mean(value * value, axis=-1, keepdims=True) + 1e-06)


MESH = pl.DeviceIdType.MESH
VMEM_BYTES = 60 * 1024 * 1024
FRONT_BYTES = 60 * 1024 * 1024
ADD_ROWS = 16
DOT_COLUMNS = 512
HID_COLUMNS = 256
LOAD_TIME = 0.6
UNIT_TIME = 0.75
SLACK = 0.05
NEAR_EIGHTHS = 5
SUM_EIGHTHS = 5
OWN_LINE, OWN_OVER, OWN_ASIDE, LOAD, NEAR, FAR, CROSS, SIDE = range(8)
COMPUTE, EXCHANGE, LINE, FINISH, BESIDE, PASS_FAR, PASS_NEAR, PAIR = range(8, 16)
STEPS = (
    (
        (OWN_LINE, 0), (OWN_OVER, 1), (LOAD,), (CROSS, 0), (NEAR, 1), (OWN_OVER, 0), (NEAR, 2), (CROSS, 1),
        (OWN_LINE, 1), (SIDE, 1), (COMPUTE, 1, 1), (NEAR, 3), (FAR, 1), (SIDE, 0), (COMPUTE, 1, 0), (SIDE, 3),
        (CROSS, 3), (EXCHANGE, 1), (LINE, 0, 1, 2), (LINE, 0, 1, 1), (FAR, 3), (COMPUTE, 3, 1), (COMPUTE, 3, 0),
        (EXCHANGE, 3), (CROSS, 2), (LINE, 0, 3, 2), (LINE, 0, 3, 1), (SIDE, 2), (FAR, 2), (COMPUTE, 2, 0),
        (OWN_ASIDE,), (LINE, 0, 3, 0), (COMPUTE, 2, 1), (EXCHANGE, 2), (LINE, 0, 2, 2), (COMPUTE, 0, 0),
        (LINE, 0, 2, 1), (COMPUTE, 0, 1), (LINE, 0, 2, 0), (EXCHANGE, 0), (FINISH, 2), (LINE, 0, 1, 0), (FINISH, 1),
        (FINISH, 0),
    ),
    (
        (OWN_OVER, 1), (OWN_OVER, 0), (OWN_LINE, 0), (NEAR, 0), (CROSS, 1), (NEAR, 2), (NEAR, 3), (CROSS, 0),
        (OWN_LINE, 1), (LOAD,), (SIDE, 2), (SIDE, 1), (SIDE, 0), (OWN_ASIDE,), (FAR, 0), (CROSS, 3),
        (FAR, 3), (FAR, 2), (COMPUTE, 0, 1), (CROSS, 2), (SIDE, 3), (COMPUTE, 0, 0), (COMPUTE, 3, 1),
        (COMPUTE, 3, 0), (EXCHANGE, 3), (COMPUTE, 2, 0), (LINE, 0, 3, 2), (EXCHANGE, 0), (COMPUTE, 2, 1),
        (LINE, 0, 3, 1), (COMPUTE, 1, 1), (EXCHANGE, 2), (LINE, 1, 0, 1), (LINE, 0, 3, 0), (COMPUTE, 1, 0),
        (LINE, 1, 0, 2), (LINE, 0, 2, 2), (LINE, 1, 0, 0), (LINE, 0, 2, 1), (EXCHANGE, 1), (FINISH, 2),
        (LINE, 0, 2, 0), (FINISH, 1), (FINISH, 0),
    ),
)


def place(count):
    z = lax.axis_index("heads")
    c = lax.axis_index("ctx")
    beside = c + 1 - 2 * lax.rem(c, 2)
    across = lax.rem(c + 2, 4)
    diagonal = lax.rem(beside + 2, 4)
    return z, c, beside, across, diagonal


def greet(z, count, beside, across):
    barrier = pltpu.get_barrier_semaphore()

    def signal(target):
        pl.semaphore_signal(barrier, inc=1, device_id=target, device_id_type=MESH)

    signal({"ctx": beside})
    signal({"ctx": across})

    @pl.when(z > 0)
    def _():
        signal({"heads": z - 1})

    @pl.when(z < count - 1)
    def _():
        signal({"heads": z + 1})

    pl.semaphore_wait(barrier, 2 + jnp.minimum(z, 1) + jnp.minimum(count - 1 - z, 1))


def nearest(count, z, index):
    index = count - 1 - index
    more = jnp.maximum(z, count - 1 - z)
    fewer = count - 1 - more
    alone = more - fewer
    paired = jnp.maximum(index - alone, 0)
    up = jnp.where(z + more < count, more - index, index - more)
    both = (fewer - paired // 2) * (1 - 2 * (paired % 2))
    offset = jnp.where(index < alone, up, both)
    return z + jnp.where(index < count - 1, offset, 0)


def attend_kernel(
    count, tokens_ref, share_hbm, table_ref, state_ref, past_hbm, qkv_hbm,
    hidden_ref, normed_ref, tables_ref,
    slab_ref, qkv_ref, w_ref, query_ref, kv_ref, before_ref, inside_ref, linear_ref,
    state_out, states_in, heads_out, heads_in,
    local_sem, token_send, token_recv, share_send, share_recv,
    tail_send, tail_recv, state_send, state_recv, head_send, head_recv,
):
    z, c, beside, across, diagonal = place(count)
    row_count, width = tokens_ref.shape
    slab_rows = count * row_count
    share = w_ref.shape[0] // (4 * count)

    def rows_of(index, size):
        return pl.ds(pl.multiple_of(index * size, size), size)

    def share_block(kind, zz, cc):
        if kind == 0:
            return w_ref.at[rows_of(zz * 4 + cc, share), :]
        return tables_ref.at[cc * count + zz]

    def share_source(kind):
        return table_ref if kind else share_hbm.at[rows_of(c, share), :]

    local = [
        pltpu.make_async_copy(source, target, local_sem.at[index])
        for index, (source, target) in enumerate(
            [(qkv_hbm.at[one], qkv_ref.at[:, one * HDIM : (one + 1) * HDIM]) for one in range(3)]
            + [(tokens_ref, slab_ref.at[z])]
            + [(share_source(kind), share_block(kind, z, c)) for kind in (0, 1)]
        )
    ]
    past_copy = pltpu.make_async_copy(past_hbm, before_ref, local_sem.at[6])
    for copy in local:
        copy.start()

    @pl.when(c == 0)
    def _():
        past_copy.start()

    barrier = pltpu.get_barrier_semaphore()
    for target in (beside, across, diagonal):
        pl.semaphore_signal(barrier, inc=1, device_id={"ctx": target}, device_id_type=MESH)
    for zz in range(count):

        @pl.when(zz != z)
        def _():
            pl.semaphore_signal(barrier, inc=1, device_id={"heads": zz}, device_id_type=MESH)

    pl.semaphore_wait(barrier, 3 + count - 1)

    def remote(source, target, send, recv, device):
        return pltpu.make_async_remote_copy(
            src_ref=source, dst_ref=target, send_sem=send, recv_sem=recv,
            device_id=device, device_id_type=MESH,
        )

    def started(copy):
        copy.start()

    def left(copy):
        copy.wait_send()

    def along(act, zz, copy):
        @pl.when(jnp.logical_and(zz >= z, z > 0))
        def _():
            act(copy(0, {"heads": z - 1}))

        @pl.when(jnp.logical_and(zz <= z, z < count - 1))
        def _():
            act(copy(1, {"heads": z + 1}))

    def token_copy(zz, own=False):
        def copy(way, device):
            source = tokens_ref if own else slab_ref.at[zz]
            return remote(source, slab_ref.at[zz], token_send.at[way, zz], token_recv.at[zz], device)

        return copy

    def share_copy(kind, zz, cc, own=False):
        def copy(way, device):
            block = share_block(kind, zz, cc)
            slot = zz * 4 + cc
            source = share_source(kind) if own else block
            return remote(
                source, block, share_send.at[kind, way, slot], share_recv.at[kind, slot], device
            )

        return copy

    def aside(act, zz, cc, own=False):
        for kind in (0, 1):
            act(share_copy(kind, zz, cc, own)(3, {"ctx": beside}))

    def share_relay(act, zz, own=False):
        for kind in (0, 1):
            act(share_copy(kind, zz, c, own)(2, {"ctx": across}))
        aside(act, zz, c, own)

    def share_along(act, zz, own=False):
        for kind in (0, 1):
            along(act, zz, share_copy(kind, zz, c, own))

    def share_received(zz, cc):
        for kind in (0, 1):
            share_copy(kind, zz, cc)(3, {"ctx": beside}).wait_recv()

    def at_distance(distance, act):
        @pl.when(z >= distance)
        def _():
            act(z - distance)

        @pl.when(z + distance < count)
        def _():
            act(z + distance)

    def share_onward(zz):
        share_received(zz, c)
        share_along(started, zz)
        share_relay(started, zz)

    def share_over(zz):
        share_received(zz, across)
        aside(started, zz, across)

    along(started, z, token_copy(z, True))
    share_relay(started, z, True)
    for copy in local:
        copy.wait()

    def project(zz):
        product = jnp.dot(slab_ref[zz], qkv_ref[...], preferred_element_type=jnp.float32)
        product = product.astype(query_ref.dtype)
        rows = rows_of(zz, row_count)
        query_ref[rows, :] = product[:, :HDIM]
        kv_ref[0, rows, :] = product[:, HDIM : 2 * HDIM]
        kv_ref[1, rows, :] = product[:, 2 * HDIM :]

    def token_relay(zz):
        token_copy(zz)(0, {"heads": z - 1}).wait_recv()
        along(started, zz, token_copy(zz))

    def step(index, _):
        zz = nearest(count, z, index)
        last = nearest(count, z, jnp.maximum(index - 1, 0))
        after = nearest(count, z, jnp.minimum(index + 1, count - 1))
        opens = jnp.logical_and(index > 0, jnp.abs(zz - z) != jnp.abs(last - z))
        double = jnp.logical_and(index < count - 1, jnp.abs(after - z) == jnp.abs(zz - z))

        @pl.when(opens)
        def _():
            token_relay(zz)

        @pl.when(jnp.logical_and(opens, double))
        def _():
            token_relay(after)

        project(zz)
        alone = jnp.logical_and(index > 0, jnp.logical_not(jnp.logical_and(opens, double)))
        distance = jnp.abs(zz - z)

        @pl.when(jnp.logical_and(alone, distance == 1))
        def _():
            share_along(started, z, True)

        @pl.when(jnp.logical_and(alone, distance > 1))
        def _():
            at_distance(distance - 1, share_onward)

        return 0

    lax.fori_loop(0, count, step, 0)

    tail = remote(kv_ref, before_ref, tail_send, tail_recv, {"ctx": jnp.minimum(c + 1, 3)})

    @pl.when(c < 3)
    def _():
        tail.start()

    local_state = lax.dot_general(
        kv_ref[0], kv_ref[1], (((0,), (0,)), ((), ())), preferred_element_type=jnp.float32
    )
    state_out[...] = local_state.astype(state_out.dtype)
    others = [beside, across, diagonal]
    state_copies = [
        remote(state_out, states_in.at[c], state_send.at[way], state_recv.at[c], {"ctx": target})
        for way, target in enumerate(others)
    ]
    for copy in state_copies:
        copy.start()
    share_over(z)

    blocks = slab_rows // row_count
    for block in range(blocks):
        first, end = block * row_count, (block + 1) * row_count
        query = query_ref[first:end, :]
        scores = lax.dot_general(
            query, kv_ref[0, :end, :], (((1,), (1,)), ((), ())), preferred_element_type=jnp.float32
        )
        shape = scores.shape
        causal = lax.broadcasted_iota(jnp.int32, shape, 1) <= first + lax.broadcasted_iota(
            jnp.int32, shape, 0
        )
        inside_ref[first:end, :end] = scores
        weights = jnp.where(causal, scores, 0.0).astype(kv_ref.dtype)
        linear_ref[first:end, :] = jnp.dot(
            weights, kv_ref[1, :end, :], preferred_element_type=jnp.float32
        )

    for target in others:
        remote(
            state_out, states_in.at[target], state_send.at[0], state_recv.at[target],
            {"ctx": beside},
        ).wait_recv()
    start = state_ref[...]
    for cc in range(4):
        start = start + jnp.where(cc < c, states_in[cc].astype(jnp.float32), 0.0)

    @pl.when(c == 0)
    def _():
        past_copy.wait()

    @pl.when(c > 0)
    def _():
        tail.wait_recv()

    scale = 1.0 / math.sqrt(HDIM)

    def head_copy(zz):
        columns = pl.ds(pl.multiple_of(z * HDIM, HDIM), HDIM)
        return remote(
            heads_out.at[zz], heads_in.at[:, columns], head_send.at[zz], head_recv.at[z],
            {"heads": zz},
        )

    for block in range(blocks):
        first, end = block * row_count, (block + 1) * row_count
        query = query_ref[first:end, :]
        old = lax.dot_general(
            query, before_ref[0, first:, :], (((1,), (1,)), ((), ())),
            preferred_element_type=jnp.float32,
        )
        old_seen = lax.broadcasted_iota(jnp.int32, old.shape, 1) > lax.broadcasted_iota(
            jnp.int32, old.shape, 0
        )
        old = jnp.where(old_seen, old * scale, -jnp.inf)
        new = inside_ref[first:end, :end]
        new_seen = lax.broadcasted_iota(jnp.int32, new.shape, 1) <= first + lax.broadcasted_iota(
            jnp.int32, new.shape, 0
        )
        new = jnp.where(new_seen, new * scale, -jnp.inf)
        top = jnp.maximum(
            jnp.max(old, axis=-1, keepdims=True), jnp.max(new, axis=-1, keepdims=True)
        )
        old = jnp.exp(old - top)
        new = jnp.exp(new - top)
        inverse = 1.0 / (
            jnp.sum(old, axis=-1, keepdims=True) + jnp.sum(new, axis=-1, keepdims=True)
        )
        window = jnp.dot(
            (old * inverse).astype(kv_ref.dtype), before_ref[1, first:, :],
            preferred_element_type=jnp.float32,
        ) + jnp.dot(
            (new * inverse).astype(kv_ref.dtype), kv_ref[1, :end, :],
            preferred_element_type=jnp.float32,
        )
        linear = linear_ref[first:end, :] + jnp.dot(
            query.astype(jnp.float32), start, precision=lax.Precision.HIGHEST,
            preferred_element_type=jnp.float32,
        )
        heads_out[block] = (normalize(linear) + window).astype(heads_out.dtype)

        @pl.when(block != z)
        def _():
            head_copy(block).start()

        @pl.when(block == z)
        def _():
            columns = pl.ds(pl.multiple_of(z * HDIM, HDIM), HDIM)
            heads_in[:, columns] = heads_out[block]

        if block == 0:
            at_distance(jnp.maximum(z, count - 1 - z), share_onward)
        if block + 1 < count:
            at_distance(block + 1, share_over)

    for zz in range(count):
        share_received(zz, beside)
        share_received(zz, diagonal)

        @pl.when(zz != z)
        def _():
            remote(
                heads_out.at[zz], heads_in.at[:, zz * HDIM : (zz + 1) * HDIM], head_send.at[zz],
                head_recv.at[zz], {"heads": zz},
            ).wait_recv()

    def out_tile(index, total):
        columns = pl.ds(pl.multiple_of(index * DOT_COLUMNS, DOT_COLUMNS), DOT_COLUMNS)
        attn = jnp.dot(heads_in[...], w_ref[:, columns], preferred_element_type=jnp.float32)
        hidden = (tokens_ref[:, columns].astype(jnp.float32) + attn).astype(hidden_ref.dtype)
        hidden_ref[:, columns] = hidden
        hidden = hidden.astype(jnp.float32)
        return total + jnp.sum(hidden * hidden, axis=-1, keepdims=True)

    total = lax.fori_loop(
        0, width // DOT_COLUMNS, out_tile, jnp.zeros((row_count, 1), jnp.float32)
    )
    inverse = lax.rsqrt(total / width + 1e-06)
    for first in range(0, width, DOT_COLUMNS):
        hidden = hidden_ref[:, first : first + DOT_COLUMNS].astype(jnp.float32)
        normed_ref[:, first : first + DOT_COLUMNS] = (hidden * inverse).astype(normed_ref.dtype)

    along(left, z, token_copy(z, True))
    share_along(left, z, True)
    share_relay(left, z, True)

    @pl.when(c < 3)
    def _():
        tail.wait_send()

    for copy in state_copies:
        copy.wait_send()
    for zz in range(count):
        aside(left, zz, across)

        @pl.when(zz != z)
        def _():
            along(left, zz, token_copy(zz))
            share_along(left, zz)
            share_relay(left, zz)
            head_copy(zz).wait_send()


def plan_steps(count, at, share):
    near, far = 2 * share, 2 * (1 - share)
    stage = near + 2 * far

    def begin(place, zz):
        return (abs(zz - place) - 1) * stage

    def arrivals(place):
        events = [(2.0, (CROSS, place)), (2.0, (SIDE, place))]
        ready = {(place, 0): LOAD_TIME, (place, 1): 2.1}
        link = 2.0
        for zz in sorted(set(range(count)) - {place}, key=lambda other: abs(other - place)):
            first = begin(place, zz)
            events.append((first + near, (NEAR, zz)))
            events.append((first + near + far, (FAR, zz)))
            events.append((first + stage, (CROSS, zz)))
            link = max(link, first + near) + near
            events.append((link, (SIDE, zz)))
            ready[zz, 0] = first + near + far + 0.1
            ready[zz, 1] = max(first + stage, link) + 0.1
        return sorted(events, key=lambda event: event[0]), ready

    def simulate(place):
        events, ready = arrivals(place)
        segments, order, now, ends, current = [], [], 0.0, {}, []
        while ready or events:
            while events and events[0][0] <= now + SLACK:
                when, op = events.pop(0)
                current.append(op)
                zz = op[-1]
                if op[0] == EXCHANGE and zz != place and place in (0, count - 1):
                    events.append((now, (PASS_FAR, int(zz < place), zz)))
                    events.append((now + near + 0.3, (PASS_NEAR, int(zz < place), zz)))
                    events.sort(key=lambda event: event[0])
            able = [unit for unit in ready if ready[unit] <= now + SLACK]
            if not able and not ready and not events:
                break
            if not able:
                now = min([event[0] for event in events[:1]] + list(ready.values()))
                continue
            unit = min(able, key=lambda one: ready[one])
            del ready[unit]
            segments.append(current + [(PAIR,) + unit])
            order.append(unit)
            now += UNIT_TIME
            zz, pair = unit
            ends[zz] = ends.get(zz, 0) + 1
            current = [(BESIDE, zz, 1 - pair)]
            if ends[zz] == 2:
                events.append((now + 0.5, (EXCHANGE, zz)))
                events.sort(key=lambda event: event[0])
                ends[zz] = now + 1.0
        segments.append(current)
        return segments, order, ends

    everyone = [simulate(place) for place in range(count)]
    segments, order, _ = everyone[at]
    if 0 < at < count - 1:

        def chain(side, zz, place, op):
            own = everyone[place][2][zz] + (near if op == PASS_NEAR else 0)
            if place == side * (count - 1):
                return own
            hop = near if op == PASS_NEAR else 2 * far
            return max(own, chain(side, zz, place + 2 * side - 1, op) + hop + 0.2)

        passes = [
            (op, int(zz < at), zz)
            for zz in range(count)
            for op in (PASS_FAR, PASS_NEAR)
            if zz != at
        ]
        passes.sort(key=lambda one: chain(one[1], one[2], at, one[0]))
        segments = segments[:-1] + [segments[-1] + passes]
    steps = [(OWN_LINE, 0), (OWN_OVER, 0), (OWN_ASIDE,), (OWN_LINE, 1), (OWN_OVER, 1), (LOAD,)]
    for index, ops in enumerate(segments):
        for op, *where in ops:
            if op == EXCHANGE:
                steps.append((EXCHANGE, *where))
            elif op == PASS_FAR:
                steps += [(LINE, *where, 1), (LINE, *where, 2)]
            elif op == PASS_NEAR:
                steps.append((LINE, *where, 0))
            elif op not in (PAIR, BESIDE):
                steps.append((op, *where))
        if index < len(order):
            steps.append((COMPUTE,) + order[index])
    return steps + [(FINISH, 2), (FINISH, 0), (FINISH, 1)]


def mirrored(step, count):
    op, *where = step
    if op in (NEAR, FAR, CROSS, SIDE, EXCHANGE, COMPUTE):
        return (op, count - 1 - where[0], *where[1:])
    if op == LINE:
        return (op, 1 - where[0], count - 1 - where[1], where[2])
    return step


def steps_of(count, at, share):
    if count != len(STEPS) * 2:
        return plan_steps(count, at, share)
    if at < len(STEPS):
        return list(STEPS[at])
    return [mirrored(step, count) for step in STEPS[count - 1 - at]]


def expert_kernel(
    count, near_rows, sum_rows, hidden_ref, own_ref, table_ref, gate_hbm, up_hbm, down_hbm, out_ref,
    rows_ref, part_ref, hid_ref, scale_ref, gate_ref, up_ref, down_ref,
    from_beside, to_across, from_across, line_out, line_in, last_out, last_in,
    local_sem, row_send, row_recv, beside_send, beside_recv, across_send, across_recv,
    line_send, line_recv, last_send, last_recv,
):
    z, c, beside, across, diagonal = place(count)
    row_count, width = own_ref.shape
    far_rows = row_count - near_rows
    spans = [(0, near_rows), (near_rows, far_rows)]
    sum_spans = [(0, sum_rows), (sum_rows, row_count - sum_rows)]
    expert = c * count + z
    local = [
        pltpu.make_async_copy(source, target, local_sem.at[index])
        for index, (source, target) in enumerate(
            [
                (gate_hbm, gate_ref),
                (up_hbm, up_ref),
                (down_hbm, down_ref),
                (own_ref, rows_ref.at[z, pl.ds(pl.multiple_of(c * row_count, row_count), row_count), :]),
            ]
        )
    ]
    for copy in local:
        copy.start()
    greet(z, count, beside, across)

    def window(cc, span):
        first, size = spans[span]
        return pl.ds(pl.multiple_of(cc * row_count + first, 16), size)

    def row_copy(zz, cc, span, way, target, own=False):
        first, size = spans[span]
        slot = zz * 4 + cc
        block = rows_ref.at[zz, window(cc, span), :]
        return pltpu.make_async_remote_copy(
            src_ref=own_ref.at[pl.ds(first, size), :] if own else block,
            dst_ref=block,
            send_sem=row_send.at[way, span, slot],
            recv_sem=row_recv.at[span, slot],
            device_id=target,
            device_id_type=MESH,
        )

    def started(copy):
        copy.start()

    def left(copy):
        copy.wait_send()

    def received(zz, cc, span):
        row_copy(zz, cc, span, 0, {"ctx": beside}).wait_recv()

    def along(act, at, zz, cc, span, own=False):
        if zz >= at and at > 0:
            act(row_copy(zz, cc, span, 0, {"heads": at - 1}, own))
        if zz <= at and at < count - 1:
            act(row_copy(zz, cc, span, 1, {"heads": at + 1}, own))

    def over(act, zz, cc, span, own=False):
        act(row_copy(zz, cc, span, 2, {"ctx": across}, own))

    def aside(act, zz, cc, span, own=False):
        act(row_copy(zz, cc, span, 3, {"ctx": beside}, own))

    def relays(op, at, zz, act, wait):
        cc = c if op in (NEAR, FAR) else across
        span = 0 if op in (NEAR, SIDE) else 1
        if wait:
            received(zz, cc, span)
        if op != SIDE:
            along(act, at, zz, cc, span)
        if op == NEAR:
            over(act, zz, cc, span)
        aside(act, zz, cc, span)

    def paired(zz, pair):
        for span in (0, 1):
            received(zz, diagonal if pair else beside, span)

    def compute(zz, pair):
        half = jnp.where(pair == 0, c // 2, 1 - c // 2)
        for core in range(2):
            row = table_ref[(half * 2 + core) * count + zz, pl.ds(expert, 1), :]
            scale_ref[core * row_count : (core + 1) * row_count, :] = jnp.broadcast_to(
                row, (HDIM, row_count)
            ).T

        inner = gate_ref.shape[1]
        rows = pl.ds(pl.multiple_of(half * 2 * row_count, 2 * row_count), 2 * row_count)

        def hidden_tile(index, _):
            columns = pl.ds(pl.multiple_of(index * HID_COLUMNS, HID_COLUMNS), HID_COLUMNS)
            block = rows_ref[zz, rows, :]
            gate = jnp.dot(block, gate_ref[:, columns], preferred_element_type=jnp.float32)
            up = jnp.dot(block, up_ref[:, columns], preferred_element_type=jnp.float32)
            scale = jnp.concatenate([scale_ref[...]] * (HID_COLUMNS // HDIM), axis=1)
            hid_ref[:, columns] = (jax.nn.silu(gate) * up * scale).astype(hid_ref.dtype)
            return 0

        lax.fori_loop(0, inner // HID_COLUMNS, hidden_tile, 0)

        def out_tile(index, _):
            columns = pl.ds(pl.multiple_of(index * DOT_COLUMNS, DOT_COLUMNS), DOT_COLUMNS)
            product = jnp.dot(
                hid_ref[...], down_ref[:, columns], preferred_element_type=jnp.float32
            )
            part_ref[zz, rows, columns] = product.astype(part_ref.dtype)
            return 0

        lax.fori_loop(0, width // DOT_COLUMNS, out_tile, 0)

    def beside_copy(kind, zz):
        cc = diagonal if kind == 0 else beside
        return pltpu.make_async_remote_copy(
            src_ref=part_ref.at[zz, pl.ds(pl.multiple_of(cc * row_count, row_count), row_count), :],
            dst_ref=from_beside.at[kind, zz],
            send_sem=beside_send.at[kind, zz],
            recv_sem=beside_recv.at[kind, zz],
            device_id={"ctx": beside},
            device_id_type=MESH,
        )

    def across_copy(zz):
        return pltpu.make_async_remote_copy(
            src_ref=to_across.at[zz],
            dst_ref=from_across.at[zz],
            send_sem=across_send.at[zz],
            recv_sem=across_recv.at[zz],
            device_id={"ctx": across},
            device_id_type=MESH,
        )

    line_spans = sum_spans + [(row_count, row_count - sum_rows)]

    def line_copy(side, zz, chunk):
        first, size = line_spans[chunk]
        return pltpu.make_async_remote_copy(
            src_ref=line_out.at[zz, pl.ds(first, size), :],
            dst_ref=line_in.at[side, zz, pl.ds(first, size), :],
            send_sem=line_send.at[chunk, zz],
            recv_sem=line_recv.at[chunk, side, zz],
            device_id={"heads": z + 1 - 2 * side},
            device_id_type=MESH,
        )

    def last_copy():
        return pltpu.make_async_remote_copy(
            src_ref=last_out,
            dst_ref=last_in,
            send_sem=last_send,
            recv_sem=last_recv,
            device_id={"ctx": across},
            device_id_type=MESH,
        )

    def add(target, sources):
        def chunk(index, _):
            rows = pl.ds(pl.multiple_of(index * ADD_ROWS, ADD_ROWS), ADD_ROWS)
            total = sources[0][rows, :].astype(jnp.float32)
            for source in sources[1:]:
                total = total + source[rows, :].astype(jnp.float32)
            target[rows, :] = total.astype(target.dtype)
            return 0

        lax.fori_loop(0, target.shape[0] // ADD_ROWS, chunk, 0)

    def chip_sources(zz, chunk):
        cc, kind = (across, 0) if chunk == 2 else (c, 1)
        first, size = sum_spans[0 if chunk == 0 else 1]
        start = pl.multiple_of(cc * row_count + first, 16)
        sources = [
            part_ref.at[zz, pl.ds(start, size), :],
            from_beside.at[kind, zz, pl.ds(first, size), :],
        ]
        return sources + ([from_across.at[zz]] if chunk == 0 else [])

    def line_block(side, zz, chunk):
        first, size = line_spans[chunk]
        return line_in.at[side, zz, pl.ds(first, size), :]

    def starts(side, at):
        return at == side * (count - 1)

    def perform(at, steps, waited):
        waited = set(waited)

        def once(make, *key):
            if key not in waited:
                waited.add(key)
                make().wait_recv()

        def ready(zz, chunk):
            kind = 0 if chunk == 2 else 1
            once(lambda: beside_copy(kind, zz), kind, zz)
            if chunk == 0:
                once(lambda: across_copy(zz), 2, zz)
            return chip_sources(zz, chunk)

        def arrived(zz, chunk, sides):
            sources = ready(zz, chunk)
            for side in sides:
                if not starts(side, at):
                    line_copy(side, zz, chunk).wait_recv()
                    sources = sources + [line_block(side, zz, chunk)]
            return sources

        for op, *where in steps:
            if op == OWN_LINE:
                along(started, at, at, c, where[0], True)
            elif op == OWN_OVER:
                over(started, at, c, where[0], True)
            elif op == OWN_ASIDE:
                for span in (0, 1):
                    aside(started, at, c, span, True)
            elif op == LOAD:
                for copy in local:
                    copy.wait()
            elif op == COMPUTE:
                paired(*where)
            elif op == BESIDE:
                beside_copy(where[1], where[0]).start()
            elif op == EXCHANGE:
                zz = where[0]
                once(lambda: beside_copy(0, zz), 0, zz)
                start = pl.multiple_of(across * row_count, row_count)
                add(
                    to_across.at[zz],
                    [
                        part_ref.at[zz, pl.ds(start, sum_rows), :],
                        from_beside.at[0, zz, pl.ds(0, sum_rows), :],
                    ],
                )
                across_copy(zz).start()
            elif op == LINE:
                side, zz, chunk = where
                first, size = line_spans[chunk]
                add(line_out.at[zz, pl.ds(first, size), :], arrived(zz, chunk, (side,)))
                line_copy(side, zz, chunk).start()
            elif op == FINISH and where[0] == 2:
                add(last_out, arrived(at, 2, (0, 1)))
                last_copy().start()
            elif op == FINISH:
                first, size = sum_spans[where[0]]
                rows = pl.ds(first, size)
                sources = arrived(at, where[0], (0, 1))
                if where[0] == 1:
                    last_copy().wait_recv()
                    sources = sources + [last_in]
                add(out_ref.at[rows, :], [hidden_ref.at[rows, :]] + sources)
            else:
                relays(op, at, where[0], started, True)

    def each_place(act):
        for at in range(count):

            @pl.when(z == at)
            def _():
                act(at)

    units = 2 * count
    segments, orders = [], []
    for at in range(count):
        parts, order = [[]], []
        for one in steps_of(count, at, near_rows / row_count):
            parts[-1].append(one)
            if one[0] == COMPUTE:
                zz, pair = one[1:]
                order.append((zz, pair))
                parts.append([(BESIDE, zz, 1 - pair)])
        segments.append(parts)
        orders.append(order)

    def waits_of(at, unit):
        keys = set()
        for one in sum(segments[at][:unit], []):
            zz, chunk = at, one[-1]
            if one[0] == EXCHANGE:
                zz, chunk = one[1], 2
            elif one[0] == LINE:
                zz = one[2]
            elif one[0] != FINISH:
                continue
            keys.add((0 if chunk == 2 else 1, zz))
            if chunk == 0:
                keys.add((2, zz))
        return keys

    def choose(index, pick):
        value = jnp.int32(0)
        for at in range(count):
            for unit in range(units):
                here = jnp.logical_and(z == at, index == unit)
                value = jnp.where(here, pick(orders[at][unit]), value)
        return value

    def step(index, _):
        def segment(at):
            for unit in range(units):

                @pl.when(index == unit)
                def _():
                    perform(at, segments[at][unit], waits_of(at, unit))

        each_place(segment)
        compute(choose(index, lambda unit: unit[0]), choose(index, lambda unit: unit[1]))
        return 0

    lax.fori_loop(0, units, step, 0)

    def finish(at):
        perform(at, segments[at][units], waits_of(at, units))
        last_copy().wait_send()
        for span in (0, 1):
            along(left, at, at, c, span, True)
            over(left, at, c, span, True)
            aside(left, at, c, span, True)
        relays(SIDE, at, at, left, False)
        relays(CROSS, at, at, left, False)
        for zz in range(count):
            beside_copy(0, zz).wait_send()
            beside_copy(1, zz).wait_send()
            across_copy(zz).wait_send()
            if zz != at:
                for op in (NEAR, FAR, CROSS, SIDE):
                    relays(op, at, zz, left, False)
                for chunk in range(3):
                    line_copy(int(zz < at), zz, chunk).wait_send()

    each_place(finish)


def attend(tokens, w_out, table, state_in, past_kv, w_qkv):
    count = lax.axis_size("heads")
    row_count, width = tokens.shape
    slab_rows = count * row_count
    kind = tokens.dtype
    slots = 4 * count
    dma = pltpu.SemaphoreType.DMA
    vmem, anywhere = pl.BlockSpec(memory_space=pltpu.VMEM), pl.BlockSpec(memory_space=pl.ANY)
    return pl.pallas_call(
        functools.partial(attend_kernel, count),
        out_shape=[
            jax.ShapeDtypeStruct((row_count, width), kind),
            jax.ShapeDtypeStruct((row_count, width), kind),
            jax.ShapeDtypeStruct((slots,) + table.shape, table.dtype),
        ],
        in_specs=[vmem, anywhere, vmem, vmem, anywhere, anywhere],
        out_specs=[vmem, vmem, anywhere],
        scratch_shapes=[
            pltpu.VMEM((count, row_count, width), kind),
            pltpu.VMEM((width, 3 * HDIM), kind),
            pltpu.VMEM((count * HDIM, width), kind),
            pltpu.VMEM((slab_rows, HDIM), kind),
            pltpu.VMEM((2, slab_rows, HDIM), kind),
            pltpu.VMEM((2, WINDOW, HDIM), kind),
            pltpu.VMEM((slab_rows, slab_rows), jnp.float32),
            pltpu.VMEM((slab_rows, HDIM), jnp.float32),
            pltpu.VMEM((HDIM, HDIM), kind),
            pltpu.VMEM((4, HDIM, HDIM), kind),
            pltpu.VMEM((count, row_count, HDIM), kind),
            pltpu.VMEM((row_count, count * HDIM), kind),
            dma((7,)),
            dma((2, count)),
            dma((count,)),
            dma((2, 4, slots)),
            dma((2, slots)),
            dma(()),
            dma(()),
            dma((3,)),
            dma((4,)),
            dma((count,)),
            dma((count,)),
        ],
        compiler_params=pltpu.CompilerParams(
            collective_id=2, has_side_effects=True, vmem_limit_bytes=FRONT_BYTES
        ),
        name="attend",
    )(tokens, w_out, table, state_in, past_kv, w_qkv)


def near_share(row_count, eighths):
    return max(16, row_count * eighths // 8 // 16 * 16)


def run_experts(hidden, normed, tables, w_gate, w_up, w_down):
    count = lax.axis_size("heads")
    row_count, width = normed.shape
    inner = w_gate.shape[1]
    near_rows = near_share(row_count, NEAR_EIGHTHS)
    sum_rows = near_share(row_count, SUM_EIGHTHS)
    far_rows = row_count - sum_rows
    dma = pltpu.SemaphoreType.DMA
    kind = normed.dtype
    vmem, anywhere = pl.BlockSpec(memory_space=pltpu.VMEM), pl.BlockSpec(memory_space=pl.ANY)
    return pl.pallas_call(
        functools.partial(expert_kernel, count, near_rows, sum_rows),
        out_shape=jax.ShapeDtypeStruct((row_count, width), kind),
        in_specs=[vmem] * 3 + [anywhere] * 3,
        out_specs=vmem,
        scratch_shapes=[
            pltpu.VMEM((count, 4 * row_count, width), kind),
            pltpu.VMEM((count, 4 * row_count, width), kind),
            pltpu.VMEM((2 * row_count, inner), kind),
            pltpu.VMEM((2 * row_count, HDIM), jnp.float32),
            pltpu.VMEM(w_gate.shape, kind),
            pltpu.VMEM(w_up.shape, kind),
            pltpu.VMEM(w_down.shape, kind),
            pltpu.VMEM((2, count, row_count, width), kind),
            pltpu.VMEM((count, sum_rows, width), kind),
            pltpu.VMEM((count, sum_rows, width), kind),
            pltpu.VMEM((count, row_count + far_rows, width), kind),
            pltpu.VMEM((2, count, row_count + far_rows, width), kind),
            pltpu.VMEM((far_rows, width), kind),
            pltpu.VMEM((far_rows, width), kind),
            dma((4,)),
            dma((4, 2, 4 * count)),
            dma((2, 4 * count)),
            dma((2, count)),
            dma((2, count)),
            dma((count,)),
            dma((count,)),
            dma((3, count)),
            dma((3, 2, count)),
            dma(()),
            dma(()),
        ],
        compiler_params=pltpu.CompilerParams(
            collective_id=0, has_side_effects=True, vmem_limit_bytes=VMEM_BYTES
        ),
        name="run_experts",
    )(hidden, normed, tables, w_gate, w_up, w_down)


def expert_table(expert_ids, gate_weights, expert_count):
    chosen = expert_ids[:, :, None] == jnp.arange(expert_count, dtype=jnp.int32)
    return jnp.sum(jnp.where(chosen, gate_weights[:, :, None], 0.0), axis=1).T


def on_device(
    tokens, state_in, past_kv, w_qkv, w_out, w_gate, w_up, w_down, expert_ids, gate_weights
):
    row_count, model_width = tokens.shape
    inner_width = w_qkv.shape[2]
    local_heads = inner_width // HDIM
    ctx_count = lax.axis_size("ctx")
    head_count = lax.axis_size("heads")
    exp_local = w_gate.shape[0]
    devices = ctx_count * head_count
    expert_count = exp_local * devices
    top_count = expert_ids.shape[1]
    capacity = max(2, 2 * row_count * top_count // expert_count)
    dense = (
        ctx_count == 4
        and exp_local == 1
        and row_count % HDIM == 0
        and local_heads == 1
        and head_count * row_count == WINDOW
        and w_gate.shape[2] % HID_COLUMNS == 0
        and row_count * devices <= expert_count * capacity
    )
    if dense:
        table = expert_table(expert_ids, gate_weights, expert_count)
        hidden_state, normed, tables = attend(
            tokens, w_out, table, state_in[0], past_kv, jnp.transpose(w_qkv, (1, 0, 2))
        )
        return run_experts(hidden_state, normed, tables, w_gate[0], w_up[0], w_down[0])
    slab, w_rows = [
        lax.all_gather(value, "heads", axis=0, tiled=True) for value in (tokens, w_out)
    ]
    projected = jnp.dot(
        slab,
        w_qkv.reshape(model_width, 3 * inner_width),
        preferred_element_type=jnp.float32,
    ).astype(jnp.bfloat16)
    slab_rows = projected.shape[0]
    projected = projected.reshape(slab_rows, 3, local_heads, HDIM)
    query = jnp.transpose(projected[:, 0], (1, 0, 2))
    keys = jnp.transpose(projected[:, 1], (1, 0, 2))
    values = jnp.transpose(projected[:, 2], (1, 0, 2))
    local_state = jnp.einsum("hsd,hse->hde", keys, values, preferred_element_type=jnp.float32)
    earlier_state = entering(
        local_state, "ctx", lambda first, second: first + second, jnp.zeros_like(local_state)
    )
    start_state = state_in + earlier_state
    tail = jnp.stack([keys, values], axis=0)
    arrived = from_behind(tail, "ctx", 1)
    past = jnp.transpose(past_kv.reshape(2, WINDOW, local_heads, HDIM), (0, 2, 1, 3))
    previous = jnp.where(lax.axis_index("ctx") == 0, past, arrived)
    all_keys = jnp.concatenate([previous[0], keys], axis=1)
    all_values = jnp.concatenate([previous[1], values], axis=1)
    block_rows = min(slab_rows, 512)
    block_count = slab_rows // block_rows
    scale = 1.0 / math.sqrt(HDIM)
    causal = jnp.arange(block_rows)[:, None] >= jnp.arange(block_rows)[None, :]
    offsets = jnp.arange(WINDOW + block_rows)[None, :] - jnp.arange(block_rows)[:, None]
    in_window = (offsets > 0) & (offsets <= WINDOW)

    def block_step(state, index):
        first = index * block_rows
        carried = jnp.einsum(
            "hsd,hde->hse", query.astype(jnp.float32), state, precision=lax.Precision.HIGHEST
        )
        inside = jnp.einsum("hsd,htd->hst", query, keys, preferred_element_type=jnp.float32)
        inside = jnp.where(causal[None], inside, 0.0).astype(jnp.bfloat16)
        linear = carried + jnp.einsum(
            "hst,hte->hse", inside, values, preferred_element_type=jnp.float32
        )
        scores = (
            jnp.einsum("hsd,htd->hst", query, all_keys, preferred_element_type=jnp.float32) * scale
        )
        scores = jnp.where(in_window[None], scores, -jnp.inf)
        top_score = jnp.max(scores, axis=-1, keepdims=True)
        expo = jnp.exp(scores - top_score)
        probs = (expo / jnp.sum(expo, axis=-1, keepdims=True)).astype(jnp.bfloat16)
        window_out = jnp.einsum(
            "hst,hte->hse", probs, all_values, preferred_element_type=jnp.float32
        )
        combined = (normalize(linear) + window_out).astype(jnp.bfloat16)
        new_state = state + jnp.einsum(
            "hsd,hse->hde", keys, values, preferred_element_type=jnp.float32
        )
        return (new_state, combined)

    _, outs = lax.scan(block_step, start_state, jnp.arange(block_count, dtype=jnp.int32))
    heads_out = jnp.transpose(outs, (0, 2, 1, 3)).reshape(slab_rows, inner_width)
    regrouped = lax.all_to_all(heads_out, "heads", split_axis=0, concat_axis=1, tiled=True)
    attn = jnp.dot(
        regrouped,
        w_rows,
        preferred_element_type=jnp.float32,
    )
    hidden_state = (tokens.astype(jnp.float32) + attn).astype(jnp.bfloat16)
    hidden_float = hidden_state.astype(jnp.float32)
    normed = normalize(hidden_float).astype(jnp.bfloat16)
    picks = expert_ids.reshape(-1)
    onehot = (picks[:, None] == jnp.arange(expert_count, dtype=jnp.int32)[None, :]).astype(
        jnp.int32
    )
    earlier = jnp.cumsum(onehot, axis=0) - onehot
    slots = jnp.sum(onehot * earlier, axis=1)
    destination = picks * capacity + slots
    source_rows = jnp.arange(row_count * top_count, dtype=jnp.int32) // top_count
    outgoing = jnp.zeros((expert_count * capacity, model_width), jnp.bfloat16)
    outgoing = outgoing.at[destination].set(normed[source_rows])
    sendable = outgoing.reshape(expert_count, 1, capacity, model_width)
    arrived_rows = lax.all_to_all(
        sendable, ("ctx", "heads"), split_axis=0, concat_axis=1, tiled=True
    )
    e_count, n_count, c_count, d_count = arrived_rows.shape
    flat = arrived_rows.reshape(e_count, n_count * c_count, d_count)
    gate_act = jnp.einsum("erd,edf->erf", flat, w_gate, preferred_element_type=jnp.float32)
    up_act = jnp.einsum("erd,edf->erf", flat, w_up, preferred_element_type=jnp.float32)
    hid = (jax.nn.silu(gate_act) * up_act).astype(jnp.bfloat16)
    out_rows = jnp.einsum("erf,efd->erd", hid, w_down, preferred_element_type=jnp.float32)
    finished = out_rows.astype(jnp.bfloat16).reshape(e_count, n_count, c_count, d_count)
    returned = lax.all_to_all(finished, ("ctx", "heads"), split_axis=1, concat_axis=0, tiled=True)
    returned = returned.reshape(expert_count * capacity, model_width)
    picked = returned[destination].reshape(row_count, top_count, model_width).astype(jnp.float32)
    routed = jnp.sum(gate_weights[:, :, None] * picked, axis=1)
    return (hidden_float + routed).astype(jnp.bfloat16)


def solution(mesh):
    return jax.shard_map(
        on_device,
        mesh=mesh,
        in_specs=(
            P(("groups", "ctx", "heads"), None),
            P("heads", "groups", None),
            P(None, "groups", "heads"),
            P(None, None, "heads"),
            P("heads", None),
            P(("ctx", "heads"), None, None),
            P(("ctx", "heads"), None, None),
            P(("ctx", "heads"), None, None),
            P(("groups", "ctx", "heads"), None),
            P(("groups", "ctx", "heads"), None),
        ),
        out_specs=P(("groups", "ctx", "heads"), None),
        check_vma=False,
    )
```

```python
import functools
import math

import jax
import jax.numpy as jnp
from jax import lax
from jax.experimental import pallas as pl
from jax.experimental.pallas import tpu as pltpu
from jax.sharding import PartitionSpec as P

HDIM = 128
WINDOW = 512


def entering(x, axis, join, neutral):
    place = lax.axis_index(axis)
    gathered = lax.all_gather(x.astype(jnp.bfloat16), axis)
    state = jnp.zeros_like(x) + jnp.asarray(neutral, x.dtype)

    def one(lap, state):
        return join(state, lax.dynamic_index_in_dim(gathered, lap, 0, False).astype(x.dtype))

    return lax.fori_loop(0, place, one, state)


def from_behind(block, axis, distance):
    devices = range(lax.axis_size(axis))
    route = [(i - distance, i) for i in devices if i - distance in devices]
    return lax.ppermute(block, axis, route)


def normalize(value):
    return value * lax.rsqrt(jnp.mean(value * value, axis=-1, keepdims=True) + 1e-06)


MESH = pl.DeviceIdType.MESH
VMEM_BYTES = 60 * 1024 * 1024
FRONT_BYTES = 60 * 1024 * 1024
ADD_ROWS = 16
DOT_COLUMNS = 512
HID_COLUMNS = 256
SPANS = ((32, 0), (32, 0), (32, 0), (32, 1))
OWN_LINE, OWN_OVER, OWN_ASIDE, LOAD, ROWS, CROSS = range(6)
COMPUTE, EXCHANGE, LINE, FINISH, BESIDE = range(6, 11)
STEPS = (
    (
        (OWN_LINE, 1), (OWN_OVER, 0), (OWN_OVER, 1), (OWN_LINE, 2), (LOAD,), (OWN_ASIDE,), (OWN_OVER, 3),
        (OWN_LINE, 0), (ROWS, 1, 0), (OWN_LINE, 3), (ROWS, 1, 2), (OWN_OVER, 2), (CROSS, 0, 3), (COMPUTE, 0, 0),
        (ROWS, 1, 3), (ROWS, 3, 1), (CROSS, 1, 2), (ROWS, 1, 1), (COMPUTE, 1, 0), (CROSS, 1, 0), (ROWS, 3, 2),
        (CROSS, 1, 1), (CROSS, 3, 1), (CROSS, 1, 3), (CROSS, 0, 0), (ROWS, 3, 0), (CROSS, 3, 2), (ROWS, 2, 2),
        (CROSS, 0, 2), (COMPUTE, 1, 1), (LINE, 0, 1, 3, 0), (CROSS, 3, 3), (CROSS, 3, 0), (EXCHANGE, 1, 2),
        (ROWS, 3, 3), (LINE, 0, 1, 3, 1), (COMPUTE, 3, 1), (ROWS, 2, 0), (LINE, 0, 1, 2, 0), (ROWS, 2, 1),
        (COMPUTE, 3, 0), (LINE, 0, 3, 3, 1), (EXCHANGE, 3, 1), (EXCHANGE, 3, 2), (CROSS, 2, 3), (EXCHANGE, 3, 0),
        (ROWS, 2, 3), (EXCHANGE, 1, 0), (CROSS, 2, 0), (CROSS, 2, 2), (CROSS, 2, 1), (LINE, 0, 3, 3, 0),
        (COMPUTE, 2, 0), (LINE, 0, 3, 1, 0), (EXCHANGE, 1, 1), (LINE, 0, 3, 2, 0), (COMPUTE, 2, 1),
        (LINE, 0, 2, 3, 0), (CROSS, 0, 1), (EXCHANGE, 2, 0), (EXCHANGE, 2, 1), (LINE, 0, 3, 0, 0), (LINE, 0, 2, 3, 1),
        (EXCHANGE, 2, 2), (COMPUTE, 0, 1), (LINE, 0, 2, 0, 0), (EXCHANGE, 0, 1), (EXCHANGE, 0, 0), (LINE, 0, 2, 1, 0),
        (LINE, 0, 2, 2, 0), (LINE, 0, 1, 1, 0), (EXCHANGE, 0, 2), (FINISH, 3, 1), (LINE, 0, 1, 0, 0), (FINISH, 2, 0),
        (FINISH, 1, 0), (FINISH, 0, 0), (FINISH, 3, 0),
    ),
    (
        (OWN_ASIDE,), (OWN_LINE, 0), (OWN_OVER, 3), (OWN_OVER, 0), (OWN_LINE, 2), (ROWS, 0, 1), (OWN_LINE, 3),
        (ROWS, 0, 2), (OWN_LINE, 1), (ROWS, 3, 1), (ROWS, 2, 2), (ROWS, 0, 0), (LOAD,), (CROSS, 0, 3), (ROWS, 0, 3),
        (ROWS, 3, 2), (CROSS, 1, 3), (COMPUTE, 1, 0), (ROWS, 3, 0), (OWN_OVER, 1), (CROSS, 0, 2), (CROSS, 0, 1),
        (CROSS, 0, 0), (COMPUTE, 0, 0), (CROSS, 1, 0), (CROSS, 3, 3), (ROWS, 3, 3), (ROWS, 2, 0), (CROSS, 3, 2),
        (ROWS, 2, 1), (CROSS, 3, 0), (COMPUTE, 0, 1), (OWN_OVER, 2), (CROSS, 2, 3), (CROSS, 3, 1), (CROSS, 2, 2),
        (COMPUTE, 3, 0), (EXCHANGE, 0, 0), (CROSS, 2, 1), (EXCHANGE, 0, 2), (ROWS, 2, 3), (CROSS, 2, 0),
        (COMPUTE, 3, 1), (CROSS, 1, 1), (COMPUTE, 2, 1), (EXCHANGE, 0, 1), (CROSS, 1, 2), (COMPUTE, 2, 0),
        (LINE, 0, 3, 3, 1), (EXCHANGE, 3, 1), (EXCHANGE, 3, 2), (LINE, 0, 3, 3, 0), (COMPUTE, 1, 1), (EXCHANGE, 3, 0),
        (LINE, 0, 3, 1, 0), (LINE, 0, 3, 2, 0), (EXCHANGE, 2, 1), (LINE, 0, 2, 3, 0), (LINE, 1, 0, 3, 1),
        (EXCHANGE, 2, 2), (EXCHANGE, 2, 0), (LINE, 1, 0, 2, 0), (EXCHANGE, 1, 2), (LINE, 0, 3, 0, 0),
        (LINE, 1, 0, 1, 0), (LINE, 0, 2, 3, 1), (LINE, 1, 0, 3, 0), (LINE, 1, 0, 0, 0), (LINE, 0, 2, 0, 0),
        (EXCHANGE, 1, 1), (FINISH, 3, 1), (LINE, 0, 2, 1, 0), (EXCHANGE, 1, 0), (LINE, 0, 2, 2, 0), (FINISH, 1, 0),
        (FINISH, 3, 0), (FINISH, 2, 0), (FINISH, 0, 0),
    ),
)


def place(count):
    z = lax.axis_index("heads")
    c = lax.axis_index("ctx")
    beside = c + 1 - 2 * lax.rem(c, 2)
    across = lax.rem(c + 2, 4)
    diagonal = lax.rem(beside + 2, 4)
    return z, c, beside, across, diagonal


def greet(z, count, beside, across):
    barrier = pltpu.get_barrier_semaphore()

    def signal(target):
        pl.semaphore_signal(barrier, inc=1, device_id=target, device_id_type=MESH)

    signal({"ctx": beside})
    signal({"ctx": across})

    @pl.when(z > 0)
    def _():
        signal({"heads": z - 1})

    @pl.when(z < count - 1)
    def _():
        signal({"heads": z + 1})

    pl.semaphore_wait(barrier, 2 + jnp.minimum(z, 1) + jnp.minimum(count - 1 - z, 1))


def nearest(count, z, index):
    index = count - 1 - index
    more = jnp.maximum(z, count - 1 - z)
    fewer = count - 1 - more
    alone = more - fewer
    paired = jnp.maximum(index - alone, 0)
    up = jnp.where(z + more < count, more - index, index - more)
    both = (fewer - paired // 2) * (1 - 2 * (paired % 2))
    offset = jnp.where(index < alone, up, both)
    return z + jnp.where(index < count - 1, offset, 0)


def attend_kernel(
    count, tokens_ref, share_hbm, table_ref, state_ref, past_hbm, qkv_hbm,
    hidden_ref, normed_ref, tables_ref,
    slab_ref, qkv_ref, w_ref, query_ref, kv_ref, before_ref, inside_ref, linear_ref,
    state_out, states_in, heads_out, heads_in,
    local_sem, token_send, token_recv, share_send, share_recv,
    tail_send, tail_recv, state_send, state_recv, head_send, head_recv,
):
    z, c, beside, across, diagonal = place(count)
    row_count, width = tokens_ref.shape
    slab_rows = count * row_count
    share = w_ref.shape[0] // (4 * count)

    def rows_of(index, size):
        return pl.ds(pl.multiple_of(index * size, size), size)

    def share_block(kind, zz, cc):
        if kind == 0:
            return w_ref.at[rows_of(zz * 4 + cc, share), :]
        return tables_ref.at[cc * count + zz]

    def share_source(kind):
        return table_ref if kind else share_hbm.at[rows_of(c, share), :]

    local = [
        pltpu.make_async_copy(source, target, local_sem.at[index])
        for index, (source, target) in enumerate(
            [(qkv_hbm.at[one], qkv_ref.at[:, one * HDIM : (one + 1) * HDIM]) for one in range(3)]
            + [(tokens_ref, slab_ref.at[z])]
            + [(share_source(kind), share_block(kind, z, c)) for kind in (0, 1)]
        )
    ]
    past_copy = pltpu.make_async_copy(past_hbm, before_ref, local_sem.at[6])
    for copy in local:
        copy.start()

    @pl.when(c == 0)
    def _():
        past_copy.start()

    barrier = pltpu.get_barrier_semaphore()
    for target in (beside, across, diagonal):
        pl.semaphore_signal(barrier, inc=1, device_id={"ctx": target}, device_id_type=MESH)
    for zz in range(count):

        @pl.when(zz != z)
        def _():
            pl.semaphore_signal(barrier, inc=1, device_id={"heads": zz}, device_id_type=MESH)

    pl.semaphore_wait(barrier, 3 + count - 1)

    def remote(source, target, send, recv, device):
        return pltpu.make_async_remote_copy(
            src_ref=source, dst_ref=target, send_sem=send, recv_sem=recv,
            device_id=device, device_id_type=MESH,
        )

    def started(copy):
        copy.start()

    def left(copy):
        copy.wait_send()

    def along(act, zz, copy):
        @pl.when(jnp.logical_and(zz >= z, z > 0))
        def _():
            act(copy(0, {"heads": z - 1}))

        @pl.when(jnp.logical_and(zz <= z, z < count - 1))
        def _():
            act(copy(1, {"heads": z + 1}))

    def token_copy(zz, own=False):
        def copy(way, device):
            source = tokens_ref if own else slab_ref.at[zz]
            return remote(source, slab_ref.at[zz], token_send.at[way, zz], token_recv.at[zz], device)

        return copy

    def share_copy(kind, zz, cc, own=False):
        def copy(way, device):
            block = share_block(kind, zz, cc)
            slot = zz * 4 + cc
            source = share_source(kind) if own else block
            return remote(
                source, block, share_send.at[kind, way, slot], share_recv.at[kind, slot], device
            )

        return copy

    def aside(act, zz, cc, own=False):
        for kind in (0, 1):
            act(share_copy(kind, zz, cc, own)(3, {"ctx": beside}))

    def share_relay(act, zz, own=False):
        for kind in (0, 1):
            act(share_copy(kind, zz, c, own)(2, {"ctx": across}))
        aside(act, zz, c, own)

    def share_along(act, zz, own=False):
        for kind in (0, 1):
            along(act, zz, share_copy(kind, zz, c, own))

    def share_received(zz, cc):
        for kind in (0, 1):
            share_copy(kind, zz, cc)(3, {"ctx": beside}).wait_recv()

    def at_distance(distance, act):
        @pl.when(z >= distance)
        def _():
            act(z - distance)

        @pl.when(z + distance < count)
        def _():
            act(z + distance)

    def share_onward(zz):
        share_received(zz, c)
        share_along(started, zz)
        share_relay(started, zz)

    def share_over(zz):
        share_received(zz, across)
        aside(started, zz, across)

    along(started, z, token_copy(z, True))
    share_relay(started, z, True)
    for copy in local:
        copy.wait()

    def project(zz):
        product = jnp.dot(slab_ref[zz], qkv_ref[...], preferred_element_type=jnp.float32)
        product = product.astype(query_ref.dtype)
        rows = rows_of(zz, row_count)
        query_ref[rows, :] = product[:, :HDIM]
        kv_ref[0, rows, :] = product[:, HDIM : 2 * HDIM]
        kv_ref[1, rows, :] = product[:, 2 * HDIM :]

        @pl.when(c < 3)
        def _():
            tail_copy(zz).start()

    def tail_copy(zz):
        rows = rows_of(zz, row_count)
        return remote(
            kv_ref.at[:, rows, :], before_ref.at[:, rows, :], tail_send.at[zz], tail_recv.at[zz],
            {"ctx": jnp.minimum(c + 1, 3)},
        )

    def token_relay(zz):
        token_copy(zz)(0, {"heads": z - 1}).wait_recv()
        along(started, zz, token_copy(zz))

    def step(index, _):
        zz = nearest(count, z, index)
        last = nearest(count, z, jnp.maximum(index - 1, 0))
        after = nearest(count, z, jnp.minimum(index + 1, count - 1))
        opens = jnp.logical_and(index > 0, jnp.abs(zz - z) != jnp.abs(last - z))
        double = jnp.logical_and(index < count - 1, jnp.abs(after - z) == jnp.abs(zz - z))

        @pl.when(opens)
        def _():
            token_relay(zz)

        @pl.when(jnp.logical_and(opens, double))
        def _():
            token_relay(after)

        project(zz)
        alone = jnp.logical_and(index > 0, jnp.logical_not(jnp.logical_and(opens, double)))
        distance = jnp.abs(zz - z)

        @pl.when(jnp.logical_and(alone, distance == 1))
        def _():
            share_along(started, z, True)

        @pl.when(jnp.logical_and(alone, distance > 1))
        def _():
            at_distance(distance - 1, share_onward)

        return 0

    lax.fori_loop(0, count, step, 0)

    local_state = lax.dot_general(
        kv_ref[0], kv_ref[1], (((0,), (0,)), ((), ())), preferred_element_type=jnp.float32
    )
    state_out[...] = local_state.astype(state_out.dtype)
    others = [beside, across, diagonal]
    state_copies = [
        remote(state_out, states_in.at[c], state_send.at[way], state_recv.at[c], {"ctx": target})
        for way, target in enumerate(others)
    ]
    for copy in state_copies:
        copy.start()
    share_over(z)

    blocks = slab_rows // row_count
    for block in range(blocks):
        first, end = block * row_count, (block + 1) * row_count
        query = query_ref[first:end, :]
        scores = lax.dot_general(
            query, kv_ref[0, :end, :], (((1,), (1,)), ((), ())), preferred_element_type=jnp.float32
        )
        shape = scores.shape
        causal = lax.broadcasted_iota(jnp.int32, shape, 1) <= first + lax.broadcasted_iota(
            jnp.int32, shape, 0
        )
        inside_ref[first:end, :end] = scores
        weights = jnp.where(causal, scores, 0.0).astype(kv_ref.dtype)
        linear_ref[first:end, :] = jnp.dot(
            weights, kv_ref[1, :end, :], preferred_element_type=jnp.float32
        )

    for target in others:
        remote(
            state_out, states_in.at[target], state_send.at[0], state_recv.at[target],
            {"ctx": beside},
        ).wait_recv()
    start = state_ref[...]
    for cc in range(4):
        start = start + jnp.where(cc < c, states_in[cc].astype(jnp.float32), 0.0)

    @pl.when(c == 0)
    def _():
        past_copy.wait()

    @pl.when(c > 0)
    def _():
        for zz in range(count):
            tail_copy(zz).wait_recv()

    scale = 1.0 / math.sqrt(HDIM)

    def head_copy(zz):
        columns = pl.ds(pl.multiple_of(z * HDIM, HDIM), HDIM)
        return remote(
            heads_out.at[zz], heads_in.at[:, columns], head_send.at[zz], head_recv.at[z],
            {"heads": zz},
        )

    for block in range(blocks):
        first, end = block * row_count, (block + 1) * row_count
        query = query_ref[first:end, :]
        old = lax.dot_general(
            query, before_ref[0, first:, :], (((1,), (1,)), ((), ())),
            preferred_element_type=jnp.float32,
        )
        old_seen = lax.broadcasted_iota(jnp.int32, old.shape, 1) > lax.broadcasted_iota(
            jnp.int32, old.shape, 0
        )
        old = jnp.where(old_seen, old * scale, -jnp.inf)
        new = inside_ref[first:end, :end]
        new_seen = lax.broadcasted_iota(jnp.int32, new.shape, 1) <= first + lax.broadcasted_iota(
            jnp.int32, new.shape, 0
        )
        new = jnp.where(new_seen, new * scale, -jnp.inf)
        top = jnp.maximum(
            jnp.max(old, axis=-1, keepdims=True), jnp.max(new, axis=-1, keepdims=True)
        )
        old = jnp.exp(old - top)
        new = jnp.exp(new - top)
        inverse = 1.0 / (
            jnp.sum(old, axis=-1, keepdims=True) + jnp.sum(new, axis=-1, keepdims=True)
        )
        window = jnp.dot(
            (old * inverse).astype(kv_ref.dtype), before_ref[1, first:, :],
            preferred_element_type=jnp.float32,
        ) + jnp.dot(
            (new * inverse).astype(kv_ref.dtype), kv_ref[1, :end, :],
            preferred_element_type=jnp.float32,
        )
        linear = linear_ref[first:end, :] + jnp.dot(
            query.astype(jnp.float32), start, precision=lax.Precision.HIGHEST,
            preferred_element_type=jnp.float32,
        )
        heads_out[block] = (normalize(linear) + window).astype(heads_out.dtype)

        @pl.when(block != z)
        def _():
            head_copy(block).start()

        @pl.when(block == z)
        def _():
            columns = pl.ds(pl.multiple_of(z * HDIM, HDIM), HDIM)
            heads_in[:, columns] = heads_out[block]

        if block == 0:
            at_distance(jnp.maximum(z, count - 1 - z), share_onward)
        if block + 1 < count:
            at_distance(block + 1, share_over)

    for zz in range(count):
        share_received(zz, beside)
        share_received(zz, diagonal)

        @pl.when(zz != z)
        def _():
            remote(
                heads_out.at[zz], heads_in.at[:, zz * HDIM : (zz + 1) * HDIM], head_send.at[zz],
                head_recv.at[zz], {"heads": zz},
            ).wait_recv()

    def out_tile(index, total):
        columns = pl.ds(pl.multiple_of(index * DOT_COLUMNS, DOT_COLUMNS), DOT_COLUMNS)
        attn = jnp.dot(heads_in[...], w_ref[:, columns], preferred_element_type=jnp.float32)
        hidden = (tokens_ref[:, columns].astype(jnp.float32) + attn).astype(hidden_ref.dtype)
        hidden_ref[:, columns] = hidden
        hidden = hidden.astype(jnp.float32)
        return total + jnp.sum(hidden * hidden, axis=-1, keepdims=True)

    total = lax.fori_loop(
        0, width // DOT_COLUMNS, out_tile, jnp.zeros((row_count, 1), jnp.float32)
    )
    inverse = lax.rsqrt(total / width + 1e-06)
    for first in range(0, width, DOT_COLUMNS):
        hidden = hidden_ref[:, first : first + DOT_COLUMNS].astype(jnp.float32)
        normed_ref[:, first : first + DOT_COLUMNS] = (hidden * inverse).astype(normed_ref.dtype)

    along(left, z, token_copy(z, True))
    share_along(left, z, True)
    share_relay(left, z, True)

    @pl.when(c < 3)
    def _():
        for zz in range(count):
            tail_copy(zz).wait_send()

    for copy in state_copies:
        copy.wait_send()
    for zz in range(count):
        aside(left, zz, across)

        @pl.when(zz != z)
        def _():
            along(left, zz, token_copy(zz))
            share_along(left, zz)
            share_relay(left, zz)
            head_copy(zz).wait_send()


def plain_steps(count, at):
    spans = range(len(SPANS))
    steps = [(OWN_LINE, span) for span in spans] + [(OWN_OVER, span) for span in spans]
    steps += [(OWN_ASIDE,), (LOAD,)]
    for distance in range(count):
        planes = sorted({at - distance, at + distance} & set(range(count)))
        for op in (ROWS, CROSS):
            if op == CROSS or distance:
                steps += [(op, zz, span) for zz in planes for span in reversed(spans)]
        steps += [(COMPUTE, zz, pair) for zz in planes for pair in (0, 1)]
    near = [span for span in spans if not SPANS[span][1]]
    far = [span for span in spans if SPANS[span][1]]
    steps += [(EXCHANGE, zz, span) for zz in range(count) for span in near]
    for key in range(1, count):
        links = [(0, key)] * (key > at) + [(1, count - 1 - key)] * (count - 1 - key < at)
        for link in links if at < count - 1 - at else reversed(links):
            steps += [(LINE, *link, span, 0) for span in spans]
            steps += [(LINE, *link, span, 1) for span in far]
    return steps + [(FINISH, span, 1) for span in far] + [(FINISH, span, 0) for span in spans]


def mirrored(step, count):
    op, *where = step
    if op in (ROWS, CROSS, EXCHANGE, COMPUTE):
        return (op, count - 1 - where[0], where[1])
    if op == LINE:
        return (op, 1 - where[0], count - 1 - where[1], *where[2:])
    return step


def steps_of(count, at):
    if count != len(STEPS) * 2:
        return plain_steps(count, at)
    if at < len(STEPS):
        return list(STEPS[at])
    return [mirrored(step, count) for step in STEPS[count - 1 - at]]


def span_rows(row_count):
    spans, first = [], 0
    for share, far in SPANS:
        spans.append((first, row_count * share // 128, far))
        first += row_count * share // 128
    return spans, sum(size for _, size, far in spans if far)


def expert_kernel(
    count, hidden_ref, own_ref, table_ref, gate_hbm, up_hbm, down_hbm, out_ref,
    rows_ref, part_ref, hid_ref, scale_ref, gate_ref, up_ref, down_ref,
    from_beside, to_across, from_across, line_out, line_in, last_out, last_in,
    local_sem, row_send, row_recv, beside_send, beside_recv, across_send, across_recv,
    line_send, line_recv, last_send, last_recv,
):
    z, c, beside, across, diagonal = place(count)
    row_count, width = own_ref.shape
    spans, far_rows = span_rows(row_count)
    near_rows = row_count - far_rows
    expert = c * count + z
    local = [
        pltpu.make_async_copy(source, target, local_sem.at[index])
        for index, (source, target) in enumerate(
            [
                (gate_hbm, gate_ref),
                (up_hbm, up_ref),
                (down_hbm, down_ref),
                (own_ref, rows_ref.at[z, pl.ds(pl.multiple_of(c * row_count, row_count), row_count), :]),
            ]
        )
    ]
    for copy in local:
        copy.start()
    greet(z, count, beside, across)

    def window(cc, span):
        first, size, _ = spans[span]
        return pl.ds(pl.multiple_of(cc * row_count + first, 16), size)

    def row_copy(zz, cc, span, way, target, own=False):
        first, size, _ = spans[span]
        slot = zz * 4 + cc
        block = rows_ref.at[zz, window(cc, span), :]
        return pltpu.make_async_remote_copy(
            src_ref=own_ref.at[pl.ds(first, size), :] if own else block,
            dst_ref=block,
            send_sem=row_send.at[way, span, slot],
            recv_sem=row_recv.at[span, slot],
            device_id=target,
            device_id_type=MESH,
        )

    def started(copy):
        copy.start()

    def left(copy):
        copy.wait_send()

    def received(zz, cc, span):
        row_copy(zz, cc, span, 0, {"ctx": beside}).wait_recv()

    def along(act, at, zz, cc, span, own=False):
        if zz >= at and at > 0:
            act(row_copy(zz, cc, span, 0, {"heads": at - 1}, own))
        if zz <= at and at < count - 1:
            act(row_copy(zz, cc, span, 1, {"heads": at + 1}, own))

    def over(act, zz, cc, span, own=False):
        act(row_copy(zz, cc, span, 2, {"ctx": across}, own))

    def aside(act, zz, cc, span, own=False):
        act(row_copy(zz, cc, span, 3, {"ctx": beside}, own))

    def relays(op, at, zz, span, act, wait):
        cc = c if op == ROWS else across
        far = spans[span][2]
        if wait:
            received(zz, cc, span)
        if op == ROWS or far:
            along(act, at, zz, cc, span)
        if op == ROWS and not far:
            over(act, zz, cc, span)
        aside(act, zz, cc, span)

    def paired(zz, pair):
        for span in range(len(spans)):
            received(zz, diagonal if pair else beside, span)

    def compute(zz, pair):
        half = jnp.where(pair == 0, c // 2, 1 - c // 2)
        for core in range(2):
            row = table_ref[(half * 2 + core) * count + zz, pl.ds(expert, 1), :]
            scale_ref[core * row_count : (core + 1) * row_count, :] = jnp.broadcast_to(
                row, (HDIM, row_count)
            ).T

        inner = gate_ref.shape[1]
        rows = pl.ds(pl.multiple_of(half * 2 * row_count, 2 * row_count), 2 * row_count)

        def hidden_tile(index, _):
            columns = pl.ds(pl.multiple_of(index * HID_COLUMNS, HID_COLUMNS), HID_COLUMNS)
            block = rows_ref[zz, rows, :]
            gate = jnp.dot(block, gate_ref[:, columns], preferred_element_type=jnp.float32)
            up = jnp.dot(block, up_ref[:, columns], preferred_element_type=jnp.float32)
            scale = jnp.concatenate([scale_ref[...]] * (HID_COLUMNS // HDIM), axis=1)
            hid_ref[:, columns] = (jax.nn.silu(gate) * up * scale).astype(hid_ref.dtype)
            return 0

        lax.fori_loop(0, inner // HID_COLUMNS, hidden_tile, 0)

        def out_tile(index, _):
            columns = pl.ds(pl.multiple_of(index * DOT_COLUMNS, DOT_COLUMNS), DOT_COLUMNS)
            product = jnp.dot(
                hid_ref[...], down_ref[:, columns], preferred_element_type=jnp.float32
            )
            part_ref[zz, rows, columns] = product.astype(part_ref.dtype)
            return 0

        lax.fori_loop(0, width // DOT_COLUMNS, out_tile, 0)

    def beside_copy(kind, zz):
        cc = diagonal if kind == 0 else beside
        return pltpu.make_async_remote_copy(
            src_ref=part_ref.at[zz, pl.ds(pl.multiple_of(cc * row_count, row_count), row_count), :],
            dst_ref=from_beside.at[kind, zz],
            send_sem=beside_send.at[kind, zz],
            recv_sem=beside_recv.at[kind, zz],
            device_id={"ctx": beside},
            device_id_type=MESH,
        )

    def across_copy(zz, span):
        first, size, _ = spans[span]
        return pltpu.make_async_remote_copy(
            src_ref=to_across.at[zz, pl.ds(first, size), :],
            dst_ref=from_across.at[zz, pl.ds(first, size), :],
            send_sem=across_send.at[span, zz],
            recv_sem=across_recv.at[span, zz],
            device_id={"ctx": across},
            device_id_type=MESH,
        )

    def line_rows(span, other):
        first, size, _ = spans[span]
        return pl.ds(row_count + first - near_rows if other else first, size)

    def line_copy(side, zz, span, other):
        return pltpu.make_async_remote_copy(
            src_ref=line_out.at[zz, line_rows(span, other), :],
            dst_ref=line_in.at[side, zz, line_rows(span, other), :],
            send_sem=line_send.at[2 * span + other, zz],
            recv_sem=line_recv.at[2 * span + other, side, zz],
            device_id={"heads": z + 1 - 2 * side},
            device_id_type=MESH,
        )

    def last_rows(span):
        first, size, _ = spans[span]
        return pl.ds(first - near_rows, size)

    def last_copy(span):
        return pltpu.make_async_remote_copy(
            src_ref=last_out.at[last_rows(span), :],
            dst_ref=last_in.at[last_rows(span), :],
            send_sem=last_send.at[span],
            recv_sem=last_recv.at[span],
            device_id={"ctx": across},
            device_id_type=MESH,
        )

    def add(target, sources):
        def chunk(index, _):
            rows = pl.ds(pl.multiple_of(index * ADD_ROWS, ADD_ROWS), ADD_ROWS)
            total = sources[0][rows, :].astype(jnp.float32)
            for source in sources[1:]:
                total = total + source[rows, :].astype(jnp.float32)
            target[rows, :] = total.astype(target.dtype)
            return 0

        lax.fori_loop(0, target.shape[0] // ADD_ROWS, chunk, 0)

    def starts(side, at):
        return at == side * (count - 1)

    def chip_sources(zz, span, other):
        first, size, far = spans[span]
        start = pl.multiple_of((across if other else c) * row_count + first, 16)
        sources = [
            part_ref.at[zz, pl.ds(start, size), :],
            from_beside.at[1 - other, zz, pl.ds(first, size), :],
        ]
        if not far and not other:
            sources.append(from_across.at[zz, pl.ds(first, size), :])
        return sources

    def perform(at, steps, waited):
        waited = set(waited)

        def once(kind, zz):
            if (kind, zz) not in waited:
                waited.add((kind, zz))
                beside_copy(kind, zz).wait_recv()

        def arrived(zz, span, other, sides):
            once(1 - other, zz)
            if not spans[span][2]:
                across_copy(zz, span).wait_recv()
            sources = chip_sources(zz, span, other)
            for side in sides:
                if not starts(side, at):
                    line_copy(side, zz, span, other).wait_recv()
                    sources.append(line_in.at[side, zz, line_rows(span, other), :])
            return sources

        for op, *where in steps:
            if op == OWN_LINE:
                along(started, at, at, c, where[0], True)
            elif op == OWN_OVER:
                over(started, at, c, where[0], True)
            elif op == OWN_ASIDE:
                for span in range(len(spans)):
                    aside(started, at, c, span, True)
            elif op == LOAD:
                for copy in local:
                    copy.wait()
            elif op == COMPUTE:
                paired(*where)
            elif op == BESIDE:
                beside_copy(where[1], where[0]).start()
            elif op == EXCHANGE:
                zz, span = where
                once(0, zz)
                first, size, _ = spans[span]
                start = pl.multiple_of(across * row_count + first, 16)
                add(
                    to_across.at[zz, pl.ds(first, size), :],
                    [
                        part_ref.at[zz, pl.ds(start, size), :],
                        from_beside.at[0, zz, pl.ds(first, size), :],
                    ],
                )
                across_copy(zz, span).start()
            elif op == LINE:
                side, zz, span, other = where
                add(line_out.at[zz, line_rows(span, other), :], arrived(zz, span, other, (side,)))
                line_copy(side, zz, span, other).start()
            elif op == FINISH and where[1]:
                span = where[0]
                add(last_out.at[last_rows(span), :], arrived(at, span, 1, (0, 1)))
                last_copy(span).start()
            elif op == FINISH:
                span = where[0]
                first, size, far = spans[span]
                rows = pl.ds(first, size)
                sources = arrived(at, span, 0, (0, 1))
                if far:
                    last_copy(span).wait_recv()
                    sources.append(last_in.at[last_rows(span), :])
                add(out_ref.at[rows, :], [hidden_ref.at[rows, :]] + sources)
            else:
                relays(op, at, *where, started, True)

    def each_place(act):
        for at in range(count):

            @pl.when(z == at)
            def _():
                act(at)

    units = 2 * count
    segments, orders = [], []
    for at in range(count):
        parts, order = [[]], []
        for one in steps_of(count, at):
            parts[-1].append(one)
            if one[0] == COMPUTE:
                zz, pair = one[1:]
                order.append((zz, pair))
                parts.append([(BESIDE, zz, 1 - pair)])
        segments.append(parts)
        orders.append(order)

    def waits_of(at, unit):
        keys = set()
        for op, *where in sum(segments[at][:unit], []):
            if op == EXCHANGE:
                keys.add((0, where[0]))
            elif op == LINE:
                keys.add((1 - where[3], where[1]))
            elif op == FINISH:
                keys.add((1 - where[1], at))
        return keys

    def choose(index, pick):
        value = jnp.int32(0)
        for at in range(count):
            for unit in range(units):
                here = jnp.logical_and(z == at, index == unit)
                value = jnp.where(here, pick(orders[at][unit]), value)
        return value

    def step(index, _):
        def segment(at):
            for unit in range(units):

                @pl.when(index == unit)
                def _():
                    perform(at, segments[at][unit], waits_of(at, unit))

        each_place(segment)
        compute(choose(index, lambda unit: unit[0]), choose(index, lambda unit: unit[1]))
        return 0

    lax.fori_loop(0, units, step, 0)

    def finish(at):
        perform(at, segments[at][units], waits_of(at, units))
        for span, (_, _, far) in enumerate(spans):
            if far:
                last_copy(span).wait_send()
            along(left, at, at, c, span, True)
            over(left, at, c, span, True)
            aside(left, at, c, span, True)
            for zz in range(count):
                relays(CROSS, at, zz, span, left, False)
                if not far:
                    across_copy(zz, span).wait_send()
                if zz != at:
                    relays(ROWS, at, zz, span, left, False)
                    for other in range(1 + far):
                        line_copy(int(zz < at), zz, span, other).wait_send()
        for zz in range(count):
            beside_copy(0, zz).wait_send()
            beside_copy(1, zz).wait_send()

    each_place(finish)


def attend(tokens, w_out, table, state_in, past_kv, w_qkv):
    count = lax.axis_size("heads")
    row_count, width = tokens.shape
    slab_rows = count * row_count
    kind = tokens.dtype
    slots = 4 * count
    dma = pltpu.SemaphoreType.DMA
    vmem, anywhere = pl.BlockSpec(memory_space=pltpu.VMEM), pl.BlockSpec(memory_space=pl.ANY)
    return pl.pallas_call(
        functools.partial(attend_kernel, count),
        out_shape=[
            jax.ShapeDtypeStruct((row_count, width), kind),
            jax.ShapeDtypeStruct((row_count, width), kind),
            jax.ShapeDtypeStruct((slots,) + table.shape, table.dtype),
        ],
        in_specs=[vmem, anywhere, vmem, vmem, anywhere, anywhere],
        out_specs=[vmem, vmem, anywhere],
        scratch_shapes=[
            pltpu.VMEM((count, row_count, width), kind),
            pltpu.VMEM((width, 3 * HDIM), kind),
            pltpu.VMEM((count * HDIM, width), kind),
            pltpu.VMEM((slab_rows, HDIM), kind),
            pltpu.VMEM((2, slab_rows, HDIM), kind),
            pltpu.VMEM((2, WINDOW, HDIM), kind),
            pltpu.VMEM((slab_rows, slab_rows), jnp.float32),
            pltpu.VMEM((slab_rows, HDIM), jnp.float32),
            pltpu.VMEM((HDIM, HDIM), kind),
            pltpu.VMEM((4, HDIM, HDIM), kind),
            pltpu.VMEM((count, row_count, HDIM), kind),
            pltpu.VMEM((row_count, count * HDIM), kind),
            dma((7,)),
            dma((2, count)),
            dma((count,)),
            dma((2, 4, slots)),
            dma((2, slots)),
            dma((count,)),
            dma((count,)),
            dma((3,)),
            dma((4,)),
            dma((count,)),
            dma((count,)),
        ],
        compiler_params=pltpu.CompilerParams(
            collective_id=2, has_side_effects=True, vmem_limit_bytes=FRONT_BYTES
        ),
        name="attend",
    )(tokens, w_out, table, state_in, past_kv, w_qkv)


def run_experts(hidden, normed, tables, w_gate, w_up, w_down):
    count = lax.axis_size("heads")
    row_count, width = normed.shape
    inner = w_gate.shape[1]
    far_rows = span_rows(row_count)[1]
    near_rows = row_count - far_rows
    cuts = len(SPANS)
    dma = pltpu.SemaphoreType.DMA
    kind = normed.dtype
    vmem, anywhere = pl.BlockSpec(memory_space=pltpu.VMEM), pl.BlockSpec(memory_space=pl.ANY)
    return pl.pallas_call(
        functools.partial(expert_kernel, count),
        out_shape=jax.ShapeDtypeStruct((row_count, width), kind),
        in_specs=[vmem] * 3 + [anywhere] * 3,
        out_specs=vmem,
        scratch_shapes=[
            pltpu.VMEM((count, 4 * row_count, width), kind),
            pltpu.VMEM((count, 4 * row_count, width), kind),
            pltpu.VMEM((2 * row_count, inner), kind),
            pltpu.VMEM((2 * row_count, HDIM), jnp.float32),
            pltpu.VMEM(w_gate.shape, kind),
            pltpu.VMEM(w_up.shape, kind),
            pltpu.VMEM(w_down.shape, kind),
            pltpu.VMEM((2, count, row_count, width), kind),
            pltpu.VMEM((count, near_rows, width), kind),
            pltpu.VMEM((count, near_rows, width), kind),
            pltpu.VMEM((count, row_count + far_rows, width), kind),
            pltpu.VMEM((2, count, row_count + far_rows, width), kind),
            pltpu.VMEM((far_rows, width), kind),
            pltpu.VMEM((far_rows, width), kind),
            dma((4,)),
            dma((4, cuts, 4 * count)),
            dma((cuts, 4 * count)),
            dma((2, count)),
            dma((2, count)),
            dma((cuts, count)),
            dma((cuts, count)),
            dma((2 * cuts, count)),
            dma((2 * cuts, 2, count)),
            dma((cuts,)),
            dma((cuts,)),
        ],
        compiler_params=pltpu.CompilerParams(
            collective_id=0, has_side_effects=True, vmem_limit_bytes=VMEM_BYTES
        ),
        name="run_experts",
    )(hidden, normed, tables, w_gate, w_up, w_down)


def expert_table(expert_ids, gate_weights, expert_count):
    chosen = expert_ids[:, :, None] == jnp.arange(expert_count, dtype=jnp.int32)
    return jnp.sum(jnp.where(chosen, gate_weights[:, :, None], 0.0), axis=1).T


def on_device(
    tokens, state_in, past_kv, w_qkv, w_out, w_gate, w_up, w_down, expert_ids, gate_weights
):
    row_count, model_width = tokens.shape
    inner_width = w_qkv.shape[2]
    local_heads = inner_width // HDIM
    ctx_count = lax.axis_size("ctx")
    head_count = lax.axis_size("heads")
    exp_local = w_gate.shape[0]
    devices = ctx_count * head_count
    expert_count = exp_local * devices
    top_count = expert_ids.shape[1]
    capacity = max(2, 2 * row_count * top_count // expert_count)
    dense = (
        ctx_count == 4
        and exp_local == 1
        and row_count % HDIM == 0
        and local_heads == 1
        and head_count * row_count == WINDOW
        and w_gate.shape[2] % HID_COLUMNS == 0
        and row_count * devices <= expert_count * capacity
    )
    if dense:
        table = expert_table(expert_ids, gate_weights, expert_count)
        hidden_state, normed, tables = attend(
            tokens, w_out, table, state_in[0], past_kv, jnp.transpose(w_qkv, (1, 0, 2))
        )
        return run_experts(hidden_state, normed, tables, w_gate[0], w_up[0], w_down[0])
    slab, w_rows = [
        lax.all_gather(value, "heads", axis=0, tiled=True) for value in (tokens, w_out)
    ]
    projected = jnp.dot(
        slab,
        w_qkv.reshape(model_width, 3 * inner_width),
        preferred_element_type=jnp.float32,
    ).astype(jnp.bfloat16)
    slab_rows = projected.shape[0]
    projected = projected.reshape(slab_rows, 3, local_heads, HDIM)
    query = jnp.transpose(projected[:, 0], (1, 0, 2))
    keys = jnp.transpose(projected[:, 1], (1, 0, 2))
    values = jnp.transpose(projected[:, 2], (1, 0, 2))
    local_state = jnp.einsum("hsd,hse->hde", keys, values, preferred_element_type=jnp.float32)
    earlier_state = entering(
        local_state, "ctx", lambda first, second: first + second, jnp.zeros_like(local_state)
    )
    start_state = state_in + earlier_state
    tail = jnp.stack([keys, values], axis=0)
    arrived = from_behind(tail, "ctx", 1)
    past = jnp.transpose(past_kv.reshape(2, WINDOW, local_heads, HDIM), (0, 2, 1, 3))
    previous = jnp.where(lax.axis_index("ctx") == 0, past, arrived)
    all_keys = jnp.concatenate([previous[0], keys], axis=1)
    all_values = jnp.concatenate([previous[1], values], axis=1)
    block_rows = min(slab_rows, 512)
    block_count = slab_rows // block_rows
    scale = 1.0 / math.sqrt(HDIM)
    causal = jnp.arange(block_rows)[:, None] >= jnp.arange(block_rows)[None, :]
    offsets = jnp.arange(WINDOW + block_rows)[None, :] - jnp.arange(block_rows)[:, None]
    in_window = (offsets > 0) & (offsets <= WINDOW)

    def block_step(state, index):
        first = index * block_rows
        carried = jnp.einsum(
            "hsd,hde->hse", query.astype(jnp.float32), state, precision=lax.Precision.HIGHEST
        )
        inside = jnp.einsum("hsd,htd->hst", query, keys, preferred_element_type=jnp.float32)
        inside = jnp.where(causal[None], inside, 0.0).astype(jnp.bfloat16)
        linear = carried + jnp.einsum(
            "hst,hte->hse", inside, values, preferred_element_type=jnp.float32
        )
        scores = (
            jnp.einsum("hsd,htd->hst", query, all_keys, preferred_element_type=jnp.float32) * scale
        )
        scores = jnp.where(in_window[None], scores, -jnp.inf)
        top_score = jnp.max(scores, axis=-1, keepdims=True)
        expo = jnp.exp(scores - top_score)
        probs = (expo / jnp.sum(expo, axis=-1, keepdims=True)).astype(jnp.bfloat16)
        window_out = jnp.einsum(
            "hst,hte->hse", probs, all_values, preferred_element_type=jnp.float32
        )
        combined = (normalize(linear) + window_out).astype(jnp.bfloat16)
        new_state = state + jnp.einsum(
            "hsd,hse->hde", keys, values, preferred_element_type=jnp.float32
        )
        return (new_state, combined)

    _, outs = lax.scan(block_step, start_state, jnp.arange(block_count, dtype=jnp.int32))
    heads_out = jnp.transpose(outs, (0, 2, 1, 3)).reshape(slab_rows, inner_width)
    regrouped = lax.all_to_all(heads_out, "heads", split_axis=0, concat_axis=1, tiled=True)
    attn = jnp.dot(
        regrouped,
        w_rows,
        preferred_element_type=jnp.float32,
    )
    hidden_state = (tokens.astype(jnp.float32) + attn).astype(jnp.bfloat16)
    hidden_float = hidden_state.astype(jnp.float32)
    normed = normalize(hidden_float).astype(jnp.bfloat16)
    picks = expert_ids.reshape(-1)
    onehot = (picks[:, None] == jnp.arange(expert_count, dtype=jnp.int32)[None, :]).astype(
        jnp.int32
    )
    earlier = jnp.cumsum(onehot, axis=0) - onehot
    slots = jnp.sum(onehot * earlier, axis=1)
    destination = picks * capacity + slots
    source_rows = jnp.arange(row_count * top_count, dtype=jnp.int32) // top_count
    outgoing = jnp.zeros((expert_count * capacity, model_width), jnp.bfloat16)
    outgoing = outgoing.at[destination].set(normed[source_rows])
    sendable = outgoing.reshape(expert_count, 1, capacity, model_width)
    arrived_rows = lax.all_to_all(
        sendable, ("ctx", "heads"), split_axis=0, concat_axis=1, tiled=True
    )
    e_count, n_count, c_count, d_count = arrived_rows.shape
    flat = arrived_rows.reshape(e_count, n_count * c_count, d_count)
    gate_act = jnp.einsum("erd,edf->erf", flat, w_gate, preferred_element_type=jnp.float32)
    up_act = jnp.einsum("erd,edf->erf", flat, w_up, preferred_element_type=jnp.float32)
    hid = (jax.nn.silu(gate_act) * up_act).astype(jnp.bfloat16)
    out_rows = jnp.einsum("erf,efd->erd", hid, w_down, preferred_element_type=jnp.float32)
    finished = out_rows.astype(jnp.bfloat16).reshape(e_count, n_count, c_count, d_count)
    returned = lax.all_to_all(finished, ("ctx", "heads"), split_axis=1, concat_axis=0, tiled=True)
    returned = returned.reshape(expert_count * capacity, model_width)
    picked = returned[destination].reshape(row_count, top_count, model_width).astype(jnp.float32)
    routed = jnp.sum(gate_weights[:, :, None] * picked, axis=1)
    return (hidden_float + routed).astype(jnp.bfloat16)


def solution(mesh):
    return jax.shard_map(
        on_device,
        mesh=mesh,
        in_specs=(
            P(("groups", "ctx", "heads"), None),
            P("heads", "groups", None),
            P(None, "groups", "heads"),
            P(None, None, "heads"),
            P("heads", None),
            P(("ctx", "heads"), None, None),
            P(("ctx", "heads"), None, None),
            P(("ctx", "heads"), None, None),
            P(("groups", "ctx", "heads"), None),
            P(("groups", "ctx", "heads"), None),
        ),
        out_specs=P(("groups", "ctx", "heads"), None),
        check_vma=False,
    )
```

```python
import functools
import math

import jax
import jax.numpy as jnp
from jax import lax
from jax.experimental import pallas as pl
from jax.experimental.pallas import tpu as pltpu
from jax.sharding import PartitionSpec as P

HDIM = 128
WINDOW = 512


def entering(x, axis, join, neutral):
    place = lax.axis_index(axis)
    gathered = lax.all_gather(x.astype(jnp.bfloat16), axis)
    state = jnp.zeros_like(x) + jnp.asarray(neutral, x.dtype)

    def one(lap, state):
        return join(state, lax.dynamic_index_in_dim(gathered, lap, 0, False).astype(x.dtype))

    return lax.fori_loop(0, place, one, state)


def from_behind(block, axis, distance):
    devices = range(lax.axis_size(axis))
    route = [(i - distance, i) for i in devices if i - distance in devices]
    return lax.ppermute(block, axis, route)


def normalize(value):
    return value * lax.rsqrt(jnp.mean(value * value, axis=-1, keepdims=True) + 1e-06)


MESH = pl.DeviceIdType.MESH
VMEM_BYTES = 62 * 1024 * 1024
ADD_ROWS = 16
PIECES = 2
DOT_COLUMNS = 512
HID_COLUMNS = 256
SPANS = ((32, 0), (32, 0), (32, 0), (32, 1))
OWN_LINE, OWN_OVER, OWN_ASIDE, LOAD, ROWS, CROSS = range(6)
COMPUTE, EXCHANGE, LINE, FINISH, BESIDE = range(6, 11)
STEPS = (
    (
        (OWN_LINE, 1), (OWN_OVER, 0), (OWN_OVER, 1), (OWN_LINE, 2), (LOAD,), (OWN_ASIDE,), (OWN_OVER, 3),
        (OWN_LINE, 0), (ROWS, 1, 0), (OWN_LINE, 3), (ROWS, 1, 2), (OWN_OVER, 2), (CROSS, 0, 3), (COMPUTE, 0, 0),
        (ROWS, 1, 3), (ROWS, 3, 1), (CROSS, 1, 2), (ROWS, 1, 1), (COMPUTE, 1, 0), (CROSS, 1, 0), (ROWS, 3, 2),
        (CROSS, 1, 1), (CROSS, 3, 1), (CROSS, 1, 3), (CROSS, 0, 0), (ROWS, 3, 0), (CROSS, 3, 2), (ROWS, 2, 2),
        (CROSS, 0, 2), (COMPUTE, 1, 1), (LINE, 0, 1, 3, 0), (CROSS, 3, 3), (CROSS, 3, 0), (EXCHANGE, 1, 2),
        (ROWS, 3, 3), (LINE, 0, 1, 3, 1), (COMPUTE, 3, 1), (ROWS, 2, 0), (LINE, 0, 1, 2, 0), (ROWS, 2, 1),
        (COMPUTE, 3, 0), (LINE, 0, 3, 3, 1), (EXCHANGE, 3, 1), (EXCHANGE, 3, 2), (CROSS, 2, 3), (EXCHANGE, 3, 0),
        (ROWS, 2, 3), (EXCHANGE, 1, 0), (CROSS, 2, 0), (CROSS, 2, 2), (CROSS, 2, 1), (LINE, 0, 3, 3, 0),
        (COMPUTE, 2, 0), (LINE, 0, 3, 1, 0), (EXCHANGE, 1, 1), (LINE, 0, 3, 2, 0), (COMPUTE, 2, 1),
        (LINE, 0, 2, 3, 0), (CROSS, 0, 1), (EXCHANGE, 2, 0), (EXCHANGE, 2, 1), (LINE, 0, 3, 0, 0), (LINE, 0, 2, 3, 1),
        (EXCHANGE, 2, 2), (COMPUTE, 0, 1), (LINE, 0, 2, 0, 0), (EXCHANGE, 0, 1), (EXCHANGE, 0, 0), (LINE, 0, 2, 1, 0),
        (LINE, 0, 2, 2, 0), (LINE, 0, 1, 1, 0), (EXCHANGE, 0, 2), (FINISH, 3, 1), (LINE, 0, 1, 0, 0), (FINISH, 2, 0),
        (FINISH, 1, 0), (FINISH, 0, 0), (FINISH, 3, 0),
    ),
    (
        (OWN_ASIDE,), (OWN_LINE, 0), (OWN_OVER, 3), (OWN_OVER, 0), (OWN_LINE, 2), (ROWS, 0, 1), (OWN_LINE, 3),
        (ROWS, 0, 2), (OWN_LINE, 1), (ROWS, 3, 1), (ROWS, 2, 2), (ROWS, 0, 0), (LOAD,), (CROSS, 0, 3), (ROWS, 0, 3),
        (ROWS, 3, 2), (CROSS, 1, 3), (COMPUTE, 1, 0), (ROWS, 3, 0), (OWN_OVER, 1), (CROSS, 0, 2), (CROSS, 0, 1),
        (CROSS, 0, 0), (COMPUTE, 0, 0), (CROSS, 1, 0), (CROSS, 3, 3), (ROWS, 3, 3), (ROWS, 2, 0), (CROSS, 3, 2),
        (ROWS, 2, 1), (CROSS, 3, 0), (COMPUTE, 0, 1), (OWN_OVER, 2), (CROSS, 2, 3), (CROSS, 3, 1), (CROSS, 2, 2),
        (COMPUTE, 3, 0), (EXCHANGE, 0, 0), (CROSS, 2, 1), (EXCHANGE, 0, 2), (ROWS, 2, 3), (CROSS, 2, 0),
        (COMPUTE, 3, 1), (CROSS, 1, 1), (COMPUTE, 2, 1), (EXCHANGE, 0, 1), (CROSS, 1, 2), (COMPUTE, 2, 0),
        (LINE, 0, 3, 3, 1), (EXCHANGE, 3, 1), (EXCHANGE, 3, 2), (LINE, 0, 3, 3, 0), (COMPUTE, 1, 1), (EXCHANGE, 3, 0),
        (LINE, 0, 3, 1, 0), (LINE, 0, 3, 2, 0), (EXCHANGE, 2, 1), (LINE, 0, 2, 3, 0), (LINE, 1, 0, 3, 1),
        (EXCHANGE, 2, 2), (EXCHANGE, 2, 0), (LINE, 1, 0, 2, 0), (EXCHANGE, 1, 2), (LINE, 0, 3, 0, 0),
        (LINE, 1, 0, 1, 0), (LINE, 0, 2, 3, 1), (LINE, 1, 0, 3, 0), (LINE, 1, 0, 0, 0), (LINE, 0, 2, 0, 0),
        (EXCHANGE, 1, 1), (FINISH, 3, 1), (LINE, 0, 2, 1, 0), (EXCHANGE, 1, 0), (LINE, 0, 2, 2, 0), (FINISH, 1, 0),
        (FINISH, 3, 0), (FINISH, 2, 0), (FINISH, 0, 0),
    ),
)


def place(count):
    z = lax.axis_index("heads")
    c = lax.axis_index("ctx")
    beside = c + 1 - 2 * lax.rem(c, 2)
    across = lax.rem(c + 2, 4)
    diagonal = lax.rem(beside + 2, 4)
    return z, c, beside, across, diagonal


def nearest(count, z, index):
    index = count - 1 - index
    more = jnp.maximum(z, count - 1 - z)
    fewer = count - 1 - more
    alone = more - fewer
    paired = jnp.maximum(index - alone, 0)
    up = jnp.where(z + more < count, more - index, index - more)
    both = (fewer - paired // 2) * (1 - 2 * (paired % 2))
    offset = jnp.where(index < alone, up, both)
    return z + jnp.where(index < count - 1, offset, 0)


def attend_kernel(
    count, tokens_ref, share_hbm, table_ref, state_ref, past_hbm, qkv_hbm,
    hidden_ref, normed_ref, tables_ref,
    slab_ref, qkv_ref, w_ref, query_ref, kv_ref, before_ref, inside_ref, linear_ref,
    state_out, states_in, heads_out, heads_in,
    local_sem, token_send, token_recv, share_send, share_recv,
    tail_send, tail_recv, state_send, state_recv, head_send, head_recv,
):
    z, c, beside, across, diagonal = place(count)
    row_count, width = tokens_ref.shape
    slab_rows = count * row_count
    share = w_ref.shape[0] // (4 * count)

    def rows_of(index, size):
        return pl.ds(pl.multiple_of(index * size, size), size)

    def share_block(kind, zz, cc):
        if kind == 0:
            return w_ref.at[rows_of(zz * 4 + cc, share), :]
        return tables_ref.at[cc * count + zz]

    def share_source(kind):
        return table_ref if kind else share_hbm.at[rows_of(c, share), :]

    local = [
        pltpu.make_async_copy(source, target, local_sem.at[index])
        for index, (source, target) in enumerate(
            [(qkv_hbm.at[one], qkv_ref.at[:, one * HDIM : (one + 1) * HDIM]) for one in range(3)]
            + [(tokens_ref, slab_ref.at[z])]
            + [(share_source(kind), share_block(kind, z, c)) for kind in (0, 1)]
        )
    ]
    past_copy = pltpu.make_async_copy(past_hbm, before_ref, local_sem.at[6])
    for copy in local:
        copy.start()

    @pl.when(c == 0)
    def _():
        past_copy.start()

    barrier = pltpu.get_barrier_semaphore()
    for target in (beside, across, diagonal):
        pl.semaphore_signal(barrier, inc=1, device_id={"ctx": target}, device_id_type=MESH)
    for zz in range(count):

        @pl.when(zz != z)
        def _():
            pl.semaphore_signal(barrier, inc=1, device_id={"heads": zz}, device_id_type=MESH)

    pl.semaphore_wait(barrier, 3 + count - 1)

    def remote(source, target, send, recv, device):
        return pltpu.make_async_remote_copy(
            src_ref=source, dst_ref=target, send_sem=send, recv_sem=recv,
            device_id=device, device_id_type=MESH,
        )

    def started(copy):
        copy.start()

    def left(copy):
        copy.wait_send()

    def along(act, zz, copy):
        @pl.when(jnp.logical_and(zz >= z, z > 0))
        def _():
            act(copy(0, {"heads": z - 1}))

        @pl.when(jnp.logical_and(zz <= z, z < count - 1))
        def _():
            act(copy(1, {"heads": z + 1}))

    def token_copy(zz, piece, own=False):
        rows = pl.ds(piece * row_count // PIECES, row_count // PIECES)

        def copy(way, device):
            block = slab_ref.at[zz, rows, :]
            source = tokens_ref.at[rows, :] if own else block
            return remote(
                source, block, token_send.at[way, piece, zz], token_recv.at[piece, zz], device
            )

        return copy

    def share_copy(kind, zz, cc, own=False):
        def copy(way, device):
            block = share_block(kind, zz, cc)
            slot = zz * 4 + cc
            source = share_source(kind) if own else block
            return remote(
                source, block, share_send.at[kind, way, slot], share_recv.at[kind, slot], device
            )

        return copy

    def aside(act, zz, cc, own=False):
        for kind in (0, 1):
            act(share_copy(kind, zz, cc, own)(3, {"ctx": beside}))

    def share_relay(act, zz, own=False):
        for kind in (0, 1):
            act(share_copy(kind, zz, c, own)(2, {"ctx": across}))
        aside(act, zz, c, own)

    def share_along(act, zz, own=False):
        for kind in (0, 1):
            along(act, zz, share_copy(kind, zz, c, own))

    def share_received(zz, cc):
        for kind in (0, 1):
            share_copy(kind, zz, cc)(3, {"ctx": beside}).wait_recv()

    def at_distance(distance, act):
        @pl.when(z >= distance)
        def _():
            act(z - distance)

        @pl.when(z + distance < count)
        def _():
            act(z + distance)

    def share_onward(zz):
        share_received(zz, c)
        share_along(started, zz)
        share_relay(started, zz)

    def share_over(zz):
        share_received(zz, across)
        aside(started, zz, across)

    for piece in range(PIECES):
        along(started, z, token_copy(z, piece, True))
    share_relay(started, z, True)
    for copy in local:
        copy.wait()

    def project(zz):
        product = jnp.dot(slab_ref[zz], qkv_ref[...], preferred_element_type=jnp.float32)
        product = product.astype(query_ref.dtype)
        rows = rows_of(zz, row_count)
        query_ref[rows, :] = product[:, :HDIM]
        kv_ref[0, rows, :] = product[:, HDIM : 2 * HDIM]
        kv_ref[1, rows, :] = product[:, 2 * HDIM :]

        @pl.when(c < 3)
        def _():
            tail_copy(zz).start()

    def tail_copy(zz):
        rows = rows_of(zz, row_count)
        return remote(
            kv_ref.at[:, rows, :], before_ref.at[:, rows, :], tail_send.at[zz], tail_recv.at[zz],
            {"ctx": jnp.minimum(c + 1, 3)},
        )

    def token_relay(zz, piece):
        token_copy(zz, piece)(0, {"heads": z - 1}).wait_recv()
        along(started, zz, token_copy(zz, piece))

    def step(index, _):
        zz = nearest(count, z, index)
        last = nearest(count, z, jnp.maximum(index - 1, 0))
        after = nearest(count, z, jnp.minimum(index + 1, count - 1))
        opens = jnp.logical_and(index > 0, jnp.abs(zz - z) != jnp.abs(last - z))
        double = jnp.logical_and(index < count - 1, jnp.abs(after - z) == jnp.abs(zz - z))

        for piece in range(PIECES):

            @pl.when(opens)
            def _():
                token_relay(zz, piece)

            @pl.when(jnp.logical_and(opens, double))
            def _():
                token_relay(after, piece)

        project(zz)
        alone = jnp.logical_and(index > 0, jnp.logical_not(jnp.logical_and(opens, double)))
        distance = jnp.abs(zz - z)

        @pl.when(jnp.logical_and(alone, distance == 1))
        def _():
            share_along(started, z, True)

        @pl.when(jnp.logical_and(alone, distance > 1))
        def _():
            at_distance(distance - 1, share_onward)

        return 0

    lax.fori_loop(0, count, step, 0)

    local_state = lax.dot_general(
        kv_ref[0], kv_ref[1], (((0,), (0,)), ((), ())), preferred_element_type=jnp.float32
    )
    state_out[...] = local_state.astype(state_out.dtype)
    others = [beside, across, diagonal]
    state_copies = [
        remote(state_out, states_in.at[c], state_send.at[way], state_recv.at[c], {"ctx": target})
        for way, target in enumerate(others)
    ]
    for copy in state_copies:
        copy.start()
    share_over(z)

    blocks = slab_rows // row_count
    for block in range(blocks):
        first, end = block * row_count, (block + 1) * row_count
        query = query_ref[first:end, :]
        scores = lax.dot_general(
            query, kv_ref[0, :end, :], (((1,), (1,)), ((), ())), preferred_element_type=jnp.float32
        )
        shape = scores.shape
        causal = lax.broadcasted_iota(jnp.int32, shape, 1) <= first + lax.broadcasted_iota(
            jnp.int32, shape, 0
        )
        inside_ref[first:end, :end] = scores
        weights = jnp.where(causal, scores, 0.0).astype(kv_ref.dtype)
        linear_ref[first:end, :] = jnp.dot(
            weights, kv_ref[1, :end, :], preferred_element_type=jnp.float32
        )

    for target in others:
        remote(
            state_out, states_in.at[target], state_send.at[0], state_recv.at[target],
            {"ctx": beside},
        ).wait_recv()
    start = state_ref[...]
    for cc in range(4):
        start = start + jnp.where(cc < c, states_in[cc].astype(jnp.float32), 0.0)

    @pl.when(c == 0)
    def _():
        past_copy.wait()

    @pl.when(c > 0)
    def _():
        for zz in range(count):
            tail_copy(zz).wait_recv()

    scale = 1.0 / math.sqrt(HDIM)

    def head_copy(zz):
        columns = pl.ds(pl.multiple_of(z * HDIM, HDIM), HDIM)
        return remote(
            heads_out.at[zz], heads_in.at[:, columns], head_send.at[zz], head_recv.at[z],
            {"heads": zz},
        )

    for block in range(blocks):
        first, end = block * row_count, (block + 1) * row_count
        query = query_ref[first:end, :]
        old = lax.dot_general(
            query, before_ref[0, first:, :], (((1,), (1,)), ((), ())),
            preferred_element_type=jnp.float32,
        )
        old_seen = lax.broadcasted_iota(jnp.int32, old.shape, 1) > lax.broadcasted_iota(
            jnp.int32, old.shape, 0
        )
        old = jnp.where(old_seen, old * scale, -jnp.inf)
        new = inside_ref[first:end, :end]
        new_seen = lax.broadcasted_iota(jnp.int32, new.shape, 1) <= first + lax.broadcasted_iota(
            jnp.int32, new.shape, 0
        )
        new = jnp.where(new_seen, new * scale, -jnp.inf)
        top = jnp.maximum(
            jnp.max(old, axis=-1, keepdims=True), jnp.max(new, axis=-1, keepdims=True)
        )
        old = jnp.exp(old - top)
        new = jnp.exp(new - top)
        inverse = 1.0 / (
            jnp.sum(old, axis=-1, keepdims=True) + jnp.sum(new, axis=-1, keepdims=True)
        )
        window = jnp.dot(
            (old * inverse).astype(kv_ref.dtype), before_ref[1, first:, :],
            preferred_element_type=jnp.float32,
        ) + jnp.dot(
            (new * inverse).astype(kv_ref.dtype), kv_ref[1, :end, :],
            preferred_element_type=jnp.float32,
        )
        linear = linear_ref[first:end, :] + jnp.dot(
            query.astype(jnp.float32), start, precision=lax.Precision.HIGHEST,
            preferred_element_type=jnp.float32,
        )
        heads_out[block] = (normalize(linear) + window).astype(heads_out.dtype)

        @pl.when(block != z)
        def _():
            head_copy(block).start()

        @pl.when(block == z)
        def _():
            columns = pl.ds(pl.multiple_of(z * HDIM, HDIM), HDIM)
            heads_in[:, columns] = heads_out[block]

        if block == 0:
            at_distance(jnp.maximum(z, count - 1 - z), share_onward)
        if block + 1 < count:
            at_distance(block + 1, share_over)

    for zz in range(count):
        share_received(zz, beside)
        share_received(zz, diagonal)

        @pl.when(zz != z)
        def _():
            remote(
                heads_out.at[zz], heads_in.at[:, zz * HDIM : (zz + 1) * HDIM], head_send.at[zz],
                head_recv.at[zz], {"heads": zz},
            ).wait_recv()

    def out_tile(index, total):
        columns = pl.ds(pl.multiple_of(index * DOT_COLUMNS, DOT_COLUMNS), DOT_COLUMNS)
        attn = jnp.dot(heads_in[...], w_ref[:, columns], preferred_element_type=jnp.float32)
        hidden = (tokens_ref[:, columns].astype(jnp.float32) + attn).astype(hidden_ref.dtype)
        hidden_ref[:, columns] = hidden
        hidden = hidden.astype(jnp.float32)
        return total + jnp.sum(hidden * hidden, axis=-1, keepdims=True)

    total = lax.fori_loop(
        0, width // DOT_COLUMNS, out_tile, jnp.zeros((row_count, 1), jnp.float32)
    )
    inverse = lax.rsqrt(total / width + 1e-06)
    for first in range(0, width, DOT_COLUMNS):
        hidden = hidden_ref[:, first : first + DOT_COLUMNS].astype(jnp.float32)
        normed_ref[:, first : first + DOT_COLUMNS] = (hidden * inverse).astype(normed_ref.dtype)

    for piece in range(PIECES):
        along(left, z, token_copy(z, piece, True))
    share_along(left, z, True)
    share_relay(left, z, True)

    @pl.when(c < 3)
    def _():
        for zz in range(count):
            tail_copy(zz).wait_send()

    for copy in state_copies:
        copy.wait_send()
    for zz in range(count):
        aside(left, zz, across)

        @pl.when(zz != z)
        def _():
            for piece in range(PIECES):
                along(left, zz, token_copy(zz, piece))
            share_along(left, zz)
            share_relay(left, zz)
            head_copy(zz).wait_send()


def plain_steps(count, at):
    spans = range(len(SPANS))
    steps = [(OWN_LINE, span) for span in spans] + [(OWN_OVER, span) for span in spans]
    steps += [(OWN_ASIDE,), (LOAD,)]
    for distance in range(count):
        planes = sorted({at - distance, at + distance} & set(range(count)))
        for op in (ROWS, CROSS):
            if op == CROSS or distance:
                steps += [(op, zz, span) for zz in planes for span in reversed(spans)]
        steps += [(COMPUTE, zz, pair) for zz in planes for pair in (0, 1)]
    near = [span for span in spans if not SPANS[span][1]]
    far = [span for span in spans if SPANS[span][1]]
    steps += [(EXCHANGE, zz, span) for zz in range(count) for span in near]
    for key in range(1, count):
        links = [(0, key)] * (key > at) + [(1, count - 1 - key)] * (count - 1 - key < at)
        for link in links if at < count - 1 - at else reversed(links):
            steps += [(LINE, *link, span, 0) for span in spans]
            steps += [(LINE, *link, span, 1) for span in far]
    return steps + [(FINISH, span, 1) for span in far] + [(FINISH, span, 0) for span in spans]


def mirrored(step, count):
    op, *where = step
    if op in (ROWS, CROSS, EXCHANGE, COMPUTE):
        return (op, count - 1 - where[0], where[1])
    if op == LINE:
        return (op, 1 - where[0], count - 1 - where[1], *where[2:])
    return step


def steps_of(count, at):
    if count != len(STEPS) * 2:
        return plain_steps(count, at)
    if at < len(STEPS):
        return list(STEPS[at])
    return [mirrored(step, count) for step in STEPS[count - 1 - at]]


def span_rows(row_count):
    spans, first = [], 0
    for share, far in SPANS:
        spans.append((first, row_count * share // 128, far))
        first += row_count * share // 128
    return spans, sum(size for _, size, far in spans if far)


def expert_kernel(
    count, weight_copies, hidden_ref, own_ref, table_ref, out_ref,
    rows_ref, part_ref, hid_ref, scale_ref, gate_ref, up_ref, down_ref,
    from_beside, to_across, from_across, line_out, line_in, last_out, last_in,
    local_sem, row_send, row_recv, beside_send, beside_recv, across_send, across_recv,
    line_send, line_recv, last_send, last_recv,
):
    z, c, beside, across, diagonal = place(count)
    row_count, width = own_ref.shape
    spans, far_rows = span_rows(row_count)
    near_rows = row_count - far_rows
    expert = c * count + z
    own_rows = pl.ds(pl.multiple_of(c * row_count, row_count), row_count)
    own_copy = pltpu.make_async_copy(own_ref, rows_ref.at[z, own_rows, :], local_sem)
    own_copy.start()
    local = weight_copies + [own_copy]

    def window(cc, span):
        first, size, _ = spans[span]
        return pl.ds(pl.multiple_of(cc * row_count + first, 16), size)

    def row_copy(zz, cc, span, way, target, own=False):
        first, size, _ = spans[span]
        slot = zz * 4 + cc
        block = rows_ref.at[zz, window(cc, span), :]
        return pltpu.make_async_remote_copy(
            src_ref=own_ref.at[pl.ds(first, size), :] if own else block,
            dst_ref=block,
            send_sem=row_send.at[way, span, slot],
            recv_sem=row_recv.at[span, slot],
            device_id=target,
            device_id_type=MESH,
        )

    def started(copy):
        copy.start()

    def left(copy):
        copy.wait_send()

    def received(zz, cc, span):
        row_copy(zz, cc, span, 0, {"ctx": beside}).wait_recv()

    def along(act, at, zz, cc, span, own=False):
        if zz >= at and at > 0:
            act(row_copy(zz, cc, span, 0, {"heads": at - 1}, own))
        if zz <= at and at < count - 1:
            act(row_copy(zz, cc, span, 1, {"heads": at + 1}, own))

    def over(act, zz, cc, span, own=False):
        act(row_copy(zz, cc, span, 2, {"ctx": across}, own))

    def aside(act, zz, cc, span, own=False):
        act(row_copy(zz, cc, span, 3, {"ctx": beside}, own))

    def relays(op, at, zz, span, act, wait):
        cc = c if op == ROWS else across
        far = spans[span][2]
        if wait:
            received(zz, cc, span)
        if op == ROWS or far:
            along(act, at, zz, cc, span)
        if op == ROWS and not far:
            over(act, zz, cc, span)
        aside(act, zz, cc, span)

    def paired(zz, pair):
        for span in range(len(spans)):
            received(zz, diagonal if pair else beside, span)

    def compute(zz, pair):
        half = jnp.where(pair == 0, c // 2, 1 - c // 2)
        for core in range(2):
            row = table_ref[(half * 2 + core) * count + zz, pl.ds(expert, 1), :]
            scale_ref[core * row_count : (core + 1) * row_count, :] = jnp.broadcast_to(
                row, (HDIM, row_count)
            ).T

        inner = gate_ref.shape[1]
        rows = pl.ds(pl.multiple_of(half * 2 * row_count, 2 * row_count), 2 * row_count)

        def hidden_tile(index, _):
            columns = pl.ds(pl.multiple_of(index * HID_COLUMNS, HID_COLUMNS), HID_COLUMNS)
            block = rows_ref[zz, rows, :]
            gate = jnp.dot(block, gate_ref[:, columns], preferred_element_type=jnp.float32)
            up = jnp.dot(block, up_ref[:, columns], preferred_element_type=jnp.float32)
            scale = jnp.concatenate([scale_ref[...]] * (HID_COLUMNS // HDIM), axis=1)
            hid_ref[:, columns] = (jax.nn.silu(gate) * up * scale).astype(hid_ref.dtype)
            return 0

        lax.fori_loop(0, inner // HID_COLUMNS, hidden_tile, 0)

        def out_tile(index, _):
            columns = pl.ds(pl.multiple_of(index * DOT_COLUMNS, DOT_COLUMNS), DOT_COLUMNS)
            product = jnp.dot(
                hid_ref[...], down_ref[:, columns], preferred_element_type=jnp.float32
            )
            part_ref[zz, rows, columns] = product.astype(part_ref.dtype)
            return 0

        lax.fori_loop(0, width // DOT_COLUMNS, out_tile, 0)

    def beside_copy(kind, zz):
        cc = diagonal if kind == 0 else beside
        return pltpu.make_async_remote_copy(
            src_ref=part_ref.at[zz, pl.ds(pl.multiple_of(cc * row_count, row_count), row_count), :],
            dst_ref=from_beside.at[kind, zz],
            send_sem=beside_send.at[kind, zz],
            recv_sem=beside_recv.at[kind, zz],
            device_id={"ctx": beside},
            device_id_type=MESH,
        )

    def across_copy(zz, span):
        first, size, _ = spans[span]
        return pltpu.make_async_remote_copy(
            src_ref=to_across.at[zz, pl.ds(first, size), :],
            dst_ref=from_across.at[zz, pl.ds(first, size), :],
            send_sem=across_send.at[span, zz],
            recv_sem=across_recv.at[span, zz],
            device_id={"ctx": across},
            device_id_type=MESH,
        )

    def line_rows(span, other):
        first, size, _ = spans[span]
        return pl.ds(row_count + first - near_rows if other else first, size)

    def line_copy(side, zz, span, other):
        return pltpu.make_async_remote_copy(
            src_ref=line_out.at[zz, line_rows(span, other), :],
            dst_ref=line_in.at[side, zz, line_rows(span, other), :],
            send_sem=line_send.at[2 * span + other, zz],
            recv_sem=line_recv.at[2 * span + other, side, zz],
            device_id={"heads": z + 1 - 2 * side},
            device_id_type=MESH,
        )

    def last_rows(span):
        first, size, _ = spans[span]
        return pl.ds(first - near_rows, size)

    def last_copy(span):
        return pltpu.make_async_remote_copy(
            src_ref=last_out.at[last_rows(span), :],
            dst_ref=last_in.at[last_rows(span), :],
            send_sem=last_send.at[span],
            recv_sem=last_recv.at[span],
            device_id={"ctx": across},
            device_id_type=MESH,
        )

    def add(target, sources):
        def chunk(index, _):
            rows = pl.ds(pl.multiple_of(index * ADD_ROWS, ADD_ROWS), ADD_ROWS)
            total = sources[0][rows, :].astype(jnp.float32)
            for source in sources[1:]:
                total = total + source[rows, :].astype(jnp.float32)
            target[rows, :] = total.astype(target.dtype)
            return 0

        lax.fori_loop(0, target.shape[0] // ADD_ROWS, chunk, 0)

    def starts(side, at):
        return at == side * (count - 1)

    def chip_sources(zz, span, other):
        first, size, far = spans[span]
        start = pl.multiple_of((across if other else c) * row_count + first, 16)
        sources = [
            part_ref.at[zz, pl.ds(start, size), :],
            from_beside.at[1 - other, zz, pl.ds(first, size), :],
        ]
        if not far and not other:
            sources.append(from_across.at[zz, pl.ds(first, size), :])
        return sources

    def perform(at, steps, waited):
        waited = set(waited)

        def once(kind, zz):
            if (kind, zz) not in waited:
                waited.add((kind, zz))
                beside_copy(kind, zz).wait_recv()

        def arrived(zz, span, other, sides):
            once(1 - other, zz)
            if not spans[span][2]:
                across_copy(zz, span).wait_recv()
            sources = chip_sources(zz, span, other)
            for side in sides:
                if not starts(side, at):
                    line_copy(side, zz, span, other).wait_recv()
                    sources.append(line_in.at[side, zz, line_rows(span, other), :])
            return sources

        for op, *where in steps:
            if op == OWN_LINE:
                along(started, at, at, c, where[0], True)
            elif op == OWN_OVER:
                over(started, at, c, where[0], True)
            elif op == OWN_ASIDE:
                for span in range(len(spans)):
                    aside(started, at, c, span, True)
            elif op == LOAD:
                for copy in local:
                    copy.wait()
            elif op == COMPUTE:
                paired(*where)
            elif op == BESIDE:
                beside_copy(where[1], where[0]).start()
            elif op == EXCHANGE:
                zz, span = where
                once(0, zz)
                first, size, _ = spans[span]
                start = pl.multiple_of(across * row_count + first, 16)
                add(
                    to_across.at[zz, pl.ds(first, size), :],
                    [
                        part_ref.at[zz, pl.ds(start, size), :],
                        from_beside.at[0, zz, pl.ds(first, size), :],
                    ],
                )
                across_copy(zz, span).start()
            elif op == LINE:
                side, zz, span, other = where
                add(line_out.at[zz, line_rows(span, other), :], arrived(zz, span, other, (side,)))
                line_copy(side, zz, span, other).start()
            elif op == FINISH and where[1]:
                span = where[0]
                add(last_out.at[last_rows(span), :], arrived(at, span, 1, (0, 1)))
                last_copy(span).start()
            elif op == FINISH:
                span = where[0]
                first, size, far = spans[span]
                rows = pl.ds(first, size)
                sources = arrived(at, span, 0, (0, 1))
                if far:
                    last_copy(span).wait_recv()
                    sources.append(last_in.at[last_rows(span), :])
                add(out_ref.at[rows, :], [hidden_ref.at[rows, :]] + sources)
            else:
                relays(op, at, *where, started, True)

    def each_place(act):
        for at in range(count):

            @pl.when(z == at)
            def _():
                act(at)

    units = 2 * count
    segments, orders = [], []
    for at in range(count):
        parts, order = [[]], []
        for one in steps_of(count, at):
            parts[-1].append(one)
            if one[0] == COMPUTE:
                zz, pair = one[1:]
                order.append((zz, pair))
                parts.append([(BESIDE, zz, 1 - pair)])
        segments.append(parts)
        orders.append(order)

    def waits_of(at, unit):
        keys = set()
        for op, *where in sum(segments[at][:unit], []):
            if op == EXCHANGE:
                keys.add((0, where[0]))
            elif op == LINE:
                keys.add((1 - where[3], where[1]))
            elif op == FINISH:
                keys.add((1 - where[1], at))
        return keys

    def choose(index, pick):
        value = jnp.int32(0)
        for at in range(count):
            for unit in range(units):
                here = jnp.logical_and(z == at, index == unit)
                value = jnp.where(here, pick(orders[at][unit]), value)
        return value

    def step(index, _):
        def segment(at):
            for unit in range(units):

                @pl.when(index == unit)
                def _():
                    perform(at, segments[at][unit], waits_of(at, unit))

        each_place(segment)
        compute(choose(index, lambda unit: unit[0]), choose(index, lambda unit: unit[1]))
        return 0

    lax.fori_loop(0, units, step, 0)

    def finish(at):
        perform(at, segments[at][units], waits_of(at, units))
        for span, (_, _, far) in enumerate(spans):
            if far:
                last_copy(span).wait_send()
            along(left, at, at, c, span, True)
            over(left, at, c, span, True)
            aside(left, at, c, span, True)
            for zz in range(count):
                relays(CROSS, at, zz, span, left, False)
                if not far:
                    across_copy(zz, span).wait_send()
                if zz != at:
                    relays(ROWS, at, zz, span, left, False)
                    for other in range(1 + far):
                        line_copy(int(zz < at), zz, span, other).wait_send()
        for zz in range(count):
            beside_copy(0, zz).wait_send()
            beside_copy(1, zz).wait_send()

    each_place(finish)


def layer_kernel(
    count, front_size, tokens_ref, share_hbm, table_ref, state_ref, past_hbm, qkv_hbm,
    gate_hbm, up_hbm, down_hbm, out_ref, hidden_ref, normed_ref, tables_ref, weight_sem, *scratch
):
    front, back = scratch[:front_size], scratch[front_size:]
    weight_copies = [
        pltpu.make_async_copy(source, target, weight_sem.at[index])
        for index, (source, target) in enumerate(zip((gate_hbm, up_hbm, down_hbm), back[4:7]))
    ]
    for copy in weight_copies:
        copy.start()
    attend_kernel(
        count, tokens_ref, share_hbm, table_ref, state_ref, past_hbm, qkv_hbm,
        hidden_ref, normed_ref, tables_ref, *front,
    )
    expert_kernel(count, weight_copies, hidden_ref, normed_ref, tables_ref, out_ref, *back)


def run_layer(tokens, w_out, table, state_in, past_kv, w_qkv, w_gate, w_up, w_down):
    count = lax.axis_size("heads")
    row_count, width = tokens.shape
    slab_rows = count * row_count
    inner = w_gate.shape[1]
    kind = tokens.dtype
    slots = 4 * count
    far_rows = span_rows(row_count)[1]
    near_rows = row_count - far_rows
    cuts = len(SPANS)
    dma = pltpu.SemaphoreType.DMA
    vmem, anywhere = pl.BlockSpec(memory_space=pltpu.VMEM), pl.BlockSpec(memory_space=pl.ANY)
    shared = [
        pltpu.VMEM((row_count, width), kind),
        pltpu.VMEM((row_count, width), kind),
        pltpu.VMEM((slots,) + table.shape, table.dtype),
        dma((3,)),
    ]
    front = [
        pltpu.VMEM((count, row_count, width), kind),
        pltpu.VMEM((width, 3 * HDIM), kind),
        pltpu.VMEM((count * HDIM, width), kind),
        pltpu.VMEM((slab_rows, HDIM), kind),
        pltpu.VMEM((2, slab_rows, HDIM), kind),
        pltpu.VMEM((2, WINDOW, HDIM), kind),
        pltpu.VMEM((slab_rows, slab_rows), jnp.float32),
        pltpu.VMEM((slab_rows, HDIM), jnp.float32),
        pltpu.VMEM((HDIM, HDIM), kind),
        pltpu.VMEM((4, HDIM, HDIM), kind),
        pltpu.VMEM((count, row_count, HDIM), kind),
        pltpu.VMEM((row_count, count * HDIM), kind),
        dma((7,)),
        dma((2, PIECES, count)),
        dma((PIECES, count)),
        dma((2, 4, slots)),
        dma((2, slots)),
        dma((count,)),
        dma((count,)),
        dma((3,)),
        dma((4,)),
        dma((count,)),
        dma((count,)),
    ]
    back = [
        pltpu.VMEM((count, 4 * row_count, width), kind),
        pltpu.VMEM((count, 4 * row_count, width), kind),
        pltpu.VMEM((2 * row_count, inner), kind),
        pltpu.VMEM((2 * row_count, HDIM), jnp.float32),
        pltpu.VMEM(w_gate.shape, kind),
        pltpu.VMEM(w_up.shape, kind),
        pltpu.VMEM(w_down.shape, kind),
        pltpu.VMEM((2, count, row_count, width), kind),
        pltpu.VMEM((count, near_rows, width), kind),
        pltpu.VMEM((count, near_rows, width), kind),
        pltpu.VMEM((count, row_count + far_rows, width), kind),
        pltpu.VMEM((2, count, row_count + far_rows, width), kind),
        pltpu.VMEM((far_rows, width), kind),
        pltpu.VMEM((far_rows, width), kind),
        dma(()),
        dma((4, cuts, 4 * count)),
        dma((cuts, 4 * count)),
        dma((2, count)),
        dma((2, count)),
        dma((cuts, count)),
        dma((cuts, count)),
        dma((2 * cuts, count)),
        dma((2 * cuts, 2, count)),
        dma((cuts,)),
        dma((cuts,)),
    ]
    return pl.pallas_call(
        functools.partial(layer_kernel, count, len(front)),
        out_shape=jax.ShapeDtypeStruct((row_count, width), kind),
        in_specs=[vmem, anywhere, vmem, vmem] + [anywhere] * 5,
        out_specs=vmem,
        scratch_shapes=shared + front + back,
        compiler_params=pltpu.CompilerParams(
            collective_id=0, has_side_effects=True, vmem_limit_bytes=VMEM_BYTES
        ),
        name="run_layer",
    )(tokens, w_out, table, state_in, past_kv, w_qkv, w_gate, w_up, w_down)


def expert_table(expert_ids, gate_weights, expert_count):
    chosen = expert_ids[:, :, None] == jnp.arange(expert_count, dtype=jnp.int32)
    return jnp.sum(jnp.where(chosen, gate_weights[:, :, None], 0.0), axis=1).T


def on_device(
    tokens, state_in, past_kv, w_qkv, w_out, w_gate, w_up, w_down, expert_ids, gate_weights
):
    row_count, model_width = tokens.shape
    inner_width = w_qkv.shape[2]
    local_heads = inner_width // HDIM
    ctx_count = lax.axis_size("ctx")
    head_count = lax.axis_size("heads")
    exp_local = w_gate.shape[0]
    devices = ctx_count * head_count
    expert_count = exp_local * devices
    top_count = expert_ids.shape[1]
    capacity = max(2, 2 * row_count * top_count // expert_count)
    dense = (
        ctx_count == 4
        and exp_local == 1
        and row_count % HDIM == 0
        and local_heads == 1
        and head_count * row_count == WINDOW
        and w_gate.shape[2] % HID_COLUMNS == 0
        and row_count * devices <= expert_count * capacity
    )
    if dense:
        table = expert_table(expert_ids, gate_weights, expert_count)
        return run_layer(
            tokens, w_out, table, state_in[0], past_kv, jnp.transpose(w_qkv, (1, 0, 2)),
            w_gate[0], w_up[0], w_down[0],
        )
    slab, w_rows = [
        lax.all_gather(value, "heads", axis=0, tiled=True) for value in (tokens, w_out)
    ]
    projected = jnp.dot(
        slab,
        w_qkv.reshape(model_width, 3 * inner_width),
        preferred_element_type=jnp.float32,
    ).astype(jnp.bfloat16)
    slab_rows = projected.shape[0]
    projected = projected.reshape(slab_rows, 3, local_heads, HDIM)
    query = jnp.transpose(projected[:, 0], (1, 0, 2))
    keys = jnp.transpose(projected[:, 1], (1, 0, 2))
    values = jnp.transpose(projected[:, 2], (1, 0, 2))
    local_state = jnp.einsum("hsd,hse->hde", keys, values, preferred_element_type=jnp.float32)
    earlier_state = entering(
        local_state, "ctx", lambda first, second: first + second, jnp.zeros_like(local_state)
    )
    start_state = state_in + earlier_state
    tail = jnp.stack([keys, values], axis=0)
    arrived = from_behind(tail, "ctx", 1)
    past = jnp.transpose(past_kv.reshape(2, WINDOW, local_heads, HDIM), (0, 2, 1, 3))
    previous = jnp.where(lax.axis_index("ctx") == 0, past, arrived)
    all_keys = jnp.concatenate([previous[0], keys], axis=1)
    all_values = jnp.concatenate([previous[1], values], axis=1)
    block_rows = min(slab_rows, 512)
    block_count = slab_rows // block_rows
    scale = 1.0 / math.sqrt(HDIM)
    causal = jnp.arange(block_rows)[:, None] >= jnp.arange(block_rows)[None, :]
    offsets = jnp.arange(WINDOW + block_rows)[None, :] - jnp.arange(block_rows)[:, None]
    in_window = (offsets > 0) & (offsets <= WINDOW)

    def block_step(state, index):
        first = index * block_rows
        carried = jnp.einsum(
            "hsd,hde->hse", query.astype(jnp.float32), state, precision=lax.Precision.HIGHEST
        )
        inside = jnp.einsum("hsd,htd->hst", query, keys, preferred_element_type=jnp.float32)
        inside = jnp.where(causal[None], inside, 0.0).astype(jnp.bfloat16)
        linear = carried + jnp.einsum(
            "hst,hte->hse", inside, values, preferred_element_type=jnp.float32
        )
        scores = (
            jnp.einsum("hsd,htd->hst", query, all_keys, preferred_element_type=jnp.float32) * scale
        )
        scores = jnp.where(in_window[None], scores, -jnp.inf)
        top_score = jnp.max(scores, axis=-1, keepdims=True)
        expo = jnp.exp(scores - top_score)
        probs = (expo / jnp.sum(expo, axis=-1, keepdims=True)).astype(jnp.bfloat16)
        window_out = jnp.einsum(
            "hst,hte->hse", probs, all_values, preferred_element_type=jnp.float32
        )
        combined = (normalize(linear) + window_out).astype(jnp.bfloat16)
        new_state = state + jnp.einsum(
            "hsd,hse->hde", keys, values, preferred_element_type=jnp.float32
        )
        return (new_state, combined)

    _, outs = lax.scan(block_step, start_state, jnp.arange(block_count, dtype=jnp.int32))
    heads_out = jnp.transpose(outs, (0, 2, 1, 3)).reshape(slab_rows, inner_width)
    regrouped = lax.all_to_all(heads_out, "heads", split_axis=0, concat_axis=1, tiled=True)
    attn = jnp.dot(
        regrouped,
        w_rows,
        preferred_element_type=jnp.float32,
    )
    hidden_state = (tokens.astype(jnp.float32) + attn).astype(jnp.bfloat16)
    hidden_float = hidden_state.astype(jnp.float32)
    normed = normalize(hidden_float).astype(jnp.bfloat16)
    picks = expert_ids.reshape(-1)
    onehot = (picks[:, None] == jnp.arange(expert_count, dtype=jnp.int32)[None, :]).astype(
        jnp.int32
    )
    earlier = jnp.cumsum(onehot, axis=0) - onehot
    slots = jnp.sum(onehot * earlier, axis=1)
    destination = picks * capacity + slots
    source_rows = jnp.arange(row_count * top_count, dtype=jnp.int32) // top_count
    outgoing = jnp.zeros((expert_count * capacity, model_width), jnp.bfloat16)
    outgoing = outgoing.at[destination].set(normed[source_rows])
    sendable = outgoing.reshape(expert_count, 1, capacity, model_width)
    arrived_rows = lax.all_to_all(
        sendable, ("ctx", "heads"), split_axis=0, concat_axis=1, tiled=True
    )
    e_count, n_count, c_count, d_count = arrived_rows.shape
    flat = arrived_rows.reshape(e_count, n_count * c_count, d_count)
    gate_act = jnp.einsum("erd,edf->erf", flat, w_gate, preferred_element_type=jnp.float32)
    up_act = jnp.einsum("erd,edf->erf", flat, w_up, preferred_element_type=jnp.float32)
    hid = (jax.nn.silu(gate_act) * up_act).astype(jnp.bfloat16)
    out_rows = jnp.einsum("erf,efd->erd", hid, w_down, preferred_element_type=jnp.float32)
    finished = out_rows.astype(jnp.bfloat16).reshape(e_count, n_count, c_count, d_count)
    returned = lax.all_to_all(finished, ("ctx", "heads"), split_axis=1, concat_axis=0, tiled=True)
    returned = returned.reshape(expert_count * capacity, model_width)
    picked = returned[destination].reshape(row_count, top_count, model_width).astype(jnp.float32)
    routed = jnp.sum(gate_weights[:, :, None] * picked, axis=1)
    return (hidden_float + routed).astype(jnp.bfloat16)


def solution(mesh):
    return jax.shard_map(
        on_device,
        mesh=mesh,
        in_specs=(
            P(("groups", "ctx", "heads"), None),
            P("heads", "groups", None),
            P(None, "groups", "heads"),
            P(None, None, "heads"),
            P("heads", None),
            P(("ctx", "heads"), None, None),
            P(("ctx", "heads"), None, None),
            P(("ctx", "heads"), None, None),
            P(("groups", "ctx", "heads"), None),
            P(("groups", "ctx", "heads"), None),
        ),
        out_specs=P(("groups", "ctx", "heads"), None),
        check_vma=False,
    )
```

```python
import functools
import math

import jax
import jax.numpy as jnp
from jax import lax
from jax.experimental import pallas as pl
from jax.experimental.pallas import tpu as pltpu
from jax.sharding import PartitionSpec as P

HDIM = 128
WINDOW = 512


def entering(x, axis, join, neutral):
    place = lax.axis_index(axis)
    gathered = lax.all_gather(x.astype(jnp.bfloat16), axis)
    state = jnp.zeros_like(x) + jnp.asarray(neutral, x.dtype)

    def one(lap, state):
        return join(state, lax.dynamic_index_in_dim(gathered, lap, 0, False).astype(x.dtype))

    return lax.fori_loop(0, place, one, state)


def from_behind(block, axis, distance):
    devices = range(lax.axis_size(axis))
    route = [(i - distance, i) for i in devices if i - distance in devices]
    return lax.ppermute(block, axis, route)


def normalize(value):
    return value * lax.rsqrt(jnp.mean(value * value, axis=-1, keepdims=True) + 1e-06)


MESH = pl.DeviceIdType.MESH
VMEM_BYTES = 62 * 1024 * 1024
ADD_ROWS = 16
PIECES = 2
DOT_COLUMNS = 512
HID_COLUMNS = 256
SPANS = ((32, 0), (32, 0), (32, 0), (32, 1))
OWN_LINE, OWN_OVER, OWN_ASIDE, LOAD, ROWS, CROSS = range(6)
COMPUTE, EXCHANGE, LINE, FINISH, BESIDE = range(6, 11)
STEPS = (
    (
        (OWN_LINE, 1), (OWN_OVER, 0), (OWN_OVER, 1), (OWN_LINE, 2), (LOAD,), (OWN_ASIDE,), (OWN_OVER, 3),
        (OWN_LINE, 0), (ROWS, 1, 0), (OWN_LINE, 3), (ROWS, 1, 2), (OWN_OVER, 2), (CROSS, 0, 3), (COMPUTE, 0, 0),
        (ROWS, 1, 3), (ROWS, 3, 1), (CROSS, 1, 2), (ROWS, 1, 1), (COMPUTE, 1, 0), (CROSS, 1, 0), (ROWS, 3, 2),
        (CROSS, 1, 1), (CROSS, 3, 1), (CROSS, 1, 3), (CROSS, 0, 0), (ROWS, 3, 0), (CROSS, 3, 2), (ROWS, 2, 2),
        (CROSS, 0, 2), (COMPUTE, 1, 1), (LINE, 0, 1, 3, 0), (CROSS, 3, 3), (CROSS, 3, 0), (EXCHANGE, 1, 2),
        (ROWS, 3, 3), (LINE, 0, 1, 3, 1), (COMPUTE, 3, 1), (ROWS, 2, 0), (LINE, 0, 1, 2, 0), (ROWS, 2, 1),
        (COMPUTE, 3, 0), (LINE, 0, 3, 3, 1), (EXCHANGE, 3, 1), (EXCHANGE, 3, 2), (CROSS, 2, 3), (EXCHANGE, 3, 0),
        (ROWS, 2, 3), (EXCHANGE, 1, 0), (CROSS, 2, 0), (CROSS, 2, 2), (CROSS, 2, 1), (LINE, 0, 3, 3, 0),
        (COMPUTE, 2, 0), (LINE, 0, 3, 1, 0), (EXCHANGE, 1, 1), (LINE, 0, 3, 2, 0), (COMPUTE, 2, 1),
        (LINE, 0, 2, 3, 0), (CROSS, 0, 1), (EXCHANGE, 2, 0), (EXCHANGE, 2, 1), (LINE, 0, 3, 0, 0), (LINE, 0, 2, 3, 1),
        (EXCHANGE, 2, 2), (COMPUTE, 0, 1), (LINE, 0, 2, 0, 0), (EXCHANGE, 0, 1), (EXCHANGE, 0, 0), (LINE, 0, 2, 1, 0),
        (LINE, 0, 2, 2, 0), (LINE, 0, 1, 1, 0), (EXCHANGE, 0, 2), (FINISH, 3, 1), (LINE, 0, 1, 0, 0), (FINISH, 2, 0),
        (FINISH, 1, 0), (FINISH, 0, 0), (FINISH, 3, 0),
    ),
    (
        (OWN_ASIDE,), (OWN_LINE, 0), (OWN_OVER, 3), (OWN_OVER, 0), (OWN_LINE, 2), (ROWS, 0, 1), (OWN_LINE, 3),
        (ROWS, 0, 2), (OWN_LINE, 1), (ROWS, 3, 1), (ROWS, 2, 2), (ROWS, 0, 0), (LOAD,), (CROSS, 0, 3), (ROWS, 0, 3),
        (ROWS, 3, 2), (CROSS, 1, 3), (COMPUTE, 1, 0), (ROWS, 3, 0), (OWN_OVER, 1), (CROSS, 0, 2), (CROSS, 0, 1),
        (CROSS, 0, 0), (COMPUTE, 0, 0), (CROSS, 1, 0), (CROSS, 3, 3), (ROWS, 3, 3), (ROWS, 2, 0), (CROSS, 3, 2),
        (ROWS, 2, 1), (CROSS, 3, 0), (COMPUTE, 0, 1), (OWN_OVER, 2), (CROSS, 2, 3), (CROSS, 3, 1), (CROSS, 2, 2),
        (COMPUTE, 3, 0), (EXCHANGE, 0, 0), (CROSS, 2, 1), (EXCHANGE, 0, 2), (ROWS, 2, 3), (CROSS, 2, 0),
        (COMPUTE, 3, 1), (CROSS, 1, 1), (COMPUTE, 2, 1), (EXCHANGE, 0, 1), (CROSS, 1, 2), (COMPUTE, 2, 0),
        (LINE, 0, 3, 3, 1), (EXCHANGE, 3, 1), (EXCHANGE, 3, 2), (LINE, 0, 3, 3, 0), (COMPUTE, 1, 1), (EXCHANGE, 3, 0),
        (LINE, 0, 3, 1, 0), (LINE, 0, 3, 2, 0), (EXCHANGE, 2, 1), (LINE, 0, 2, 3, 0), (LINE, 1, 0, 3, 1),
        (EXCHANGE, 2, 2), (EXCHANGE, 2, 0), (LINE, 1, 0, 2, 0), (EXCHANGE, 1, 2), (LINE, 0, 3, 0, 0),
        (LINE, 1, 0, 1, 0), (LINE, 0, 2, 3, 1), (LINE, 1, 0, 3, 0), (LINE, 1, 0, 0, 0), (LINE, 0, 2, 0, 0),
        (EXCHANGE, 1, 1), (FINISH, 3, 1), (LINE, 0, 2, 1, 0), (EXCHANGE, 1, 0), (LINE, 0, 2, 2, 0), (FINISH, 1, 0),
        (FINISH, 3, 0), (FINISH, 2, 0), (FINISH, 0, 0),
    ),
)


def place(count):
    z = lax.axis_index("heads")
    c = lax.axis_index("ctx")
    beside = c + 1 - 2 * lax.rem(c, 2)
    across = lax.rem(c + 2, 4)
    diagonal = lax.rem(beside + 2, 4)
    return z, c, beside, across, diagonal


def nearest(count, z, index):
    index = count - 1 - index
    more = jnp.maximum(z, count - 1 - z)
    fewer = count - 1 - more
    alone = more - fewer
    paired = jnp.maximum(index - alone, 0)
    up = jnp.where(z + more < count, more - index, index - more)
    both = (fewer - paired // 2) * (1 - 2 * (paired % 2))
    offset = jnp.where(index < alone, up, both)
    return z + jnp.where(index < count - 1, offset, 0)


def attend_kernel(
    count, tokens_ref, share_hbm, table_ref, state_ref, past_hbm, qkv_hbm,
    hidden_ref, normed_ref, tables_ref,
    slab_ref, qkv_ref, w_ref, query_ref, kv_ref, before_ref, inside_ref, linear_ref,
    state_out, states_in, heads_out, heads_in,
    local_sem, token_send, token_recv, share_send, share_recv,
    tail_send, tail_recv, state_send, state_recv, head_send, head_recv,
):
    z, c, beside, across, diagonal = place(count)
    row_count, width = tokens_ref.shape
    slab_rows = count * row_count
    share = w_ref.shape[0] // (4 * count)

    def rows_of(index, size):
        return pl.ds(pl.multiple_of(index * size, size), size)

    def share_block(kind, zz, cc):
        if kind == 0:
            return w_ref.at[rows_of(zz * 4 + cc, share), :]
        return tables_ref.at[cc * count + zz]

    def share_source(kind):
        return table_ref if kind else share_hbm.at[rows_of(c, share), :]

    local = [
        pltpu.make_async_copy(source, target, local_sem.at[index])
        for index, (source, target) in enumerate(
            [(qkv_hbm.at[one], qkv_ref.at[:, one * HDIM : (one + 1) * HDIM]) for one in range(3)]
            + [(tokens_ref, slab_ref.at[z])]
            + [(share_source(kind), share_block(kind, z, c)) for kind in (0, 1)]
        )
    ]
    past_copy = pltpu.make_async_copy(past_hbm, before_ref, local_sem.at[6])
    for copy in local:
        copy.start()

    @pl.when(c == 0)
    def _():
        past_copy.start()

    barrier = pltpu.get_barrier_semaphore()
    for target in (beside, across, diagonal):
        pl.semaphore_signal(barrier, inc=1, device_id={"ctx": target}, device_id_type=MESH)
    for zz in range(count):

        @pl.when(zz != z)
        def _():
            pl.semaphore_signal(barrier, inc=1, device_id={"heads": zz}, device_id_type=MESH)

    pl.semaphore_wait(barrier, 3 + count - 1)

    def remote(source, target, send, recv, device):
        return pltpu.make_async_remote_copy(
            src_ref=source, dst_ref=target, send_sem=send, recv_sem=recv,
            device_id=device, device_id_type=MESH,
        )

    def started(copy):
        copy.start()

    def left(copy):
        copy.wait_send()

    def along(act, zz, copy):
        @pl.when(jnp.logical_and(zz >= z, z > 0))
        def _():
            act(copy(0, {"heads": z - 1}))

        @pl.when(jnp.logical_and(zz <= z, z < count - 1))
        def _():
            act(copy(1, {"heads": z + 1}))

    def token_copy(zz, piece, own=False):
        rows = pl.ds(piece * row_count // PIECES, row_count // PIECES)

        def copy(way, device):
            block = slab_ref.at[zz, rows, :]
            source = tokens_ref.at[rows, :] if own else block
            return remote(
                source, block, token_send.at[way, piece, zz], token_recv.at[piece, zz], device
            )

        return copy

    def share_copy(kind, zz, cc, own=False):
        def copy(way, device):
            block = share_block(kind, zz, cc)
            slot = zz * 4 + cc
            source = share_source(kind) if own else block
            return remote(
                source, block, share_send.at[kind, way, slot], share_recv.at[kind, slot], device
            )

        return copy

    def aside(act, zz, cc, own=False):
        for kind in (0, 1):
            act(share_copy(kind, zz, cc, own)(3, {"ctx": beside}))

    def share_relay(act, zz, own=False):
        for kind in (0, 1):
            act(share_copy(kind, zz, c, own)(2, {"ctx": across}))
        aside(act, zz, c, own)

    def share_along(act, zz, own=False):
        for kind in (0, 1):
            along(act, zz, share_copy(kind, zz, c, own))

    def share_received(zz, cc):
        for kind in (0, 1):
            share_copy(kind, zz, cc)(3, {"ctx": beside}).wait_recv()

    def at_distance(distance, act):
        @pl.when(z >= distance)
        def _():
            act(z - distance)

        @pl.when(z + distance < count)
        def _():
            act(z + distance)

    def share_onward(zz):
        share_received(zz, c)
        share_along(started, zz)
        share_relay(started, zz)

    def share_over(zz):
        share_received(zz, across)
        aside(started, zz, across)

    for piece in range(PIECES):
        along(started, z, token_copy(z, piece, True))
    share_relay(started, z, True)
    for copy in local:
        copy.wait()

    def project(zz):
        product = jnp.dot(slab_ref[zz], qkv_ref[...], preferred_element_type=jnp.float32)
        product = product.astype(query_ref.dtype)
        rows = rows_of(zz, row_count)
        query_ref[rows, :] = product[:, :HDIM]
        kv_ref[0, rows, :] = product[:, HDIM : 2 * HDIM]
        kv_ref[1, rows, :] = product[:, 2 * HDIM :]

        @pl.when(c < 3)
        def _():
            tail_copy(zz).start()

    def tail_copy(zz):
        rows = rows_of(zz, row_count)
        return remote(
            kv_ref.at[:, rows, :], before_ref.at[:, rows, :], tail_send.at[zz], tail_recv.at[zz],
            {"ctx": jnp.minimum(c + 1, 3)},
        )

    def token_relay(zz, piece):
        token_copy(zz, piece)(0, {"heads": z - 1}).wait_recv()
        along(started, zz, token_copy(zz, piece))

    def step(index, _):
        zz = nearest(count, z, index)
        last = nearest(count, z, jnp.maximum(index - 1, 0))
        after = nearest(count, z, jnp.minimum(index + 1, count - 1))
        opens = jnp.logical_and(index > 0, jnp.abs(zz - z) != jnp.abs(last - z))
        double = jnp.logical_and(index < count - 1, jnp.abs(after - z) == jnp.abs(zz - z))

        for piece in range(PIECES):

            @pl.when(opens)
            def _():
                token_relay(zz, piece)

            @pl.when(jnp.logical_and(opens, double))
            def _():
                token_relay(after, piece)

        project(zz)
        alone = jnp.logical_and(index > 0, jnp.logical_not(jnp.logical_and(opens, double)))
        distance = jnp.abs(zz - z)

        @pl.when(jnp.logical_and(alone, distance == 1))
        def _():
            share_along(started, z, True)

        @pl.when(jnp.logical_and(alone, distance > 1))
        def _():
            at_distance(distance - 1, share_onward)

        return 0

    lax.fori_loop(0, count, step, 0)

    local_state = lax.dot_general(
        kv_ref[0], kv_ref[1], (((0,), (0,)), ((), ())), preferred_element_type=jnp.float32
    )
    state_out[...] = local_state.astype(state_out.dtype)
    others = [beside, across, diagonal]
    state_copies = [
        remote(state_out, states_in.at[c], state_send.at[way], state_recv.at[c], {"ctx": target})
        for way, target in enumerate(others)
    ]
    for copy in state_copies:
        copy.start()
    share_over(z)

    blocks = slab_rows // row_count
    for block in range(blocks):
        first, end = block * row_count, (block + 1) * row_count
        query = query_ref[first:end, :]
        scores = lax.dot_general(
            query, kv_ref[0, :end, :], (((1,), (1,)), ((), ())), preferred_element_type=jnp.float32
        )
        shape = scores.shape
        causal = lax.broadcasted_iota(jnp.int32, shape, 1) <= first + lax.broadcasted_iota(
            jnp.int32, shape, 0
        )
        inside_ref[first:end, :end] = scores
        weights = jnp.where(causal, scores, 0.0).astype(kv_ref.dtype)
        linear_ref[first:end, :] = jnp.dot(
            weights, kv_ref[1, :end, :], preferred_element_type=jnp.float32
        )

    for target in others:
        remote(
            state_out, states_in.at[target], state_send.at[0], state_recv.at[target],
            {"ctx": beside},
        ).wait_recv()
    start = state_ref[...]
    for cc in range(4):
        start = start + jnp.where(cc < c, states_in[cc].astype(jnp.float32), 0.0)

    @pl.when(c == 0)
    def _():
        past_copy.wait()

    @pl.when(c > 0)
    def _():
        for zz in range(count):
            tail_copy(zz).wait_recv()

    scale = 1.0 / math.sqrt(HDIM)

    def head_copy(zz):
        columns = pl.ds(pl.multiple_of(z * HDIM, HDIM), HDIM)
        return remote(
            heads_out.at[zz], heads_in.at[:, columns], head_send.at[zz], head_recv.at[z],
            {"heads": zz},
        )

    for block in range(blocks):
        first, end = block * row_count, (block + 1) * row_count
        query = query_ref[first:end, :]
        old = lax.dot_general(
            query, before_ref[0, first:, :], (((1,), (1,)), ((), ())),
            preferred_element_type=jnp.float32,
        )
        old_seen = lax.broadcasted_iota(jnp.int32, old.shape, 1) > lax.broadcasted_iota(
            jnp.int32, old.shape, 0
        )
        old = jnp.where(old_seen, old * scale, -jnp.inf)
        new = inside_ref[first:end, :end]
        new_seen = lax.broadcasted_iota(jnp.int32, new.shape, 1) <= first + lax.broadcasted_iota(
            jnp.int32, new.shape, 0
        )
        new = jnp.where(new_seen, new * scale, -jnp.inf)
        top = jnp.maximum(
            jnp.max(old, axis=-1, keepdims=True), jnp.max(new, axis=-1, keepdims=True)
        )
        old = jnp.exp(old - top)
        new = jnp.exp(new - top)
        inverse = 1.0 / (
            jnp.sum(old, axis=-1, keepdims=True) + jnp.sum(new, axis=-1, keepdims=True)
        )
        window = jnp.dot(
            (old * inverse).astype(kv_ref.dtype), before_ref[1, first:, :],
            preferred_element_type=jnp.float32,
        ) + jnp.dot(
            (new * inverse).astype(kv_ref.dtype), kv_ref[1, :end, :],
            preferred_element_type=jnp.float32,
        )
        linear = linear_ref[first:end, :] + jnp.dot(
            query.astype(jnp.float32), start, precision=lax.Precision.HIGHEST,
            preferred_element_type=jnp.float32,
        )
        heads_out[block] = (normalize(linear) + window).astype(heads_out.dtype)

        @pl.when(block != z)
        def _():
            head_copy(block).start()

        @pl.when(block == z)
        def _():
            columns = pl.ds(pl.multiple_of(z * HDIM, HDIM), HDIM)
            heads_in[:, columns] = heads_out[block]

        if block == 0:
            at_distance(jnp.maximum(z, count - 1 - z), share_onward)
        if block + 1 < count:
            at_distance(block + 1, share_over)

    for zz in range(count):
        share_received(zz, beside)
        share_received(zz, diagonal)

        @pl.when(zz != z)
        def _():
            remote(
                heads_out.at[zz], heads_in.at[:, zz * HDIM : (zz + 1) * HDIM], head_send.at[zz],
                head_recv.at[zz], {"heads": zz},
            ).wait_recv()

    def out_tile(index, total):
        columns = pl.ds(pl.multiple_of(index * DOT_COLUMNS, DOT_COLUMNS), DOT_COLUMNS)
        attn = jnp.dot(heads_in[...], w_ref[:, columns], preferred_element_type=jnp.float32)
        hidden = (slab_ref[z, :, columns].astype(jnp.float32) + attn).astype(hidden_ref.dtype)
        hidden_ref[:, columns] = hidden
        hidden = hidden.astype(jnp.float32)
        return total + jnp.sum(hidden * hidden, axis=-1, keepdims=True)

    total = lax.fori_loop(
        0, width // DOT_COLUMNS, out_tile, jnp.zeros((row_count, 1), jnp.float32)
    )
    inverse = lax.rsqrt(total / width + 1e-06)
    for first in range(0, width, DOT_COLUMNS):
        hidden = hidden_ref[:, first : first + DOT_COLUMNS].astype(jnp.float32)
        normed_ref[:, first : first + DOT_COLUMNS] = (hidden * inverse).astype(normed_ref.dtype)

    for piece in range(PIECES):
        along(left, z, token_copy(z, piece, True))
    share_along(left, z, True)
    share_relay(left, z, True)

    @pl.when(c < 3)
    def _():
        for zz in range(count):
            tail_copy(zz).wait_send()

    for copy in state_copies:
        copy.wait_send()
    for zz in range(count):
        aside(left, zz, across)

        @pl.when(zz != z)
        def _():
            for piece in range(PIECES):
                along(left, zz, token_copy(zz, piece))
            share_along(left, zz)
            share_relay(left, zz)
            head_copy(zz).wait_send()


def plain_steps(count, at):
    spans = range(len(SPANS))
    steps = [(OWN_LINE, span) for span in spans] + [(OWN_OVER, span) for span in spans]
    steps += [(OWN_ASIDE,), (LOAD,)]
    for distance in range(count):
        planes = sorted({at - distance, at + distance} & set(range(count)))
        for op in (ROWS, CROSS):
            if op == CROSS or distance:
                steps += [(op, zz, span) for zz in planes for span in reversed(spans)]
        steps += [(COMPUTE, zz, pair) for zz in planes for pair in (0, 1)]
    near = [span for span in spans if not SPANS[span][1]]
    far = [span for span in spans if SPANS[span][1]]
    steps += [(EXCHANGE, zz, span) for zz in range(count) for span in near]
    for key in range(1, count):
        links = [(0, key)] * (key > at) + [(1, count - 1 - key)] * (count - 1 - key < at)
        for link in links if at < count - 1 - at else reversed(links):
            steps += [(LINE, *link, span, 0) for span in spans]
            steps += [(LINE, *link, span, 1) for span in far]
    return steps + [(FINISH, span, 1) for span in far] + [(FINISH, span, 0) for span in spans]


def mirrored(step, count):
    op, *where = step
    if op in (ROWS, CROSS, EXCHANGE, COMPUTE):
        return (op, count - 1 - where[0], where[1])
    if op == LINE:
        return (op, 1 - where[0], count - 1 - where[1], *where[2:])
    return step


def steps_of(count, at):
    if count != len(STEPS) * 2:
        return plain_steps(count, at)
    if at < len(STEPS):
        return list(STEPS[at])
    return [mirrored(step, count) for step in STEPS[count - 1 - at]]


def span_rows(row_count):
    spans, first = [], 0
    for share, far in SPANS:
        spans.append((first, row_count * share // 128, far))
        first += row_count * share // 128
    return spans, sum(size for _, size, far in spans if far)


def expert_kernel(
    count, weight_copies, hidden_ref, own_ref, table_ref, out_ref,
    rows_ref, part_ref, hid_ref, scale_ref, gate_ref, up_ref, down_ref,
    from_beside, to_across, from_across, line_out, line_in, last_out, last_in,
    local_sem, row_send, row_recv, beside_send, beside_recv, across_send, across_recv,
    line_send, line_recv, last_send, last_recv,
):
    z, c, beside, across, diagonal = place(count)
    row_count, width = own_ref.shape
    spans, far_rows = span_rows(row_count)
    near_rows = row_count - far_rows
    expert = c * count + z
    own_rows = pl.ds(pl.multiple_of(c * row_count, row_count), row_count)
    own_copy = pltpu.make_async_copy(own_ref, rows_ref.at[z, own_rows, :], local_sem)
    own_copy.start()
    local = weight_copies + [own_copy]

    def window(cc, span):
        first, size, _ = spans[span]
        return pl.ds(pl.multiple_of(cc * row_count + first, 16), size)

    def row_copy(zz, cc, span, way, target, own=False):
        first, size, _ = spans[span]
        slot = zz * 4 + cc
        block = rows_ref.at[zz, window(cc, span), :]
        return pltpu.make_async_remote_copy(
            src_ref=own_ref.at[pl.ds(first, size), :] if own else block,
            dst_ref=block,
            send_sem=row_send.at[way, span, slot],
            recv_sem=row_recv.at[span, slot],
            device_id=target,
            device_id_type=MESH,
        )

    def started(copy):
        copy.start()

    def left(copy):
        copy.wait_send()

    def received(zz, cc, span):
        row_copy(zz, cc, span, 0, {"ctx": beside}).wait_recv()

    def along(act, at, zz, cc, span, own=False):
        if zz >= at and at > 0:
            act(row_copy(zz, cc, span, 0, {"heads": at - 1}, own))
        if zz <= at and at < count - 1:
            act(row_copy(zz, cc, span, 1, {"heads": at + 1}, own))

    def over(act, zz, cc, span, own=False):
        act(row_copy(zz, cc, span, 2, {"ctx": across}, own))

    def aside(act, zz, cc, span, own=False):
        act(row_copy(zz, cc, span, 3, {"ctx": beside}, own))

    def relays(op, at, zz, span, act, wait):
        cc = c if op == ROWS else across
        far = spans[span][2]
        if wait:
            received(zz, cc, span)
        if op == ROWS or far:
            along(act, at, zz, cc, span)
        if op == ROWS and not far:
            over(act, zz, cc, span)
        aside(act, zz, cc, span)

    def paired(zz, pair):
        for span in range(len(spans)):
            received(zz, diagonal if pair else beside, span)

    def compute(zz, pair):
        half = jnp.where(pair == 0, c // 2, 1 - c // 2)
        for core in range(2):
            row = table_ref[(half * 2 + core) * count + zz, pl.ds(expert, 1), :]
            scale_ref[core * row_count : (core + 1) * row_count, :] = jnp.broadcast_to(
                row, (HDIM, row_count)
            ).T

        inner = gate_ref.shape[1]
        rows = pl.ds(pl.multiple_of(half * 2 * row_count, 2 * row_count), 2 * row_count)

        def hidden_tile(index, _):
            columns = pl.ds(pl.multiple_of(index * HID_COLUMNS, HID_COLUMNS), HID_COLUMNS)
            block = rows_ref[zz, rows, :]
            gate = jnp.dot(block, gate_ref[:, columns], preferred_element_type=jnp.float32)
            up = jnp.dot(block, up_ref[:, columns], preferred_element_type=jnp.float32)
            scale = jnp.concatenate([scale_ref[...]] * (HID_COLUMNS // HDIM), axis=1)
            hid_ref[:, columns] = (jax.nn.silu(gate) * up * scale).astype(hid_ref.dtype)
            return 0

        lax.fori_loop(0, inner // HID_COLUMNS, hidden_tile, 0)

        def out_tile(index, _):
            columns = pl.ds(pl.multiple_of(index * DOT_COLUMNS, DOT_COLUMNS), DOT_COLUMNS)
            product = jnp.dot(
                hid_ref[...], down_ref[:, columns], preferred_element_type=jnp.float32
            )
            part_ref[zz, rows, columns] = product.astype(part_ref.dtype)
            return 0

        lax.fori_loop(0, width // DOT_COLUMNS, out_tile, 0)

    def beside_copy(kind, zz):
        cc = diagonal if kind == 0 else beside
        return pltpu.make_async_remote_copy(
            src_ref=part_ref.at[zz, pl.ds(pl.multiple_of(cc * row_count, row_count), row_count), :],
            dst_ref=from_beside.at[kind, zz],
            send_sem=beside_send.at[kind, zz],
            recv_sem=beside_recv.at[kind, zz],
            device_id={"ctx": beside},
            device_id_type=MESH,
        )

    def across_copy(zz, span):
        first, size, _ = spans[span]
        return pltpu.make_async_remote_copy(
            src_ref=to_across.at[zz, pl.ds(first, size), :],
            dst_ref=from_across.at[zz, pl.ds(first, size), :],
            send_sem=across_send.at[span, zz],
            recv_sem=across_recv.at[span, zz],
            device_id={"ctx": across},
            device_id_type=MESH,
        )

    def line_rows(span, other):
        first, size, _ = spans[span]
        return pl.ds(row_count + first - near_rows if other else first, size)

    def line_copy(side, zz, span, other):
        return pltpu.make_async_remote_copy(
            src_ref=line_out.at[zz, line_rows(span, other), :],
            dst_ref=line_in.at[side, zz, line_rows(span, other), :],
            send_sem=line_send.at[2 * span + other, zz],
            recv_sem=line_recv.at[2 * span + other, side, zz],
            device_id={"heads": z + 1 - 2 * side},
            device_id_type=MESH,
        )

    def last_rows(span):
        first, size, _ = spans[span]
        return pl.ds(first - near_rows, size)

    def last_copy(span):
        return pltpu.make_async_remote_copy(
            src_ref=last_out.at[last_rows(span), :],
            dst_ref=last_in.at[last_rows(span), :],
            send_sem=last_send.at[span],
            recv_sem=last_recv.at[span],
            device_id={"ctx": across},
            device_id_type=MESH,
        )

    def add(target, sources):
        def chunk(index, _):
            rows = pl.ds(pl.multiple_of(index * ADD_ROWS, ADD_ROWS), ADD_ROWS)
            total = sources[0][rows, :].astype(jnp.float32)
            for source in sources[1:]:
                total = total + source[rows, :].astype(jnp.float32)
            target[rows, :] = total.astype(target.dtype)
            return 0

        lax.fori_loop(0, target.shape[0] // ADD_ROWS, chunk, 0)

    def starts(side, at):
        return at == side * (count - 1)

    def chip_sources(zz, span, other):
        first, size, far = spans[span]
        start = pl.multiple_of((across if other else c) * row_count + first, 16)
        sources = [
            part_ref.at[zz, pl.ds(start, size), :],
            from_beside.at[1 - other, zz, pl.ds(first, size), :],
        ]
        if not far and not other:
            sources.append(from_across.at[zz, pl.ds(first, size), :])
        return sources

    def perform(at, steps, waited):
        waited = set(waited)

        def once(kind, zz):
            if (kind, zz) not in waited:
                waited.add((kind, zz))
                beside_copy(kind, zz).wait_recv()

        def arrived(zz, span, other, sides):
            once(1 - other, zz)
            if not spans[span][2]:
                across_copy(zz, span).wait_recv()
            sources = chip_sources(zz, span, other)
            for side in sides:
                if not starts(side, at):
                    line_copy(side, zz, span, other).wait_recv()
                    sources.append(line_in.at[side, zz, line_rows(span, other), :])
            return sources

        for op, *where in steps:
            if op == OWN_LINE:
                along(started, at, at, c, where[0], True)
            elif op == OWN_OVER:
                over(started, at, c, where[0], True)
            elif op == OWN_ASIDE:
                for span in range(len(spans)):
                    aside(started, at, c, span, True)
            elif op == LOAD:
                for copy in local:
                    copy.wait()
            elif op == COMPUTE:
                paired(*where)
            elif op == BESIDE:
                beside_copy(where[1], where[0]).start()
            elif op == EXCHANGE:
                zz, span = where
                once(0, zz)
                first, size, _ = spans[span]
                start = pl.multiple_of(across * row_count + first, 16)
                add(
                    to_across.at[zz, pl.ds(first, size), :],
                    [
                        part_ref.at[zz, pl.ds(start, size), :],
                        from_beside.at[0, zz, pl.ds(first, size), :],
                    ],
                )
                across_copy(zz, span).start()
            elif op == LINE:
                side, zz, span, other = where
                add(line_out.at[zz, line_rows(span, other), :], arrived(zz, span, other, (side,)))
                line_copy(side, zz, span, other).start()
            elif op == FINISH and where[1]:
                span = where[0]
                add(last_out.at[last_rows(span), :], arrived(at, span, 1, (0, 1)))
                last_copy(span).start()
            elif op == FINISH:
                span = where[0]
                first, size, far = spans[span]
                rows = pl.ds(first, size)
                sources = arrived(at, span, 0, (0, 1))
                if far:
                    last_copy(span).wait_recv()
                    sources.append(last_in.at[last_rows(span), :])
                add(out_ref.at[rows, :], [hidden_ref.at[rows, :]] + sources)
            else:
                relays(op, at, *where, started, True)

    def each_place(act):
        for at in range(count):

            @pl.when(z == at)
            def _():
                act(at)

    units = 2 * count
    segments, orders = [], []
    for at in range(count):
        parts, order = [[]], []
        for one in steps_of(count, at):
            parts[-1].append(one)
            if one[0] == COMPUTE:
                zz, pair = one[1:]
                order.append((zz, pair))
                parts.append([(BESIDE, zz, 1 - pair)])
        segments.append(parts)
        orders.append(order)

    def waits_of(at, unit):
        keys = set()
        for op, *where in sum(segments[at][:unit], []):
            if op == EXCHANGE:
                keys.add((0, where[0]))
            elif op == LINE:
                keys.add((1 - where[3], where[1]))
            elif op == FINISH:
                keys.add((1 - where[1], at))
        return keys

    def choose(index, pick):
        value = jnp.int32(0)
        for at in range(count):
            for unit in range(units):
                here = jnp.logical_and(z == at, index == unit)
                value = jnp.where(here, pick(orders[at][unit]), value)
        return value

    def step(index, _):
        def segment(at):
            for unit in range(units):

                @pl.when(index == unit)
                def _():
                    perform(at, segments[at][unit], waits_of(at, unit))

        each_place(segment)
        compute(choose(index, lambda unit: unit[0]), choose(index, lambda unit: unit[1]))
        return 0

    lax.fori_loop(0, units, step, 0)

    def finish(at):
        perform(at, segments[at][units], waits_of(at, units))
        for span, (_, _, far) in enumerate(spans):
            if far:
                last_copy(span).wait_send()
            along(left, at, at, c, span, True)
            over(left, at, c, span, True)
            aside(left, at, c, span, True)
            for zz in range(count):
                relays(CROSS, at, zz, span, left, False)
                if not far:
                    across_copy(zz, span).wait_send()
                if zz != at:
                    relays(ROWS, at, zz, span, left, False)
                    for other in range(1 + far):
                        line_copy(int(zz < at), zz, span, other).wait_send()
        for zz in range(count):
            beside_copy(0, zz).wait_send()
            beside_copy(1, zz).wait_send()

    each_place(finish)


def layer_kernel(
    count, front_size, tokens_ref, share_hbm, ids_ref, gates_ref, state_ref, past_hbm, qkv_hbm,
    gate_hbm, up_hbm, down_hbm, out_ref, hidden_ref, normed_ref, table_ref, tables_ref, weight_sem,
    *scratch
):
    front, back = scratch[:front_size], scratch[front_size:]
    weight_copies = [
        pltpu.make_async_copy(source, target, weight_sem.at[index])
        for index, (source, target) in enumerate(zip((gate_hbm, up_hbm, down_hbm), back[4:7]))
    ]
    for copy in weight_copies:
        copy.start()
    experts = lax.broadcasted_iota(jnp.int32, table_ref.shape, 0)
    table = jnp.zeros(table_ref.shape, table_ref.dtype)
    for pick in range(ids_ref.shape[0]):
        chosen = ids_ref[pick : pick + 1, :] == experts
        table = table + jnp.where(chosen, gates_ref[pick : pick + 1, :], 0.0)
    table_ref[...] = table
    attend_kernel(
        count, tokens_ref, share_hbm, table_ref, state_ref, past_hbm, qkv_hbm,
        hidden_ref, normed_ref, tables_ref, *front,
    )
    expert_kernel(count, weight_copies, hidden_ref, normed_ref, tables_ref, out_ref, *back)


def run_layer(tokens, w_out, ids, gates, state_in, past_kv, w_qkv, w_gate, w_up, w_down):
    count = lax.axis_size("heads")
    row_count, width = tokens.shape
    slab_rows = count * row_count
    inner = w_gate.shape[1]
    kind = tokens.dtype
    slots = 4 * count
    far_rows = span_rows(row_count)[1]
    near_rows = row_count - far_rows
    cuts = len(SPANS)
    dma = pltpu.SemaphoreType.DMA
    vmem, anywhere = pl.BlockSpec(memory_space=pltpu.VMEM), pl.BlockSpec(memory_space=pl.ANY)
    shared = [
        pltpu.VMEM((row_count, width), kind),
        pltpu.VMEM((row_count, width), kind),
        pltpu.VMEM((slots, row_count), gates.dtype),
        pltpu.VMEM((slots, slots, row_count), gates.dtype),
        dma((3,)),
    ]
    front = [
        pltpu.VMEM((count, row_count, width), kind),
        pltpu.VMEM((width, 3 * HDIM), kind),
        pltpu.VMEM((count * HDIM, width), kind),
        pltpu.VMEM((slab_rows, HDIM), kind),
        pltpu.VMEM((2, slab_rows, HDIM), kind),
        pltpu.VMEM((2, WINDOW, HDIM), kind),
        pltpu.VMEM((slab_rows, slab_rows), jnp.float32),
        pltpu.VMEM((slab_rows, HDIM), jnp.float32),
        pltpu.VMEM((HDIM, HDIM), kind),
        pltpu.VMEM((4, HDIM, HDIM), kind),
        pltpu.VMEM((count, row_count, HDIM), kind),
        pltpu.VMEM((row_count, count * HDIM), kind),
        dma((7,)),
        dma((2, PIECES, count)),
        dma((PIECES, count)),
        dma((2, 4, slots)),
        dma((2, slots)),
        dma((count,)),
        dma((count,)),
        dma((3,)),
        dma((4,)),
        dma((count,)),
        dma((count,)),
    ]
    back = [
        pltpu.VMEM((count, 4 * row_count, width), kind),
        pltpu.VMEM((count, 4 * row_count, width), kind),
        pltpu.VMEM((2 * row_count, inner), kind),
        pltpu.VMEM((2 * row_count, HDIM), jnp.float32),
        pltpu.VMEM(w_gate.shape, kind),
        pltpu.VMEM(w_up.shape, kind),
        pltpu.VMEM(w_down.shape, kind),
        pltpu.VMEM((2, count, row_count, width), kind),
        pltpu.VMEM((count, near_rows, width), kind),
        pltpu.VMEM((count, near_rows, width), kind),
        pltpu.VMEM((count, row_count + far_rows, width), kind),
        pltpu.VMEM((2, count, row_count + far_rows, width), kind),
        pltpu.VMEM((far_rows, width), kind),
        pltpu.VMEM((far_rows, width), kind),
        dma(()),
        dma((4, cuts, 4 * count)),
        dma((cuts, 4 * count)),
        dma((2, count)),
        dma((2, count)),
        dma((cuts, count)),
        dma((cuts, count)),
        dma((2 * cuts, count)),
        dma((2 * cuts, 2, count)),
        dma((cuts,)),
        dma((cuts,)),
    ]
    return pl.pallas_call(
        functools.partial(layer_kernel, count, len(front)),
        out_shape=jax.ShapeDtypeStruct((row_count, width), kind),
        in_specs=[anywhere] * 2 + [vmem] * 3 + [anywhere] * 5,
        out_specs=vmem,
        scratch_shapes=shared + front + back,
        compiler_params=pltpu.CompilerParams(
            collective_id=0, has_side_effects=True, vmem_limit_bytes=VMEM_BYTES
        ),
        name="run_layer",
    )(tokens, w_out, ids, gates, state_in, past_kv, w_qkv, w_gate, w_up, w_down)


def on_device(
    tokens, state_in, past_kv, w_qkv, w_out, w_gate, w_up, w_down, expert_ids, gate_weights
):
    row_count, model_width = tokens.shape
    inner_width = w_qkv.shape[2]
    local_heads = inner_width // HDIM
    ctx_count = lax.axis_size("ctx")
    head_count = lax.axis_size("heads")
    exp_local = w_gate.shape[0]
    devices = ctx_count * head_count
    expert_count = exp_local * devices
    top_count = expert_ids.shape[1]
    capacity = max(2, 2 * row_count * top_count // expert_count)
    dense = (
        ctx_count == 4
        and exp_local == 1
        and row_count % HDIM == 0
        and local_heads == 1
        and head_count * row_count == WINDOW
        and w_gate.shape[2] % HID_COLUMNS == 0
        and row_count * devices <= expert_count * capacity
    )
    if dense:
        return run_layer(
            tokens, w_out, expert_ids.T, gate_weights.T, state_in[0], past_kv,
            jnp.transpose(w_qkv, (1, 0, 2)), w_gate[0], w_up[0], w_down[0],
        )
    slab, w_rows = [
        lax.all_gather(value, "heads", axis=0, tiled=True) for value in (tokens, w_out)
    ]
    projected = jnp.dot(
        slab,
        w_qkv.reshape(model_width, 3 * inner_width),
        preferred_element_type=jnp.float32,
    ).astype(jnp.bfloat16)
    slab_rows = projected.shape[0]
    projected = projected.reshape(slab_rows, 3, local_heads, HDIM)
    query = jnp.transpose(projected[:, 0], (1, 0, 2))
    keys = jnp.transpose(projected[:, 1], (1, 0, 2))
    values = jnp.transpose(projected[:, 2], (1, 0, 2))
    local_state = jnp.einsum("hsd,hse->hde", keys, values, preferred_element_type=jnp.float32)
    earlier_state = entering(
        local_state, "ctx", lambda first, second: first + second, jnp.zeros_like(local_state)
    )
    start_state = state_in + earlier_state
    tail = jnp.stack([keys, values], axis=0)
    arrived = from_behind(tail, "ctx", 1)
    past = jnp.transpose(past_kv.reshape(2, WINDOW, local_heads, HDIM), (0, 2, 1, 3))
    previous = jnp.where(lax.axis_index("ctx") == 0, past, arrived)
    all_keys = jnp.concatenate([previous[0], keys], axis=1)
    all_values = jnp.concatenate([previous[1], values], axis=1)
    block_rows = min(slab_rows, 512)
    block_count = slab_rows // block_rows
    scale = 1.0 / math.sqrt(HDIM)
    causal = jnp.arange(block_rows)[:, None] >= jnp.arange(block_rows)[None, :]
    offsets = jnp.arange(WINDOW + block_rows)[None, :] - jnp.arange(block_rows)[:, None]
    in_window = (offsets > 0) & (offsets <= WINDOW)

    def block_step(state, index):
        first = index * block_rows
        carried = jnp.einsum(
            "hsd,hde->hse", query.astype(jnp.float32), state, precision=lax.Precision.HIGHEST
        )
        inside = jnp.einsum("hsd,htd->hst", query, keys, preferred_element_type=jnp.float32)
        inside = jnp.where(causal[None], inside, 0.0).astype(jnp.bfloat16)
        linear = carried + jnp.einsum(
            "hst,hte->hse", inside, values, preferred_element_type=jnp.float32
        )
        scores = (
            jnp.einsum("hsd,htd->hst", query, all_keys, preferred_element_type=jnp.float32) * scale
        )
        scores = jnp.where(in_window[None], scores, -jnp.inf)
        top_score = jnp.max(scores, axis=-1, keepdims=True)
        expo = jnp.exp(scores - top_score)
        probs = (expo / jnp.sum(expo, axis=-1, keepdims=True)).astype(jnp.bfloat16)
        window_out = jnp.einsum(
            "hst,hte->hse", probs, all_values, preferred_element_type=jnp.float32
        )
        combined = (normalize(linear) + window_out).astype(jnp.bfloat16)
        new_state = state + jnp.einsum(
            "hsd,hse->hde", keys, values, preferred_element_type=jnp.float32
        )
        return (new_state, combined)

    _, outs = lax.scan(block_step, start_state, jnp.arange(block_count, dtype=jnp.int32))
    heads_out = jnp.transpose(outs, (0, 2, 1, 3)).reshape(slab_rows, inner_width)
    regrouped = lax.all_to_all(heads_out, "heads", split_axis=0, concat_axis=1, tiled=True)
    attn = jnp.dot(
        regrouped,
        w_rows,
        preferred_element_type=jnp.float32,
    )
    hidden_state = (tokens.astype(jnp.float32) + attn).astype(jnp.bfloat16)
    hidden_float = hidden_state.astype(jnp.float32)
    normed = normalize(hidden_float).astype(jnp.bfloat16)
    picks = expert_ids.reshape(-1)
    onehot = (picks[:, None] == jnp.arange(expert_count, dtype=jnp.int32)[None, :]).astype(
        jnp.int32
    )
    earlier = jnp.cumsum(onehot, axis=0) - onehot
    slots = jnp.sum(onehot * earlier, axis=1)
    destination = picks * capacity + slots
    source_rows = jnp.arange(row_count * top_count, dtype=jnp.int32) // top_count
    outgoing = jnp.zeros((expert_count * capacity, model_width), jnp.bfloat16)
    outgoing = outgoing.at[destination].set(normed[source_rows])
    sendable = outgoing.reshape(expert_count, 1, capacity, model_width)
    arrived_rows = lax.all_to_all(
        sendable, ("ctx", "heads"), split_axis=0, concat_axis=1, tiled=True
    )
    e_count, n_count, c_count, d_count = arrived_rows.shape
    flat = arrived_rows.reshape(e_count, n_count * c_count, d_count)
    gate_act = jnp.einsum("erd,edf->erf", flat, w_gate, preferred_element_type=jnp.float32)
    up_act = jnp.einsum("erd,edf->erf", flat, w_up, preferred_element_type=jnp.float32)
    hid = (jax.nn.silu(gate_act) * up_act).astype(jnp.bfloat16)
    out_rows = jnp.einsum("erf,efd->erd", hid, w_down, preferred_element_type=jnp.float32)
    finished = out_rows.astype(jnp.bfloat16).reshape(e_count, n_count, c_count, d_count)
    returned = lax.all_to_all(finished, ("ctx", "heads"), split_axis=1, concat_axis=0, tiled=True)
    returned = returned.reshape(expert_count * capacity, model_width)
    picked = returned[destination].reshape(row_count, top_count, model_width).astype(jnp.float32)
    routed = jnp.sum(gate_weights[:, :, None] * picked, axis=1)
    return (hidden_float + routed).astype(jnp.bfloat16)


def solution(mesh):
    return jax.shard_map(
        on_device,
        mesh=mesh,
        in_specs=(
            P(("groups", "ctx", "heads"), None),
            P("heads", "groups", None),
            P(None, "groups", "heads"),
            P(None, None, "heads"),
            P("heads", None),
            P(("ctx", "heads"), None, None),
            P(("ctx", "heads"), None, None),
            P(("ctx", "heads"), None, None),
            P(("groups", "ctx", "heads"), None),
            P(("groups", "ctx", "heads"), None),
        ),
        out_specs=P(("groups", "ctx", "heads"), None),
        check_vma=False,
    )
```

```python
import functools
import math

import jax
import jax.numpy as jnp
from jax import lax
from jax.experimental import pallas as pl
from jax.experimental.pallas import tpu as pltpu
from jax.sharding import PartitionSpec as P

HDIM = 128
WINDOW = 512


def entering(x, axis, join, neutral):
    place = lax.axis_index(axis)
    gathered = lax.all_gather(x.astype(jnp.bfloat16), axis)
    state = jnp.zeros_like(x) + jnp.asarray(neutral, x.dtype)

    def one(lap, state):
        return join(state, lax.dynamic_index_in_dim(gathered, lap, 0, False).astype(x.dtype))

    return lax.fori_loop(0, place, one, state)


def from_behind(block, axis, distance):
    devices = range(lax.axis_size(axis))
    route = [(i - distance, i) for i in devices if i - distance in devices]
    return lax.ppermute(block, axis, route)


def normalize(value):
    return value * lax.rsqrt(jnp.mean(value * value, axis=-1, keepdims=True) + 1e-06)


MESH = pl.DeviceIdType.MESH
VMEM_BYTES = 62 * 1024 * 1024
ADD_ROWS = 16
PIECES = 2
DOT_COLUMNS = 1024
HID_COLUMNS = 256
SPANS = ((32, 0), (32, 0), (32, 0), (32, 1))
OWN_LINE, OWN_OVER, OWN_ASIDE, LOAD, ROWS, CROSS = range(6)
COMPUTE, EXCHANGE, LINE, FINISH, BESIDE = range(6, 11)
STEPS = (
    (
        (OWN_LINE, 1), (OWN_OVER, 0), (OWN_OVER, 1), (OWN_LINE, 2), (LOAD,), (OWN_ASIDE,), (OWN_OVER, 3),
        (OWN_LINE, 0), (ROWS, 1, 0), (OWN_LINE, 3), (ROWS, 1, 2), (OWN_OVER, 2), (CROSS, 0, 3), (COMPUTE, 0, 0),
        (ROWS, 1, 3), (ROWS, 3, 1), (CROSS, 1, 2), (ROWS, 1, 1), (COMPUTE, 1, 0), (CROSS, 1, 0), (ROWS, 3, 2),
        (CROSS, 1, 1), (CROSS, 3, 1), (CROSS, 1, 3), (CROSS, 0, 0), (ROWS, 3, 0), (CROSS, 3, 2), (ROWS, 2, 2),
        (CROSS, 0, 2), (COMPUTE, 1, 1), (LINE, 0, 1, 3, 0), (CROSS, 3, 3), (CROSS, 3, 0), (EXCHANGE, 1, 2),
        (ROWS, 3, 3), (LINE, 0, 1, 3, 1), (COMPUTE, 3, 1), (ROWS, 2, 0), (LINE, 0, 1, 2, 0), (ROWS, 2, 1),
        (COMPUTE, 3, 0), (LINE, 0, 3, 3, 1), (EXCHANGE, 3, 1), (EXCHANGE, 3, 2), (CROSS, 2, 3), (EXCHANGE, 3, 0),
        (ROWS, 2, 3), (EXCHANGE, 1, 0), (CROSS, 2, 0), (CROSS, 2, 2), (CROSS, 2, 1), (LINE, 0, 3, 3, 0),
        (COMPUTE, 2, 0), (LINE, 0, 3, 1, 0), (EXCHANGE, 1, 1), (LINE, 0, 3, 2, 0), (COMPUTE, 2, 1),
        (LINE, 0, 2, 3, 0), (CROSS, 0, 1), (EXCHANGE, 2, 0), (EXCHANGE, 2, 1), (LINE, 0, 3, 0, 0), (LINE, 0, 2, 3, 1),
        (EXCHANGE, 2, 2), (COMPUTE, 0, 1), (LINE, 0, 2, 0, 0), (EXCHANGE, 0, 1), (EXCHANGE, 0, 0), (LINE, 0, 2, 1, 0),
        (LINE, 0, 2, 2, 0), (LINE, 0, 1, 1, 0), (EXCHANGE, 0, 2), (FINISH, 3, 1), (LINE, 0, 1, 0, 0), (FINISH, 2, 0),
        (FINISH, 1, 0), (FINISH, 0, 0), (FINISH, 3, 0),
    ),
    (
        (OWN_ASIDE,), (OWN_LINE, 0), (OWN_OVER, 3), (OWN_OVER, 0), (OWN_LINE, 2), (ROWS, 0, 1), (OWN_LINE, 3),
        (ROWS, 0, 2), (OWN_LINE, 1), (ROWS, 3, 1), (ROWS, 2, 2), (ROWS, 0, 0), (LOAD,), (CROSS, 0, 3), (ROWS, 0, 3),
        (ROWS, 3, 2), (CROSS, 1, 3), (COMPUTE, 1, 0), (ROWS, 3, 0), (OWN_OVER, 1), (CROSS, 0, 2), (CROSS, 0, 1),
        (CROSS, 0, 0), (COMPUTE, 0, 0), (CROSS, 1, 0), (CROSS, 3, 3), (ROWS, 3, 3), (ROWS, 2, 0), (CROSS, 3, 2),
        (ROWS, 2, 1), (CROSS, 3, 0), (COMPUTE, 0, 1), (OWN_OVER, 2), (CROSS, 2, 3), (CROSS, 3, 1), (CROSS, 2, 2),
        (COMPUTE, 3, 0), (EXCHANGE, 0, 0), (CROSS, 2, 1), (EXCHANGE, 0, 2), (ROWS, 2, 3), (CROSS, 2, 0),
        (COMPUTE, 3, 1), (CROSS, 1, 1), (COMPUTE, 2, 1), (EXCHANGE, 0, 1), (CROSS, 1, 2), (COMPUTE, 2, 0),
        (LINE, 0, 3, 3, 1), (EXCHANGE, 3, 1), (EXCHANGE, 3, 2), (LINE, 0, 3, 3, 0), (COMPUTE, 1, 1), (EXCHANGE, 3, 0),
        (LINE, 0, 3, 1, 0), (LINE, 0, 3, 2, 0), (EXCHANGE, 2, 1), (LINE, 0, 2, 3, 0), (LINE, 1, 0, 3, 1),
        (EXCHANGE, 2, 2), (EXCHANGE, 2, 0), (LINE, 1, 0, 2, 0), (EXCHANGE, 1, 2), (LINE, 0, 3, 0, 0),
        (LINE, 1, 0, 1, 0), (LINE, 0, 2, 3, 1), (LINE, 1, 0, 3, 0), (LINE, 1, 0, 0, 0), (LINE, 0, 2, 0, 0),
        (EXCHANGE, 1, 1), (FINISH, 3, 1), (LINE, 0, 2, 1, 0), (EXCHANGE, 1, 0), (LINE, 0, 2, 2, 0), (FINISH, 1, 0),
        (FINISH, 3, 0), (FINISH, 2, 0), (FINISH, 0, 0),
    ),
)


def place(count):
    z = lax.axis_index("heads")
    c = lax.axis_index("ctx")
    beside = c + 1 - 2 * lax.rem(c, 2)
    across = lax.rem(c + 2, 4)
    diagonal = lax.rem(beside + 2, 4)
    return z, c, beside, across, diagonal


def nearest(count, z, index):
    index = count - 1 - index
    more = jnp.maximum(z, count - 1 - z)
    fewer = count - 1 - more
    alone = more - fewer
    paired = jnp.maximum(index - alone, 0)
    up = jnp.where(z + more < count, more - index, index - more)
    both = (fewer - paired // 2) * (1 - 2 * (paired % 2))
    offset = jnp.where(index < alone, up, both)
    return z + jnp.where(index < count - 1, offset, 0)


def attend_kernel(
    count, tokens_ref, share_hbm, table_ref, state_ref, past_hbm, qkv_hbm,
    hidden_ref, normed_ref, tables_ref,
    slab_ref, qkv_ref, w_ref, query_ref, kv_ref, before_ref, inside_ref, linear_ref,
    state_out, states_in, heads_out, heads_in,
    local_sem, token_send, token_recv, share_send, share_recv,
    tail_send, tail_recv, state_send, state_recv, head_send, head_recv,
):
    z, c, beside, across, diagonal = place(count)
    row_count, width = tokens_ref.shape
    slab_rows = count * row_count
    share = w_ref.shape[0] // (4 * count)

    def rows_of(index, size):
        return pl.ds(pl.multiple_of(index * size, size), size)

    def share_block(kind, zz, cc):
        if kind == 0:
            return w_ref.at[rows_of(zz * 4 + cc, share), :]
        return tables_ref.at[cc * count + zz]

    def share_source(kind):
        return table_ref if kind else share_hbm.at[rows_of(c, share), :]

    local = [
        pltpu.make_async_copy(source, target, local_sem.at[index])
        for index, (source, target) in enumerate(
            [(qkv_hbm.at[one], qkv_ref.at[:, one * HDIM : (one + 1) * HDIM]) for one in range(3)]
            + [(tokens_ref, slab_ref.at[z])]
            + [(share_source(kind), share_block(kind, z, c)) for kind in (0, 1)]
        )
    ]
    past_copy = pltpu.make_async_copy(past_hbm, before_ref, local_sem.at[6])
    for copy in local:
        copy.start()

    @pl.when(c == 0)
    def _():
        past_copy.start()

    barrier = pltpu.get_barrier_semaphore()
    for target in (beside, across, diagonal):
        pl.semaphore_signal(barrier, inc=1, device_id={"ctx": target}, device_id_type=MESH)
    for zz in range(count):

        @pl.when(zz != z)
        def _():
            pl.semaphore_signal(barrier, inc=1, device_id={"heads": zz}, device_id_type=MESH)

    pl.semaphore_wait(barrier, 3 + count - 1)

    def remote(source, target, send, recv, device):
        return pltpu.make_async_remote_copy(
            src_ref=source, dst_ref=target, send_sem=send, recv_sem=recv,
            device_id=device, device_id_type=MESH,
        )

    def started(copy):
        copy.start()

    def left(copy):
        copy.wait_send()

    def along(act, zz, copy):
        @pl.when(jnp.logical_and(zz >= z, z > 0))
        def _():
            act(copy(0, {"heads": z - 1}))

        @pl.when(jnp.logical_and(zz <= z, z < count - 1))
        def _():
            act(copy(1, {"heads": z + 1}))

    def token_copy(zz, piece, own=False):
        rows = pl.ds(piece * row_count // PIECES, row_count // PIECES)

        def copy(way, device):
            block = slab_ref.at[zz, rows, :]
            source = tokens_ref.at[rows, :] if own else block
            return remote(
                source, block, token_send.at[way, piece, zz], token_recv.at[piece, zz], device
            )

        return copy

    def share_copy(kind, zz, cc, own=False):
        def copy(way, device):
            block = share_block(kind, zz, cc)
            slot = zz * 4 + cc
            source = share_source(kind) if own else block
            return remote(
                source, block, share_send.at[kind, way, slot], share_recv.at[kind, slot], device
            )

        return copy

    def aside(act, zz, cc, own=False):
        for kind in (0, 1):
            act(share_copy(kind, zz, cc, own)(3, {"ctx": beside}))

    def share_relay(act, zz, own=False):
        for kind in (0, 1):
            act(share_copy(kind, zz, c, own)(2, {"ctx": across}))
        aside(act, zz, c, own)

    def share_along(act, zz, own=False):
        for kind in (0, 1):
            along(act, zz, share_copy(kind, zz, c, own))

    def share_received(zz, cc):
        for kind in (0, 1):
            share_copy(kind, zz, cc)(3, {"ctx": beside}).wait_recv()

    def at_distance(distance, act):
        @pl.when(z >= distance)
        def _():
            act(z - distance)

        @pl.when(z + distance < count)
        def _():
            act(z + distance)

    def share_onward(zz):
        share_received(zz, c)
        share_along(started, zz)
        share_relay(started, zz)

    def share_over(zz):
        share_received(zz, across)
        aside(started, zz, across)

    for piece in range(PIECES):
        along(started, z, token_copy(z, piece, True))
    share_relay(started, z, True)
    for copy in local:
        copy.wait()

    def project(zz):
        product = jnp.dot(slab_ref[zz], qkv_ref[...], preferred_element_type=jnp.float32)
        product = product.astype(query_ref.dtype)
        rows = rows_of(zz, row_count)
        query_ref[rows, :] = product[:, :HDIM]
        kv_ref[0, rows, :] = product[:, HDIM : 2 * HDIM]
        kv_ref[1, rows, :] = product[:, 2 * HDIM :]

        @pl.when(c < 3)
        def _():
            tail_copy(zz).start()

    def tail_copy(zz):
        rows = rows_of(zz, row_count)
        return remote(
            kv_ref.at[:, rows, :], before_ref.at[:, rows, :], tail_send.at[zz], tail_recv.at[zz],
            {"ctx": jnp.minimum(c + 1, 3)},
        )

    def token_relay(zz, piece):
        token_copy(zz, piece)(0, {"heads": z - 1}).wait_recv()
        along(started, zz, token_copy(zz, piece))

    def step(index, _):
        zz = nearest(count, z, index)
        last = nearest(count, z, jnp.maximum(index - 1, 0))
        after = nearest(count, z, jnp.minimum(index + 1, count - 1))
        opens = jnp.logical_and(index > 0, jnp.abs(zz - z) != jnp.abs(last - z))
        double = jnp.logical_and(index < count - 1, jnp.abs(after - z) == jnp.abs(zz - z))

        for piece in range(PIECES):

            @pl.when(opens)
            def _():
                token_relay(zz, piece)

            @pl.when(jnp.logical_and(opens, double))
            def _():
                token_relay(after, piece)

        project(zz)
        alone = jnp.logical_and(index > 0, jnp.logical_not(jnp.logical_and(opens, double)))
        distance = jnp.abs(zz - z)

        @pl.when(jnp.logical_and(alone, distance == 1))
        def _():
            share_along(started, z, True)

        @pl.when(jnp.logical_and(alone, distance > 1))
        def _():
            at_distance(distance - 1, share_onward)

        return 0

    lax.fori_loop(0, count, step, 0)

    local_state = lax.dot_general(
        kv_ref[0], kv_ref[1], (((0,), (0,)), ((), ())), preferred_element_type=jnp.float32
    )
    state_out[...] = local_state.astype(state_out.dtype)
    others = [beside, across, diagonal]
    state_copies = [
        remote(state_out, states_in.at[c], state_send.at[way], state_recv.at[c], {"ctx": target})
        for way, target in enumerate(others)
    ]
    for copy in state_copies:
        copy.start()
    share_over(z)

    blocks = slab_rows // row_count
    for block in range(blocks):
        first, end = block * row_count, (block + 1) * row_count
        query = query_ref[first:end, :]
        scores = lax.dot_general(
            query, kv_ref[0, :end, :], (((1,), (1,)), ((), ())), preferred_element_type=jnp.float32
        )
        shape = scores.shape
        causal = lax.broadcasted_iota(jnp.int32, shape, 1) <= first + lax.broadcasted_iota(
            jnp.int32, shape, 0
        )
        inside_ref[first:end, :end] = scores
        weights = jnp.where(causal, scores, 0.0).astype(kv_ref.dtype)
        linear_ref[first:end, :] = jnp.dot(
            weights, kv_ref[1, :end, :], preferred_element_type=jnp.float32
        )

    for target in others:
        remote(
            state_out, states_in.at[target], state_send.at[0], state_recv.at[target],
            {"ctx": beside},
        ).wait_recv()
    start = state_ref[...]
    for cc in range(4):
        start = start + jnp.where(cc < c, states_in[cc].astype(jnp.float32), 0.0)

    @pl.when(c == 0)
    def _():
        past_copy.wait()

    @pl.when(c > 0)
    def _():
        for zz in range(count):
            tail_copy(zz).wait_recv()

    scale = 1.0 / math.sqrt(HDIM)

    def head_copy(zz):
        columns = pl.ds(pl.multiple_of(z * HDIM, HDIM), HDIM)
        return remote(
            heads_out.at[zz], heads_in.at[:, columns], head_send.at[zz], head_recv.at[z],
            {"heads": zz},
        )

    for block in range(blocks):
        first, end = block * row_count, (block + 1) * row_count
        query = query_ref[first:end, :]
        old = lax.dot_general(
            query, before_ref[0, first:, :], (((1,), (1,)), ((), ())),
            preferred_element_type=jnp.float32,
        )
        old_seen = lax.broadcasted_iota(jnp.int32, old.shape, 1) > lax.broadcasted_iota(
            jnp.int32, old.shape, 0
        )
        old = jnp.where(old_seen, old * scale, -jnp.inf)
        new = inside_ref[first:end, :end]
        new_seen = lax.broadcasted_iota(jnp.int32, new.shape, 1) <= first + lax.broadcasted_iota(
            jnp.int32, new.shape, 0
        )
        new = jnp.where(new_seen, new * scale, -jnp.inf)
        top = jnp.maximum(
            jnp.max(old, axis=-1, keepdims=True), jnp.max(new, axis=-1, keepdims=True)
        )
        old = jnp.exp(old - top)
        new = jnp.exp(new - top)
        inverse = 1.0 / (
            jnp.sum(old, axis=-1, keepdims=True) + jnp.sum(new, axis=-1, keepdims=True)
        )
        window = jnp.dot(
            (old * inverse).astype(kv_ref.dtype), before_ref[1, first:, :],
            preferred_element_type=jnp.float32,
        ) + jnp.dot(
            (new * inverse).astype(kv_ref.dtype), kv_ref[1, :end, :],
            preferred_element_type=jnp.float32,
        )
        linear = linear_ref[first:end, :] + jnp.dot(
            query.astype(jnp.float32), start, precision=lax.Precision.HIGHEST,
            preferred_element_type=jnp.float32,
        )
        heads_out[block] = (normalize(linear) + window).astype(heads_out.dtype)

        @pl.when(block != z)
        def _():
            head_copy(block).start()

        @pl.when(block == z)
        def _():
            columns = pl.ds(pl.multiple_of(z * HDIM, HDIM), HDIM)
            heads_in[:, columns] = heads_out[block]

        if block == 0:
            at_distance(jnp.maximum(z, count - 1 - z), share_onward)
        if block + 1 < count:
            at_distance(block + 1, share_over)

    for zz in range(count):
        share_received(zz, beside)
        share_received(zz, diagonal)

        @pl.when(zz != z)
        def _():
            remote(
                heads_out.at[zz], heads_in.at[:, zz * HDIM : (zz + 1) * HDIM], head_send.at[zz],
                head_recv.at[zz], {"heads": zz},
            ).wait_recv()

    def out_tile(index, total):
        columns = pl.ds(pl.multiple_of(index * DOT_COLUMNS, DOT_COLUMNS), DOT_COLUMNS)
        attn = jnp.dot(heads_in[...], w_ref[:, columns], preferred_element_type=jnp.float32)
        hidden = (slab_ref[z, :, columns].astype(jnp.float32) + attn).astype(hidden_ref.dtype)
        hidden_ref[:, columns] = hidden
        hidden = hidden.astype(jnp.float32)
        return total + jnp.sum(hidden * hidden, axis=-1, keepdims=True)

    total = lax.fori_loop(
        0, width // DOT_COLUMNS, out_tile, jnp.zeros((row_count, 1), jnp.float32)
    )
    inverse = lax.rsqrt(total / width + 1e-06)
    for first in range(0, width, DOT_COLUMNS):
        hidden = hidden_ref[:, first : first + DOT_COLUMNS].astype(jnp.float32)
        normed_ref[:, first : first + DOT_COLUMNS] = (hidden * inverse).astype(normed_ref.dtype)

    for piece in range(PIECES):
        along(left, z, token_copy(z, piece, True))
    share_along(left, z, True)
    share_relay(left, z, True)

    @pl.when(c < 3)
    def _():
        for zz in range(count):
            tail_copy(zz).wait_send()

    for copy in state_copies:
        copy.wait_send()
    for zz in range(count):
        aside(left, zz, across)

        @pl.when(zz != z)
        def _():
            for piece in range(PIECES):
                along(left, zz, token_copy(zz, piece))
            share_along(left, zz)
            share_relay(left, zz)
            head_copy(zz).wait_send()


def plain_steps(count, at):
    spans = range(len(SPANS))
    steps = [(OWN_LINE, span) for span in spans] + [(OWN_OVER, span) for span in spans]
    steps += [(OWN_ASIDE,), (LOAD,)]
    for distance in range(count):
        planes = sorted({at - distance, at + distance} & set(range(count)))
        for op in (ROWS, CROSS):
            if op == CROSS or distance:
                steps += [(op, zz, span) for zz in planes for span in reversed(spans)]
        steps += [(COMPUTE, zz, pair) for zz in planes for pair in (0, 1)]
    near = [span for span in spans if not SPANS[span][1]]
    far = [span for span in spans if SPANS[span][1]]
    steps += [(EXCHANGE, zz, span) for zz in range(count) for span in near]
    for key in range(1, count):
        links = [(0, key)] * (key > at) + [(1, count - 1 - key)] * (count - 1 - key < at)
        for link in links if at < count - 1 - at else reversed(links):
            steps += [(LINE, *link, span, 0) for span in spans]
            steps += [(LINE, *link, span, 1) for span in far]
    return steps + [(FINISH, span, 1) for span in far] + [(FINISH, span, 0) for span in spans]


def mirrored(step, count):
    op, *where = step
    if op in (ROWS, CROSS, EXCHANGE, COMPUTE):
        return (op, count - 1 - where[0], where[1])
    if op == LINE:
        return (op, 1 - where[0], count - 1 - where[1], *where[2:])
    return step


def steps_of(count, at):
    if count != len(STEPS) * 2:
        return plain_steps(count, at)
    if at < len(STEPS):
        return list(STEPS[at])
    return [mirrored(step, count) for step in STEPS[count - 1 - at]]


def span_rows(row_count):
    spans, first = [], 0
    for share, far in SPANS:
        spans.append((first, row_count * share // 128, far))
        first += row_count * share // 128
    return spans, sum(size for _, size, far in spans if far)


def expert_kernel(
    count, weight_copies, hidden_ref, own_ref, table_ref, out_ref,
    rows_ref, part_ref, hid_ref, scale_ref, gate_ref, up_ref, down_ref,
    from_beside, to_across, from_across, line_out, line_in, last_out, last_in,
    local_sem, row_send, row_recv, beside_send, beside_recv, across_send, across_recv,
    line_send, line_recv, last_send, last_recv,
):
    z, c, beside, across, diagonal = place(count)
    row_count, width = own_ref.shape
    spans, far_rows = span_rows(row_count)
    near_rows = row_count - far_rows
    expert = c * count + z
    own_rows = pl.ds(pl.multiple_of(c * row_count, row_count), row_count)
    own_copy = pltpu.make_async_copy(own_ref, rows_ref.at[z, own_rows, :], local_sem)
    own_copy.start()
    local = weight_copies + [own_copy]

    def window(cc, span):
        first, size, _ = spans[span]
        return pl.ds(pl.multiple_of(cc * row_count + first, 16), size)

    def row_copy(zz, cc, span, way, target, own=False):
        first, size, _ = spans[span]
        slot = zz * 4 + cc
        block = rows_ref.at[zz, window(cc, span), :]
        return pltpu.make_async_remote_copy(
            src_ref=own_ref.at[pl.ds(first, size), :] if own else block,
            dst_ref=block,
            send_sem=row_send.at[way, span, slot],
            recv_sem=row_recv.at[span, slot],
            device_id=target,
            device_id_type=MESH,
        )

    def started(copy):
        copy.start()

    def left(copy):
        copy.wait_send()

    def received(zz, cc, span):
        row_copy(zz, cc, span, 0, {"ctx": beside}).wait_recv()

    def along(act, at, zz, cc, span, own=False):
        if zz >= at and at > 0:
            act(row_copy(zz, cc, span, 0, {"heads": at - 1}, own))
        if zz <= at and at < count - 1:
            act(row_copy(zz, cc, span, 1, {"heads": at + 1}, own))

    def over(act, zz, cc, span, own=False):
        act(row_copy(zz, cc, span, 2, {"ctx": across}, own))

    def aside(act, zz, cc, span, own=False):
        act(row_copy(zz, cc, span, 3, {"ctx": beside}, own))

    def relays(op, at, zz, span, act, wait):
        cc = c if op == ROWS else across
        far = spans[span][2]
        if wait:
            received(zz, cc, span)
        if op == ROWS or far:
            along(act, at, zz, cc, span)
        if op == ROWS and not far:
            over(act, zz, cc, span)
        aside(act, zz, cc, span)

    def paired(zz, pair):
        for span in range(len(spans)):
            received(zz, diagonal if pair else beside, span)

    def compute(zz, pair):
        half = jnp.where(pair == 0, c // 2, 1 - c // 2)
        for core in range(2):
            row = table_ref[(half * 2 + core) * count + zz, pl.ds(expert, 1), :]
            scale_ref[core * row_count : (core + 1) * row_count, :] = jnp.broadcast_to(
                row, (HDIM, row_count)
            ).T

        inner = gate_ref.shape[1]
        rows = pl.ds(pl.multiple_of(half * 2 * row_count, 2 * row_count), 2 * row_count)

        def hidden_tile(index, _):
            columns = pl.ds(pl.multiple_of(index * HID_COLUMNS, HID_COLUMNS), HID_COLUMNS)
            block = rows_ref[zz, rows, :]
            gate = jnp.dot(block, gate_ref[:, columns], preferred_element_type=jnp.float32)
            up = jnp.dot(block, up_ref[:, columns], preferred_element_type=jnp.float32)
            scale = jnp.concatenate([scale_ref[...]] * (HID_COLUMNS // HDIM), axis=1)
            hid_ref[:, columns] = (jax.nn.silu(gate) * up * scale).astype(hid_ref.dtype)
            return 0

        lax.fori_loop(0, inner // HID_COLUMNS, hidden_tile, 0)

        def out_tile(index, _):
            columns = pl.ds(pl.multiple_of(index * DOT_COLUMNS, DOT_COLUMNS), DOT_COLUMNS)
            product = jnp.dot(
                hid_ref[...], down_ref[:, columns], preferred_element_type=jnp.float32
            )
            part_ref[zz, rows, columns] = product.astype(part_ref.dtype)
            return 0

        lax.fori_loop(0, width // DOT_COLUMNS, out_tile, 0)

    def beside_copy(kind, zz):
        cc = diagonal if kind == 0 else beside
        return pltpu.make_async_remote_copy(
            src_ref=part_ref.at[zz, pl.ds(pl.multiple_of(cc * row_count, row_count), row_count), :],
            dst_ref=from_beside.at[kind, zz],
            send_sem=beside_send.at[kind, zz],
            recv_sem=beside_recv.at[kind, zz],
            device_id={"ctx": beside},
            device_id_type=MESH,
        )

    def across_copy(zz, span):
        first, size, _ = spans[span]
        return pltpu.make_async_remote_copy(
            src_ref=to_across.at[zz, pl.ds(first, size), :],
            dst_ref=from_across.at[zz, pl.ds(first, size), :],
            send_sem=across_send.at[span, zz],
            recv_sem=across_recv.at[span, zz],
            device_id={"ctx": across},
            device_id_type=MESH,
        )

    def line_rows(span, other):
        first, size, _ = spans[span]
        return pl.ds(row_count + first - near_rows if other else first, size)

    def line_copy(side, zz, span, other):
        return pltpu.make_async_remote_copy(
            src_ref=line_out.at[zz, line_rows(span, other), :],
            dst_ref=line_in.at[side, zz, line_rows(span, other), :],
            send_sem=line_send.at[2 * span + other, zz],
            recv_sem=line_recv.at[2 * span + other, side, zz],
            device_id={"heads": z + 1 - 2 * side},
            device_id_type=MESH,
        )

    def last_rows(span):
        first, size, _ = spans[span]
        return pl.ds(first - near_rows, size)

    def last_copy(span):
        return pltpu.make_async_remote_copy(
            src_ref=last_out.at[last_rows(span), :],
            dst_ref=last_in.at[last_rows(span), :],
            send_sem=last_send.at[span],
            recv_sem=last_recv.at[span],
            device_id={"ctx": across},
            device_id_type=MESH,
        )

    def add(target, sources):
        def chunk(index, _):
            rows = pl.ds(pl.multiple_of(index * ADD_ROWS, ADD_ROWS), ADD_ROWS)
            total = sources[0][rows, :].astype(jnp.float32)
            for source in sources[1:]:
                total = total + source[rows, :].astype(jnp.float32)
            target[rows, :] = total.astype(target.dtype)
            return 0

        lax.fori_loop(0, target.shape[0] // ADD_ROWS, chunk, 0)

    def starts(side, at):
        return at == side * (count - 1)

    def chip_sources(zz, span, other):
        first, size, far = spans[span]
        start = pl.multiple_of((across if other else c) * row_count + first, 16)
        sources = [
            part_ref.at[zz, pl.ds(start, size), :],
            from_beside.at[1 - other, zz, pl.ds(first, size), :],
        ]
        if not far and not other:
            sources.append(from_across.at[zz, pl.ds(first, size), :])
        return sources

    def perform(at, steps, waited):
        waited = set(waited)

        def once(kind, zz):
            if (kind, zz) not in waited:
                waited.add((kind, zz))
                beside_copy(kind, zz).wait_recv()

        def arrived(zz, span, other, sides):
            once(1 - other, zz)
            if not spans[span][2]:
                across_copy(zz, span).wait_recv()
            sources = chip_sources(zz, span, other)
            for side in sides:
                if not starts(side, at):
                    line_copy(side, zz, span, other).wait_recv()
                    sources.append(line_in.at[side, zz, line_rows(span, other), :])
            return sources

        for op, *where in steps:
            if op == OWN_LINE:
                along(started, at, at, c, where[0], True)
            elif op == OWN_OVER:
                over(started, at, c, where[0], True)
            elif op == OWN_ASIDE:
                for span in range(len(spans)):
                    aside(started, at, c, span, True)
            elif op == LOAD:
                for copy in local:
                    copy.wait()
            elif op == COMPUTE:
                paired(*where)
            elif op == BESIDE:
                beside_copy(where[1], where[0]).start()
            elif op == EXCHANGE:
                zz, span = where
                once(0, zz)
                first, size, _ = spans[span]
                start = pl.multiple_of(across * row_count + first, 16)
                add(
                    to_across.at[zz, pl.ds(first, size), :],
                    [
                        part_ref.at[zz, pl.ds(start, size), :],
                        from_beside.at[0, zz, pl.ds(first, size), :],
                    ],
                )
                across_copy(zz, span).start()
            elif op == LINE:
                side, zz, span, other = where
                add(line_out.at[zz, line_rows(span, other), :], arrived(zz, span, other, (side,)))
                line_copy(side, zz, span, other).start()
            elif op == FINISH and where[1]:
                span = where[0]
                add(last_out.at[last_rows(span), :], arrived(at, span, 1, (0, 1)))
                last_copy(span).start()
            elif op == FINISH:
                span = where[0]
                first, size, far = spans[span]
                rows = pl.ds(first, size)
                sources = arrived(at, span, 0, (0, 1))
                if far:
                    last_copy(span).wait_recv()
                    sources.append(last_in.at[last_rows(span), :])
                add(out_ref.at[rows, :], [hidden_ref.at[rows, :]] + sources)
            else:
                relays(op, at, *where, started, True)

    def each_place(act):
        for at in range(count):

            @pl.when(z == at)
            def _():
                act(at)

    units = 2 * count
    segments, orders = [], []
    for at in range(count):
        parts, order = [[]], []
        for one in steps_of(count, at):
            parts[-1].append(one)
            if one[0] == COMPUTE:
                zz, pair = one[1:]
                order.append((zz, pair))
                parts.append([(BESIDE, zz, 1 - pair)])
        segments.append(parts)
        orders.append(order)

    def waits_of(at, unit):
        keys = set()
        for op, *where in sum(segments[at][:unit], []):
            if op == EXCHANGE:
                keys.add((0, where[0]))
            elif op == LINE:
                keys.add((1 - where[3], where[1]))
            elif op == FINISH:
                keys.add((1 - where[1], at))
        return keys

    def choose(index, pick):
        value = jnp.int32(0)
        for at in range(count):
            for unit in range(units):
                here = jnp.logical_and(z == at, index == unit)
                value = jnp.where(here, pick(orders[at][unit]), value)
        return value

    def step(index, _):
        def segment(at):
            for unit in range(units):

                @pl.when(index == unit)
                def _():
                    perform(at, segments[at][unit], waits_of(at, unit))

        each_place(segment)
        compute(choose(index, lambda unit: unit[0]), choose(index, lambda unit: unit[1]))
        return 0

    lax.fori_loop(0, units, step, 0)

    def finish(at):
        perform(at, segments[at][units], waits_of(at, units))
        for span, (_, _, far) in enumerate(spans):
            if far:
                last_copy(span).wait_send()
            along(left, at, at, c, span, True)
            over(left, at, c, span, True)
            aside(left, at, c, span, True)
            for zz in range(count):
                relays(CROSS, at, zz, span, left, False)
                if not far:
                    across_copy(zz, span).wait_send()
                if zz != at:
                    relays(ROWS, at, zz, span, left, False)
                    for other in range(1 + far):
                        line_copy(int(zz < at), zz, span, other).wait_send()
        for zz in range(count):
            beside_copy(0, zz).wait_send()
            beside_copy(1, zz).wait_send()

    each_place(finish)


def layer_kernel(
    count, front_size, tokens_ref, share_hbm, ids_ref, gates_ref, state_ref, past_hbm, qkv_hbm,
    gate_hbm, up_hbm, down_hbm, out_ref, hidden_ref, normed_ref, table_ref, tables_ref, weight_sem,
    *scratch
):
    front, back = scratch[:front_size], scratch[front_size:]
    weight_copies = [
        pltpu.make_async_copy(source, target, weight_sem.at[index])
        for index, (source, target) in enumerate(zip((gate_hbm, up_hbm, down_hbm), back[4:7]))
    ]
    for copy in weight_copies:
        copy.start()
    experts = lax.broadcasted_iota(jnp.int32, table_ref.shape, 0)
    table = jnp.zeros(table_ref.shape, table_ref.dtype)
    for pick in range(ids_ref.shape[0]):
        chosen = ids_ref[pick : pick + 1, :] == experts
        table = table + jnp.where(chosen, gates_ref[pick : pick + 1, :], 0.0)
    table_ref[...] = table
    attend_kernel(
        count, tokens_ref, share_hbm, table_ref, state_ref, past_hbm, qkv_hbm,
        hidden_ref, normed_ref, tables_ref, *front,
    )
    expert_kernel(count, weight_copies, hidden_ref, normed_ref, tables_ref, out_ref, *back)


def run_layer(tokens, w_out, ids, gates, state_in, past_kv, w_qkv, w_gate, w_up, w_down):
    count = lax.axis_size("heads")
    row_count, width = tokens.shape
    slab_rows = count * row_count
    inner = w_gate.shape[1]
    kind = tokens.dtype
    slots = 4 * count
    far_rows = span_rows(row_count)[1]
    near_rows = row_count - far_rows
    cuts = len(SPANS)
    dma = pltpu.SemaphoreType.DMA
    vmem, anywhere = pl.BlockSpec(memory_space=pltpu.VMEM), pl.BlockSpec(memory_space=pl.ANY)
    shared = [
        pltpu.VMEM((row_count, width), kind),
        pltpu.VMEM((row_count, width), kind),
        pltpu.VMEM((slots, row_count), gates.dtype),
        pltpu.VMEM((slots, slots, row_count), gates.dtype),
        dma((3,)),
    ]
    front = [
        pltpu.VMEM((count, row_count, width), kind),
        pltpu.VMEM((width, 3 * HDIM), kind),
        pltpu.VMEM((count * HDIM, width), kind),
        pltpu.VMEM((slab_rows, HDIM), kind),
        pltpu.VMEM((2, slab_rows, HDIM), kind),
        pltpu.VMEM((2, WINDOW, HDIM), kind),
        pltpu.VMEM((slab_rows, slab_rows), jnp.float32),
        pltpu.VMEM((slab_rows, HDIM), jnp.float32),
        pltpu.VMEM((HDIM, HDIM), kind),
        pltpu.VMEM((4, HDIM, HDIM), kind),
        pltpu.VMEM((count, row_count, HDIM), kind),
        pltpu.VMEM((row_count, count * HDIM), kind),
        dma((7,)),
        dma((2, PIECES, count)),
        dma((PIECES, count)),
        dma((2, 4, slots)),
        dma((2, slots)),
        dma((count,)),
        dma((count,)),
        dma((3,)),
        dma((4,)),
        dma((count,)),
        dma((count,)),
    ]
    back = [
        pltpu.VMEM((count, 4 * row_count, width), kind),
        pltpu.VMEM((count, 4 * row_count, width), kind),
        pltpu.VMEM((2 * row_count, inner), kind),
        pltpu.VMEM((2 * row_count, HDIM), jnp.float32),
        pltpu.VMEM(w_gate.shape, kind),
        pltpu.VMEM(w_up.shape, kind),
        pltpu.VMEM(w_down.shape, kind),
        pltpu.VMEM((2, count, row_count, width), kind),
        pltpu.VMEM((count, near_rows, width), kind),
        pltpu.VMEM((count, near_rows, width), kind),
        pltpu.VMEM((count, row_count + far_rows, width), kind),
        pltpu.VMEM((2, count, row_count + far_rows, width), kind),
        pltpu.VMEM((far_rows, width), kind),
        pltpu.VMEM((far_rows, width), kind),
        dma(()),
        dma((4, cuts, 4 * count)),
        dma((cuts, 4 * count)),
        dma((2, count)),
        dma((2, count)),
        dma((cuts, count)),
        dma((cuts, count)),
        dma((2 * cuts, count)),
        dma((2 * cuts, 2, count)),
        dma((cuts,)),
        dma((cuts,)),
    ]
    return pl.pallas_call(
        functools.partial(layer_kernel, count, len(front)),
        out_shape=jax.ShapeDtypeStruct((row_count, width), kind),
        in_specs=[anywhere] * 2 + [vmem] * 3 + [anywhere] * 5,
        out_specs=vmem,
        scratch_shapes=shared + front + back,
        compiler_params=pltpu.CompilerParams(
            collective_id=0, has_side_effects=True, vmem_limit_bytes=VMEM_BYTES
        ),
        name="run_layer",
    )(tokens, w_out, ids, gates, state_in, past_kv, w_qkv, w_gate, w_up, w_down)


def on_device(
    tokens, state_in, past_kv, w_qkv, w_out, w_gate, w_up, w_down, expert_ids, gate_weights
):
    row_count, model_width = tokens.shape
    inner_width = w_qkv.shape[2]
    local_heads = inner_width // HDIM
    ctx_count = lax.axis_size("ctx")
    head_count = lax.axis_size("heads")
    exp_local = w_gate.shape[0]
    devices = ctx_count * head_count
    expert_count = exp_local * devices
    top_count = expert_ids.shape[1]
    capacity = max(2, 2 * row_count * top_count // expert_count)
    dense = (
        ctx_count == 4
        and exp_local == 1
        and row_count % HDIM == 0
        and local_heads == 1
        and head_count * row_count == WINDOW
        and w_gate.shape[2] % HID_COLUMNS == 0
        and row_count * devices <= expert_count * capacity
    )
    if dense:
        return run_layer(
            tokens, w_out, expert_ids.T, gate_weights.T, state_in[0], past_kv,
            jnp.transpose(w_qkv, (1, 0, 2)), w_gate[0], w_up[0], w_down[0],
        )
    slab, w_rows = [
        lax.all_gather(value, "heads", axis=0, tiled=True) for value in (tokens, w_out)
    ]
    projected = jnp.dot(
        slab,
        w_qkv.reshape(model_width, 3 * inner_width),
        preferred_element_type=jnp.float32,
    ).astype(jnp.bfloat16)
    slab_rows = projected.shape[0]
    projected = projected.reshape(slab_rows, 3, local_heads, HDIM)
    query = jnp.transpose(projected[:, 0], (1, 0, 2))
    keys = jnp.transpose(projected[:, 1], (1, 0, 2))
    values = jnp.transpose(projected[:, 2], (1, 0, 2))
    local_state = jnp.einsum("hsd,hse->hde", keys, values, preferred_element_type=jnp.float32)
    earlier_state = entering(
        local_state, "ctx", lambda first, second: first + second, jnp.zeros_like(local_state)
    )
    start_state = state_in + earlier_state
    tail = jnp.stack([keys, values], axis=0)
    arrived = from_behind(tail, "ctx", 1)
    past = jnp.transpose(past_kv.reshape(2, WINDOW, local_heads, HDIM), (0, 2, 1, 3))
    previous = jnp.where(lax.axis_index("ctx") == 0, past, arrived)
    all_keys = jnp.concatenate([previous[0], keys], axis=1)
    all_values = jnp.concatenate([previous[1], values], axis=1)
    block_rows = min(slab_rows, 512)
    block_count = slab_rows // block_rows
    scale = 1.0 / math.sqrt(HDIM)
    causal = jnp.arange(block_rows)[:, None] >= jnp.arange(block_rows)[None, :]
    offsets = jnp.arange(WINDOW + block_rows)[None, :] - jnp.arange(block_rows)[:, None]
    in_window = (offsets > 0) & (offsets <= WINDOW)

    def block_step(state, index):
        first = index * block_rows
        carried = jnp.einsum(
            "hsd,hde->hse", query.astype(jnp.float32), state, precision=lax.Precision.HIGHEST
        )
        inside = jnp.einsum("hsd,htd->hst", query, keys, preferred_element_type=jnp.float32)
        inside = jnp.where(causal[None], inside, 0.0).astype(jnp.bfloat16)
        linear = carried + jnp.einsum(
            "hst,hte->hse", inside, values, preferred_element_type=jnp.float32
        )
        scores = (
            jnp.einsum("hsd,htd->hst", query, all_keys, preferred_element_type=jnp.float32) * scale
        )
        scores = jnp.where(in_window[None], scores, -jnp.inf)
        top_score = jnp.max(scores, axis=-1, keepdims=True)
        expo = jnp.exp(scores - top_score)
        probs = (expo / jnp.sum(expo, axis=-1, keepdims=True)).astype(jnp.bfloat16)
        window_out = jnp.einsum(
            "hst,hte->hse", probs, all_values, preferred_element_type=jnp.float32
        )
        combined = (normalize(linear) + window_out).astype(jnp.bfloat16)
        new_state = state + jnp.einsum(
            "hsd,hse->hde", keys, values, preferred_element_type=jnp.float32
        )
        return (new_state, combined)

    _, outs = lax.scan(block_step, start_state, jnp.arange(block_count, dtype=jnp.int32))
    heads_out = jnp.transpose(outs, (0, 2, 1, 3)).reshape(slab_rows, inner_width)
    regrouped = lax.all_to_all(heads_out, "heads", split_axis=0, concat_axis=1, tiled=True)
    attn = jnp.dot(
        regrouped,
        w_rows,
        preferred_element_type=jnp.float32,
    )
    hidden_state = (tokens.astype(jnp.float32) + attn).astype(jnp.bfloat16)
    hidden_float = hidden_state.astype(jnp.float32)
    normed = normalize(hidden_float).astype(jnp.bfloat16)
    picks = expert_ids.reshape(-1)
    onehot = (picks[:, None] == jnp.arange(expert_count, dtype=jnp.int32)[None, :]).astype(
        jnp.int32
    )
    earlier = jnp.cumsum(onehot, axis=0) - onehot
    slots = jnp.sum(onehot * earlier, axis=1)
    destination = picks * capacity + slots
    source_rows = jnp.arange(row_count * top_count, dtype=jnp.int32) // top_count
    outgoing = jnp.zeros((expert_count * capacity, model_width), jnp.bfloat16)
    outgoing = outgoing.at[destination].set(normed[source_rows])
    sendable = outgoing.reshape(expert_count, 1, capacity, model_width)
    arrived_rows = lax.all_to_all(
        sendable, ("ctx", "heads"), split_axis=0, concat_axis=1, tiled=True
    )
    e_count, n_count, c_count, d_count = arrived_rows.shape
    flat = arrived_rows.reshape(e_count, n_count * c_count, d_count)
    gate_act = jnp.einsum("erd,edf->erf", flat, w_gate, preferred_element_type=jnp.float32)
    up_act = jnp.einsum("erd,edf->erf", flat, w_up, preferred_element_type=jnp.float32)
    hid = (jax.nn.silu(gate_act) * up_act).astype(jnp.bfloat16)
    out_rows = jnp.einsum("erf,efd->erd", hid, w_down, preferred_element_type=jnp.float32)
    finished = out_rows.astype(jnp.bfloat16).reshape(e_count, n_count, c_count, d_count)
    returned = lax.all_to_all(finished, ("ctx", "heads"), split_axis=1, concat_axis=0, tiled=True)
    returned = returned.reshape(expert_count * capacity, model_width)
    picked = returned[destination].reshape(row_count, top_count, model_width).astype(jnp.float32)
    routed = jnp.sum(gate_weights[:, :, None] * picked, axis=1)
    return (hidden_float + routed).astype(jnp.bfloat16)


def solution(mesh):
    return jax.shard_map(
        on_device,
        mesh=mesh,
        in_specs=(
            P(("groups", "ctx", "heads"), None),
            P("heads", "groups", None),
            P(None, "groups", "heads"),
            P(None, None, "heads"),
            P("heads", None),
            P(("ctx", "heads"), None, None),
            P(("ctx", "heads"), None, None),
            P(("ctx", "heads"), None, None),
            P(("groups", "ctx", "heads"), None),
            P(("groups", "ctx", "heads"), None),
        ),
        out_specs=P(("groups", "ctx", "heads"), None),
        check_vma=False,
    )
```
